32 devices in a mesh: batch: 4 (over z), heads: 4 (over x, core), seq: 2 (over y).
Axes of the slice: x: 2, y: 2, z: 4, core: 2. Of those that a mesh axis runs over, the one named last changes fastest.
Arguments:
- block_input: bfloat16 [4, 2, 1024, 768], P('batch', 'seq', 'heads'), may hold values from -6 to 6
- segment_ids: int32 [4, 2048], P('batch'), may hold values from 0 to 3, never falling along the last dimension, each value on 1 to 1536 neighbouring positions
- norm1_gain: bfloat16 [768], P(('batch', 'seq')), may hold values from 0.5 to 1.5
- norm1_bias: bfloat16 [768], P(('batch', 'seq')), may hold values from -3 to 3
- qkv_weight: bfloat16 [768, 3, 768], P(('batch', 'seq'), None, 'heads'), may hold values from -0.21875 to 0.21875
- conv_kernel: bfloat16 [3, 12, 192], P(None, 'heads', ('batch', 'seq')), may hold values from -3 to 3
- out_weight: bfloat16 [768, 768], P('heads', ('batch', 'seq')), may hold values from -0.875 to 0.875
- norm2_gain: bfloat16 [768], P(('batch', 'seq')), may hold values from 0.5 to 1.5
- norm2_bias: bfloat16 [768], P(('batch', 'seq')), may hold values from -3 to 3
- inner_weight: bfloat16 [768, 3072], P(('batch', 'seq'), 'heads'), may hold values from -0.21875 to 0.21875
- outer_weight: bfloat16 [3072, 768], P('heads', ('batch', 'seq')), may hold values from -0.109375 to 0.109375
- cotangent: bfloat16 [4, 2, 1024, 768], P('batch', 'seq', 'heads'), may hold values from -6 to 6
Outputs:
- block_output: bfloat16 [4, 2, 1024, 768], P('batch', 'seq', 'heads')
- input_grad: float32 [4, 2, 1024, 768], P('batch', 'seq', 'heads')
- norm1_gain_grad: float32 [768], P(('batch', 'seq'))
- norm1_bias_grad: float32 [768], P(('batch', 'seq'))
- qkv_weight_grad: float32 [768, 3, 768], P(('batch', 'seq'), None, 'heads')
- conv_kernel_grad: float32 [3, 12, 192], P(None, 'heads', ('batch', 'seq'))
- out_weight_grad: float32 [768, 768], P('heads', ('batch', 'seq'))
- norm2_gain_grad: float32 [768], P(('batch', 'seq'))
- norm2_bias_grad: float32 [768], P(('batch', 'seq'))
- inner_weight_grad: float32 [768, 3072], P(('batch', 'seq'), 'heads')
- outer_weight_grad: float32 [3072, 768], P('heads', ('batch', 'seq'))
The draws below stay inside these ranges and needn't reach their ends.
Inputs may be any that keep to these rules, and one draw needn't show every extreme that they name: `segment_ids`: in each sequence the ids never fall, every one of the 4 documents is present with 1 to 1536 tokens, and one document has exactly that many.
All inputs are finite; a program needn't handle non-finite values.
Results may differ from the reference program's by a relative error of at most 0.015.
Values may be sent and summed in bfloat16 or wider, within the bound.
No kernel may reach another device: no remote copies, remote signals or barrier semaphores. Data moves between devices by JAX's collectives and lax.ppermute only.
A program may use at most 128 MiB of HBM per device.

```python
import math
import jax
import jax.numpy as jnp
import numpy as np
from jax import lax

HEADS = 12
HEAD_DIM = 64
D = 768
FF = 3072
KERNEL = 3
SEQ_LEN = 2048
DOCS = 4
SEQS = 4


def with_spikes(result, own_key, source, target, parts, factor):
    owner, partner = [(jnp.arange(result.shape[dim]) // (result.shape[dim] // parts)).reshape([-1 if axis == dim else 1 for axis in range(result.ndim)]) for dim in (source, target)]
    chosen = jax.random.permutation(own_key, parts)[partner]
    strong = (owner == chosen) | (owner == (partner + parts // 2) % parts)
    return jnp.where(strong, factor * result, result)


def shard_levels(key, dims, shards, smallest, high):
    def one(axis_at, shards_of):
        draws = jax.random.uniform(jax.random.fold_in(jax.random.fold_in(key, 6), axis_at), (shards_of,), jnp.float32, smallest / len(shards), high / len(shards))
        return jnp.repeat(jnp.exp(draws), dims[axis_at] // shards_of).reshape((-1,) + (1,) * (len(dims) - axis_at - 1))

    loudness = one(*shards[0])
    for cut in shards[1:]:
        loudness = loudness * one(*cut)
    return loudness


def split_up(amount, total, limit, slope):
    portions = [(1 << 20) // math.isqrt(standing ** slope) + 1 for standing in range(2, amount + 1)]
    spare, counts = total - limit - (amount - 1), [1] * (amount - 1)
    while spare > 0:
        candidates = [i for i in range(amount - 1) if counts[i] < limit]
        whole, remaining = sum([portions[i] for i in candidates]), spare
        for i in candidates:
            extra = min(limit - counts[i], max(1, remaining * portions[i] // whole), spare)
            counts[i] = counts[i] + extra
            spare = spare - extra
    return np.array([limit] + counts)


def ragged(rng, count, total, reach, lean):
    if count == 2:
        one = jax.random.randint(rng, (), max(1, total - reach), min(reach, total - 1) + 1)
        return jnp.stack([one, total - one])
    tallies = jnp.asarray(split_up(count, total, reach, lean), jnp.int32)
    twos = (count - 1) // 2
    giver, receiver = tallies[1:1 + 2 * twos:2], tallies[2:2 + 2 * twos:2]
    room = jnp.minimum(giver - 1, reach - receiver)
    passed = jax.random.randint(jax.random.fold_in(rng, 1), (twos,), 0, 1 << 20) % (room + 1)
    tallies = tallies.at[1:1 + 2 * twos:2].set(giver - passed).at[2:2 + 2 * twos:2].set(receiver + passed)
    return tallies[jax.random.permutation(jax.random.fold_in(rng, 2), count)]


def noise(own_key, extent, spread, reach, split=(), kind=jnp.bfloat16):
    loudness = shard_levels(own_key, extent, split, -0.22, 0.18) if split else 1.0
    result = jax.random.normal(own_key, extent, jnp.float32) * spread * loudness
    return jnp.minimum(jnp.maximum(result, -reach), reach).astype(kind)


def noise_with(rng, shape, deviation, reach, pieces, heavy, dtype=jnp.bfloat16):
    array = deviation * jax.random.normal(rng, shape, jnp.float32)
    if pieces:
        array = array * shard_levels(rng, shape, pieces, -0.22, 0.18)
    return jnp.clip(with_spikes(array, jax.random.fold_in(rng, 3), *heavy), -reach, reach).astype(dtype)


def setup_inputs(seed: int = 0) -> dict:
    key_list = jax.random.split(jax.random.key(seed), 13)
    return {
        "block_input": noise(key_list[0], (SEQS, 2, SEQ_LEN // 2, D), 1.0, 6.0, ((0, 4), (1, 2), (2, 4))),
        "segment_ids": jax.vmap(lambda own: jnp.searchsorted(jnp.cumsum(ragged(own, DOCS, SEQ_LEN, 3 * SEQ_LEN // 4, 0)), jnp.arange(SEQ_LEN), side="right"))(jax.random.split(key_list[1], SEQS)).reshape((SEQS, SEQ_LEN)).astype(jnp.int32),
        "norm1_gain": jnp.clip(1.0 + 0.1 * jax.random.normal(key_list[2], (D,), jnp.float32), 0.5, 1.5).astype(jnp.bfloat16),
        "norm1_bias": noise(key_list[3], (D,), 0.3, 3.0, ((0, 8),)),
        "qkv_weight": noise(key_list[4], (D, 3, D), D ** -0.5, 0.21875, ((0, 8), (2, 4))),
        "conv_kernel": noise(key_list[5], (3, HEADS, HEAD_DIM * KERNEL), 0.6, 3.0, ((1, 4), (2, 8))),
        "out_weight": noise(key_list[6], (D, D), (D // 16) ** -0.5, 0.875, ((0, 4), (1, 8))),
        "norm2_gain": jnp.clip(1.0 + 0.1 * jax.random.normal(key_list[7], (D,), jnp.float32), 0.5, 1.5).astype(jnp.bfloat16),
        "norm2_bias": noise(key_list[8], (D,), 0.3, 3.0, ((0, 8),)),
        "inner_weight": noise(key_list[9], (D, FF), D ** -0.5, 0.21875, ((0, 8), (1, 4))),
        "outer_weight": noise(key_list[10], (FF, D), FF ** -0.5, 0.109375, ((0, 4), (1, 8))),
        "cotangent": noise_with(key_list[11], (SEQS, 2, SEQ_LEN // 2, D), 1.0, 6.0, ((0, 4), (1, 2), (2, 4)), (0, 3, 4, 2.0)),
    }


@jax.custom_vjp
def low(v):
    return lax.optimization_barrier(v.astype(jnp.bfloat16)).astype(jnp.float32)

@jax.custom_vjp
def low_back(v):
    return v

def low_keep(v):
    return (low(v), None)

def low_pass(kept, grad):
    return (grad,)

def back_keep(v):
    return (v, None)

def back_low(kept, grad):
    return (low(grad),)
low.defvjp(low_keep, low_pass)
low_back.defvjp(back_keep, back_low)
highest = lax.Precision.HIGHEST
epsilon = 1e-05

def rounded_both(values):
    return low(low_back(values))

def layer_norm(values, scale_vec, shift_vec):
    average = lax.optimization_barrier(jnp.mean(values, axis=-1, keepdims=True))
    centered = values - average
    inverse = lax.rsqrt(lax.optimization_barrier(jnp.mean(centered * centered, axis=-1, keepdims=True)) + epsilon)
    return centered * inverse * scale_vec + shift_vec

def layer_forward(params, inputs, seg_row):
    gain_one, bias_one, qkv_matrix, kernel_array, proj_matrix, gain_two, bias_two, inner_matrix, outer_matrix = params
    length = inputs.shape[0]
    normed = low(layer_norm(inputs, gain_one, bias_one))
    projected = rounded_both(jnp.dot(normed, qkv_matrix.reshape(D, 3 * D), precision=highest))
    tap_weights = kernel_array.reshape(3, D, KERNEL).transpose(2, 0, 1).reshape(KERNEL, 3 * D)
    mixed_rows = tap_weights[0] * projected
    for offset in range(1, KERNEL):
        earlier = jnp.concatenate([jnp.zeros((offset, 3 * D), jnp.float32), projected[:-offset]], axis=0)
        same_doc = jnp.concatenate([jnp.zeros((offset,), jnp.float32), (seg_row[offset:] == seg_row[:-offset]).astype(jnp.float32)])
        mixed_rows = mixed_rows + tap_weights[offset] * earlier * same_doc[:, None]
    mixed_rows = rounded_both(mixed_rows)
    query_rows = mixed_rows[:, :D].reshape(length, HEADS, HEAD_DIM)
    key_rows = mixed_rows[:, D:2 * D].reshape(length, HEADS, HEAD_DIM)
    value_rows = mixed_rows[:, 2 * D:].reshape(length, HEADS, HEAD_DIM)
    scores = jnp.einsum('qhd,khd->hqk', query_rows, key_rows, precision=highest) * HEAD_DIM ** (-0.5)
    scores = low_back(scores)
    positions = jnp.arange(length)
    allowed = (positions[None, :] <= positions[:, None]) & (seg_row[None, :] == seg_row[:, None])
    scores = jnp.where(allowed[None], scores, -1e+30)
    soft_weights = low(jax.nn.softmax(scores, axis=-1))
    attended = jnp.einsum('hqk,khd->qhd', soft_weights, value_rows, precision=highest).reshape(length, D)
    attended = rounded_both(attended)
    middle = inputs + low_back(jnp.dot(attended, proj_matrix, precision=highest))
    normed_two = low(layer_norm(middle, gain_two, bias_two))
    inner_act = low_back(jnp.dot(normed_two, inner_matrix, precision=highest))
    squared = low(jnp.square(jnp.maximum(inner_act, 0.0)))
    return middle + jnp.dot(squared, outer_matrix, precision=highest)

def reference(block_input, segment_ids, norm1_gain, norm1_bias, qkv_weight, conv_kernel, out_weight, norm2_gain, norm2_bias, inner_weight, outer_weight, cotangent):
    params = (norm1_gain.astype(jnp.float32), norm1_bias.astype(jnp.float32), qkv_weight.astype(jnp.float32), conv_kernel.astype(jnp.float32), out_weight.astype(jnp.float32), norm2_gain.astype(jnp.float32), norm2_bias.astype(jnp.float32), inner_weight.astype(jnp.float32), outer_weight.astype(jnp.float32))
    flat_inputs = block_input.reshape(SEQS, SEQ_LEN, D)
    flat_cot = cotangent.reshape(SEQS, SEQ_LEN, D)

    def per_sequence(totals, entries):
        inputs, seg_row, cot_row = entries

        def closed(weights, values):
            return layer_forward(weights, values, seg_row)
        output_row, pullback = jax.vjp(closed, params, inputs.astype(jnp.float32))
        weight_grads, input_row = pullback(cot_row.astype(jnp.float32))
        totals = jax.tree.map(jnp.add, totals, weight_grads)
        return (totals, (output_row.astype(jnp.bfloat16), input_row))
    initial = jax.tree.map(jnp.zeros_like, params)
    totals, (outputs, input_grads) = lax.scan(per_sequence, initial, (flat_inputs, segment_ids, flat_cot))
    outputs = outputs.reshape(SEQS, 2, SEQ_LEN // 2, D)
    input_grads = input_grads.reshape(SEQS, 2, SEQ_LEN // 2, D)
    return (outputs, input_grads, totals[0], totals[1], totals[2], totals[3], totals[4], totals[5], totals[6], totals[7], totals[8])
```

```python
import functools

import jax
import jax.numpy as jnp
from jax import lax
from jax.experimental import pallas as pl
from jax.experimental.pallas import tpu as pltpu
from jax.sharding import PartitionSpec as P

HEAD_DIM = 64
KERNEL = 3
DOCS = 4
PADW = 256
QB = 512
KB = 256

epsilon = 1e-05
masked_score = -1e30
f32 = jnp.float32
b16 = jnp.bfloat16

VMEM = pl.BlockSpec(memory_space=pltpu.VMEM)
SMEM = pl.BlockSpec(memory_space=pltpu.SMEM)


def swap(shard, axis, by):
    return lax.ppermute(shard, axis, [(i, i ^ by) for i in range(lax.axis_size(axis))])


def gather_heads(shard):
    far = swap(shard, "heads", 2)
    near = swap(shard, "heads", 1)
    return [shard, near, far, swap(far, "heads", 1)]


def pairwise(group):
    return group % 32 == 0


def gather_rows(shard):
    if not pairwise(shard.shape[0]):
        whole = lax.all_gather(shard, ("batch", "seq"), axis=0, tiled=True)
        return tuple(whole.reshape(2, 1, -1, shard.shape[1]))
    count = lax.axis_size("batch")
    stack = jnp.stack([shard] + [swap(shard, "batch", by) for by in range(1, count)])
    return stack, swap(stack, "seq", 1)


def scatter_rows(keep, sent):
    if keep.shape[0] == 1:
        whole = jnp.concatenate([keep[0].astype(b16), sent[0]])
        return lax.psum_scatter(whole, ("batch", "seq"), scatter_dimension=0, tiled=True).astype(f32)
    got = swap(sent, "seq", 1)
    total = keep.astype(f32) + got.astype(f32)
    pieces = [swap(total[by].astype(b16), "batch", by) for by in range(1, lax.axis_size("batch"))]
    result = total[0]
    for piece in pieces:
        result = result + piece.astype(f32)
    return result


def scatter_heads(keep, sent):
    got = swap(sent, "heads", 1)
    rows = keep.shape[0] // 2
    far = (keep[rows:].astype(f32) + got[rows:].astype(f32)).astype(b16)
    here = keep[:rows].astype(f32) + got[:rows].astype(f32)
    return here, swap(far, "heads", 2)


def call(body, outs, *args, scratch=(), flops=0, limit=40):
    in_specs = [SMEM] + [VMEM] * (len(args) - 1)
    return pl.pallas_call(
        body,
        out_shape=[jax.ShapeDtypeStruct(*o) for o in outs],
        in_specs=in_specs,
        out_specs=[VMEM] * len(outs),
        scratch_shapes=list(scratch),
        compiler_params=pltpu.CompilerParams(vmem_limit_bytes=limit << 20),
        cost_estimate=pl.CostEstimate(
            flops=flops,
            transcendentals=0,
            bytes_accessed=sum(a.size * a.dtype.itemsize for a in args),
        ),
    )(*args)


def dot(a, b, ca=1, cb=0):
    return lax.dot_general(a, b, (((ca,), (cb,)), ((), ())), preferred_element_type=f32)


def edges(scal):
    return [scal[3 + d] for d in range(DOCS)]


def doc_start(pos, bounds):
    start = bounds[0] + jnp.zeros_like(pos)
    for edge in bounds[1:]:
        start = jnp.where(pos >= edge, edge, start)
    return start


def lanes_like(shape):
    return lax.broadcasted_iota(jnp.int32, shape, 1)


def half_roll(block):
    return pltpu.roll(block, 64, 1)


def norm_rows(values):
    average = jnp.mean(values, axis=-1, keepdims=True)
    centered = values - average
    inverse = lax.rsqrt(jnp.mean(centered * centered, axis=-1, keepdims=True) + epsilon)
    return centered * inverse, inverse


def group_rows(stack, rel, rel_seq, scal):
    count = stack.shape[1]
    if stack.shape[0] == 1:
        return slice(rel_seq * count, rel_seq * count + count)
    return pl.ds(pl.multiple_of(((scal[1] ^ rel) * 2 + (scal[2] ^ rel_seq)) * count, 32), count)


def ds(start, size):
    return pl.ds(pl.multiple_of(start, size), size)


def front_body(half, quarter, scal, *refs):
    pieces, refs = refs[:8], refs[8:]
    w_own, w_other, gain, bias, taps = refs[:5]
    normed, form, projected, wpad, query, key, value = refs[5:12]
    rows_in, proj = refs[12:]
    head = scal[0]
    low = lanes_like((w_own.shape[1], 128)) < 64
    for rel_seq, stack in enumerate((w_own, w_other)):
        for rel in range(stack.shape[0]):
            rows = group_rows(stack, rel, rel_seq, scal)
            for part in range(3):
                wpad[rows, part * 256 : part * 256 + 128] = stack[rel, :, part * 128 : part * 128 + 128]
            shared = stack[rel, :, 384:512].astype(f32)
            wpad[rows, 128:256] = jnp.where(low, shared, 0.0).astype(b16)
            wpad[rows, 384:512] = jnp.where(low, half_roll(shared), 0.0).astype(b16)
            wpad[rows, 640:768] = stack[rel, :, 512:640]
    for index, piece in enumerate(pieces):
        base = (head ^ (index % 4)) * quarter + (half if index < 4 else 0)
        rows_in[ds(base, quarter), :] = piece[...]
    proj[0:16, :] = jnp.zeros((16, proj.shape[1]), b16)

    def project(block, own):
        base = block * quarter
        hat, _ = norm_rows(rows_in[ds(base, quarter), :].astype(f32))
        rounded = (hat * gain[...] + bias[...]).astype(b16)
        proj[pl.ds(pl.multiple_of(base + 16, 16), quarter), :] = dot(rounded, wpad[...]).astype(b16)
        if own:
            rows = ds(base - half, quarter)
            normed[rows, :] = rounded
            form[rows, :] = hat.astype(b16)

    @pl.loop(0, 4)
    def _(block):
        project(block, False)

    @pl.loop(4, 8)
    def _(block):
        project(block, True)

    projected[...] = proj[half : 2 * half + 16, :]
    bounds = edges(scal)

    def convolve(block, own):
        base = block * quarter
        pos = base + lax.broadcasted_iota(jnp.int32, (quarter, 1), 0)
        start = doc_start(pos, bounds)
        for part, out in enumerate((query, key, value)):
            if part == 0 and not own:
                continue
            cols = slice(part * PADW, part * PADW + PADW)
            rows = proj[pl.ds(pl.multiple_of(base, 16), quarter + 16), cols].astype(f32)
            mixed = taps[0:1, cols] * rows[16:]
            for back in range(1, KERNEL):
                earlier = pltpu.roll(rows, back, 0)[16:]
                mixed = mixed + jnp.where(pos - back >= start, taps[back : back + 1, cols] * earlier, 0.0)
            mixed = mixed.astype(b16)
            if part == 0:
                out[ds(base - half, quarter), :] = mixed * jnp.asarray(HEAD_DIM**-0.5, b16)
            else:
                out[ds(base, quarter), :] = mixed

    @pl.loop(0, 4)
    def _(block):
        convolve(block, False)

    @pl.loop(4, 8)
    def _(block):
        convolve(block, True)


def masked_queries(query, slots, heads):
    lane = lanes_like(query.shape) // HEAD_DIM
    for head in range(heads):
        slots[head] = jnp.where(lane == head, query[...], jnp.zeros((), b16))


def attention_body(half, heads, scal, query, key, value, packed, out_t, lse, vt, qm, peak, total):
    bounds = edges(scal)
    masked_queries(query, qm, heads)

    @pl.loop(0, 2 * half // 256)
    def _(block):
        turned = value[ds(block * 256, 256), :].astype(f32).T
        vt[:, ds(block * 256, 256)] = turned[: heads * HEAD_DIM].astype(b16)

    out_t[...] = jnp.zeros_like(out_t)
    peak[...] = jnp.full_like(peak, masked_score)
    total[...] = jnp.zeros_like(total)
    for block in range(half // QB):
        first = half + block * QB
        cols = slice(block * QB, block * QB + QB)
        pos = first + lanes_like((1, QB))
        start = doc_start(pos, bounds)
        low = doc_start(jnp.int32(first), bounds) // KB

        @pl.loop(low, (first + QB) // KB)
        def _(kb):
            keys = key[ds(kb * KB, KB), :]
            key_pos = kb * KB + lax.broadcasted_iota(jnp.int32, (KB, 1), 0)
            allowed = (key_pos >= start) & (key_pos <= pos)
            for head in range(heads):
                rows = slice(head * HEAD_DIM, head * HEAD_DIM + HEAD_DIM)
                one = slice(head, head + 1)
                scores = dot(keys, qm[head, cols, :], 1, 1)
                scores = jnp.where(allowed, scores, masked_score)
                old = peak[one, cols]
                new = jnp.maximum(old, jnp.max(scores, axis=0, keepdims=True))
                weights = jnp.exp(scores - new)
                shrink = jnp.exp(old - new)
                peak[one, cols] = new
                total[one, cols] = shrink * total[one, cols] + jnp.sum(weights, axis=0, keepdims=True)
                out_t[rows, cols] = shrink * out_t[rows, cols] + dot(
                    vt[rows, ds(kb * KB, KB)], weights.astype(b16)
                )

    for head in range(heads):
        rows = slice(head * HEAD_DIM, head * HEAD_DIM + HEAD_DIM)
        out_t[rows, :] = out_t[rows, :] / total[head : head + 1, :]
    lse[...] = peak[...] + jnp.log(jnp.maximum(total[...], 1e-30))
    for block in range(half // 256):
        cols = slice(block * 256, block * 256 + 256)
        packed[cols, :] = out_t[0:128, cols].T.astype(b16)
    for block in range(half // 512):
        cols = slice(block * 256, block * 256 + 256)
        later = slice(half // 2 + block * 256, half // 2 + block * 256 + 256)
        both = jnp.concatenate([out_t[128:192, cols], out_t[128:192, later]], axis=0)
        packed[half + block * 256 : half + block * 256 + 256, :] = both.T.astype(b16)


def back_blocks(half, heads, scal, first_kb, last_kb, refs, finish):
    key, value, qm, dom, lse, row_dot, kt, query_t, key_sum, value_sum = refs
    bounds = edges(scal)

    @pl.loop(first_kb, last_kb)
    def _(kb):
        key_sum[...] = jnp.zeros_like(key_sum)
        value_sum[...] = jnp.zeros_like(value_sum)
        for block in range(half // QB):
            first = half + block * QB
            cols = slice(block * QB, block * QB + QB)
            low = doc_start(jnp.int32(first), bounds)

            @pl.when((kb * KB + KB > low) & (kb * KB < first + QB))
            def _():
                pos = first + lanes_like((1, QB))
                start = doc_start(pos, bounds)
                keys = key[ds(kb * KB, KB), :]
                values = value[ds(kb * KB, KB), :]
                key_pos = kb * KB + lax.broadcasted_iota(jnp.int32, (KB, 1), 0)
                allowed = (key_pos >= start) & (key_pos <= pos)
                for head in range(heads):
                    rows = slice(head * HEAD_DIM, head * HEAD_DIM + HEAD_DIM)
                    one = slice(head, head + 1)
                    own_q = qm[head, cols, :]
                    own_g = dom[head, cols, :]
                    scores = jnp.where(allowed, dot(keys, own_q, 1, 1) - lse[one, cols], masked_score)
                    weights = jnp.exp(scores)
                    grads = weights * (dot(values, own_g, 1, 1) - row_dot[one, cols])
                    grads = grads.astype(b16)
                    value_sum[...] += dot(weights.astype(b16), own_g)
                    key_sum[...] += dot(grads, own_q)
                    query_t[rows, cols] += dot(kt[rows, ds(kb * KB, KB)], grads)

        finish(kb, key_sum[...], value_sum[...])


def spread_groups(source, scal, keep, sent):
    for rel_seq, out in enumerate((keep, sent)):
        for rel in range(out.shape[0]):
            out[rel] = source[group_rows(out, rel, rel_seq, scal), :].astype(out.dtype)


def remote_back_body(half, quarter, heads, scal, *refs):
    branches, refs = refs[:4], refs[4:]
    wo, query, key, value, out_t, lse = refs[:6]
    remote, query_t, dout, row_dot, kt, proj_keep, proj_send = refs[6:13]
    qm, dom, key_sum, value_sum, proj_grad, turned = refs[13:]
    head = scal[0]
    width = heads * HEAD_DIM
    masked_queries(query, qm, heads)
    proj_grad[...] = jnp.zeros_like(proj_grad)
    row_dot[...] = jnp.zeros_like(row_dot)
    for rel, branch in enumerate(branches):
        base = (head ^ rel) * quarter
        grad = dot(branch[...], wo[...]).astype(b16)
        dout[ds(base, quarter), :] = grad
        attended = out_t[:, ds(base, quarter)]
        product = grad.astype(f32).T[:width] * attended
        for one in range(heads):
            row_dot[one : one + 1, ds(base, quarter)] = jnp.sum(
                product[one * HEAD_DIM : one * HEAD_DIM + HEAD_DIM], axis=0, keepdims=True
            )
        proj_grad[...] += dot(attended.astype(b16), branch[...])
    turned[...] = proj_grad[...].T
    spread_groups(turned, scal, proj_keep, proj_send)
    masked_queries(dout, dom, heads)

    @pl.loop(0, 2 * half // 256)
    def _(block):
        kt[:, ds(block * 256, 256)] = key[ds(block * 256, 256), :].astype(f32).T[:width].astype(b16)

    query_t[...] = jnp.zeros_like(query_t)

    def finish(kb, dk, dv):
        rows = ds(kb * KB, KB)
        remote[rows, 0:128] = dk[:, 0:128].astype(b16)
        remote[rows, 128:256] = dv[:, 0:128].astype(b16)
        remote[rows, 256:384] = (dk[:, 128:256] + half_roll(dv[:, 128:256])).astype(b16)

    back_blocks(
        half, heads, scal, 0, half // KB,
        (key, value, qm, dom, lse, row_dot, kt, query_t, key_sum, value_sum), finish,
    )


def local_back_body(half, heads, scal, *refs):
    query, key, value, dout, lse, row_dot, kt, query_in, taps = refs[:9]
    dq, dk_out, dv_out, front = refs[9:13]
    qm, dom, key_sum, value_sum, query_t = refs[13:]
    masked_queries(query, qm, heads)
    masked_queries(dout, dom, heads)
    query_t[...] = query_in[...]

    def finish(kb, dk, dv):
        rows = ds(kb * KB - half, KB)
        dk_out[rows, :] = dk
        dv_out[rows, :] = dv

    back_blocks(
        half, heads, scal, half // KB, 2 * half // KB,
        (key, value, qm, dom, lse, row_dot, kt, query_t, key_sum, value_sum), finish,
    )
    width = heads * HEAD_DIM
    scale = HEAD_DIM**-0.5
    for block in range(half // 256):
        cols = slice(block * 256, block * 256 + 256)
        turned = (query_t[:, cols] * scale).T
        dq[cols, 0:128] = turned[:, 0:128]
        dq[cols, 128:256] = jnp.concatenate(
            [turned[:, 128:width], jnp.zeros((256, PADW - width), f32)], axis=1
        )
    bounds = edges(scal)
    pos = half + lax.broadcasted_iota(jnp.int32, (8, 1), 0)
    start = doc_start(pos, bounds)
    for part, grads in enumerate((dq, dk_out, dv_out)):
        cols = slice(part * PADW, part * PADW + PADW)
        rounded = grads[0:8, :].astype(b16).astype(f32)
        result = jnp.zeros((8, PADW), f32)
        for back in range(1, KERNEL):
            moved = pltpu.roll(jnp.where(pos - back >= start, taps[back : back + 1, cols] * rounded, 0.0), 8 - back, 0)
            place = lax.broadcasted_iota(jnp.int32, (8, 1), 0)
            result = result + jnp.where(place >= 8 - back, moved, 0.0)
        front[:, cols] = result


def weights_body(scal, *refs):
    first, second, first_o, second_o, inner, wo, outer = refs
    for rel_seq, (one, two) in enumerate(((first, second), (first_o, second_o))):
        for rel in range(one.shape[0]):
            rows = group_rows(one, rel, rel_seq, scal)
            width = inner.shape[1]
            inner[rows, :] = one[rel, :, :width]
            wo[rows, :] = one[rel, :, width:]
            outer[rows, :] = two[rel]


def feed_body(half, quarter, scal, *refs):
    attended, wos, inputs, cots = refs[0:4], refs[4:8], refs[8:12], refs[12:16]
    inner, outer, gain, bias = refs[16:20]
    normed, squared, inner_grad, keep, sent, middle_own = refs[20:]
    head = scal[0]
    for rel in range(4):
        base = (head ^ rel) * quarter
        late = base >= half // 2
        middle = inputs[rel][...].astype(f32)
        for part in range(4):
            left = attended[part][ds(base, quarter), :]
            right = attended[part][ds(half + lax.rem(base, half // 2), quarter), :].astype(f32)
            right = jnp.where(late, half_roll(right), right).astype(b16)
            middle = middle + dot(jnp.concatenate([left, right], axis=1), wos[part][...], 1, 1)
        if rel == 0:
            middle_own[...] = middle
        hat, _ = norm_rows(middle)
        rounded = (hat * gain[...] + bias[...]).astype(b16)
        rows = slice(rel * quarter, rel * quarter + quarter)
        normed[rows, :] = rounded
        positive = jnp.maximum(dot(rounded, inner[...]), 0.0)
        squared[rows, :] = (positive * positive).astype(b16)
        grads = (dot(cots[rel][...], outer[...]) * 2.0 * positive).astype(b16)
        inner_grad[rows, :] = grads
        part = dot(grads, inner[...], 1, 1)
        place = slice((rel // 2) * quarter, (rel // 2) * quarter + quarter)
        if rel % 2 == 0:
            keep[place, :] = part
        else:
            sent[place, :] = part.astype(b16)


def feed_grads_body(half, quarter, scal, *refs):
    cots = refs[0:4]
    normed, squared, inner_grad, outer = refs[4:8]
    keep, sent, in_keep, in_send, out_keep, out_send = refs[8:14]
    cot, total = refs[14:]
    for rel in range(4):
        rows = slice(rel * quarter, rel * quarter + quarter)
        cot[rows, :] = cots[rel][...]
        part = dot(squared[rows, :], outer[...], 1, 1)
        place = slice((rel // 2) * quarter, (rel // 2) * quarter + quarter)
        if rel % 2 == 0:
            keep[place, :] = part
        else:
            sent[place, :] = part.astype(b16)
    for left, right, kept, away in ((cot, squared, out_keep, out_send), (normed, inner_grad, in_keep, in_send)):
        for tile in range(total.shape[0] // 256):
            cols = slice(tile * 256, tile * 256 + 256)
            total[cols, :] = dot(left[:, cols], right[...], 0, 0)
        spread_groups(total, scal, kept, away)


def norm_back_body(scal, part, got, values, skip, gain, grad_in, rounded, sums):
    del scal
    grad = part[...] + got[...].astype(f32)
    hat, inverse = norm_rows(values[...].astype(f32))
    scaled = grad * gain[...]
    back = inverse * (
        scaled
        - jnp.mean(scaled, axis=-1, keepdims=True)
        - hat * jnp.mean(scaled * hat, axis=-1, keepdims=True)
    )
    result = skip[...].astype(f32) + back
    grad_in[...] = result
    rounded[...] = result.astype(b16)
    sums[...] = jnp.zeros_like(sums)
    sums[0:1, :] = jnp.sum(grad * hat, axis=0, keepdims=True)
    sums[1:2, :] = jnp.sum(grad, axis=0, keepdims=True)


def tail_body(half, quarter, scal, *refs):
    dq, dk, dv, remote, front, projected, normed, form, wpad, taps = refs[:10]
    keep, sent, w_keep, w_send, sums = refs[10:15]
    mixed, proj_grad, total, dense = refs[15:]
    head = scal[0]
    bounds = edges(scal)
    low = lanes_like((quarter, 128)) < 64
    sums[...] = jnp.zeros_like(sums)
    for block in range(half // quarter):
        rows = slice(block * quarter, block * quarter + quarter)
        shared = remote[rows, 256:384].astype(f32)
        mixed[rows, 0:256] = dq[rows, :].astype(b16)
        mixed[rows, 256:384] = (dk[rows, 0:128] + remote[rows, 0:128].astype(f32)).astype(b16)
        mixed[rows, 384:512] = (dk[rows, 128:256] + jnp.where(low, shared, 0.0)).astype(b16)
        mixed[rows, 512:640] = (dv[rows, 0:128] + remote[rows, 128:256].astype(f32)).astype(b16)
        mixed[rows, 640:768] = (dv[rows, 128:256] + jnp.where(low, half_roll(shared), 0.0)).astype(b16)
    mixed[half : half + 16, :] = jnp.zeros((16, mixed.shape[1]), b16)

    @pl.loop(0, half // quarter)
    def _(block):
        base = block * quarter
        pos = half + base + lax.broadcasted_iota(jnp.int32, (quarter + 16, 1), 0)
        start = doc_start(pos, bounds)
        for part in range(3):
            cols = slice(part * PADW, part * PADW + PADW)
            grads = mixed[pl.ds(pl.multiple_of(base, 16), quarter + 16), cols].astype(f32)
            values = projected[pl.ds(pl.multiple_of(base, 16), quarter + 16), cols].astype(f32)
            here = grads[:quarter]
            result = taps[0:1, cols] * here
            sums[4:5, cols] += jnp.sum(here * values[16:], axis=0, keepdims=True)
            for back in range(1, KERNEL):
                same = pos - back >= start
                held = jnp.where(same, grads, 0.0)
                ahead = pltpu.roll(held, quarter + 16 - back, 0)[:quarter]
                result = result + taps[back : back + 1, cols] * ahead
                earlier = pltpu.roll(values, back, 0)[16:]
                sums[4 + back : 5 + back, cols] += jnp.sum(held[:quarter] * earlier, axis=0, keepdims=True)
            proj_grad[ds(base, quarter), cols] = result.astype(b16)

        @pl.when(block == half // quarter - 1)
        def _():
            added = jnp.concatenate([jnp.zeros((8, front.shape[1]), f32), front[...]], axis=0)
            tail_pos = 2 * half - 16 + lax.broadcasted_iota(jnp.int32, (32, 1), 0)
            tail_start = doc_start(tail_pos, bounds)
            grads = mixed[half - 16 : half + 16, :].astype(f32)
            result = taps[0:1, :] * grads[:16]
            for back in range(1, KERNEL):
                held = jnp.where(tail_pos - back >= tail_start, grads, 0.0)
                result = result + taps[back : back + 1, :] * pltpu.roll(held, 32 - back, 0)[:16]
            proj_grad[half - 16 : half, :] = (result + added).astype(b16)

    for rel in range(4):
        base = (head ^ rel) * quarter
        part = dot(proj_grad[ds(base, quarter), :], wpad[...], 1, 1)
        sums[0:1, :] += jnp.sum(part * form[ds(base, quarter), :].astype(f32), axis=0, keepdims=True)
        sums[1:2, :] += jnp.sum(part, axis=0, keepdims=True)
        place = slice((rel // 2) * quarter, (rel // 2) * quarter + quarter)
        if rel % 2 == 0:
            keep[place, :] = part
        else:
            sent[place, :] = part.astype(b16)
    for tile in range(total.shape[0] // 256):
        rows = slice(tile * 256, tile * 256 + 256)
        total[rows, :] = dot(normed[:, rows], proj_grad[...], 0, 0)
        for part in range(3):
            dense[rows, part * 128 : part * 128 + 128] = total[rows, part * 256 : part * 256 + 128]
        dense[rows, 384:512] = total[rows, 128:256] + half_roll(total[rows, 384:512])
        dense[rows, 512:640] = total[rows, 640:768]
    spread_groups(dense, scal, w_keep, w_send)


def pad_heads(values, width):
    shaped = values.reshape(values.shape[:-1] + (3, width))
    padded = jnp.pad(shaped, [(0, 0)] * (shaped.ndim - 1) + [(0, PADW - width)])
    return padded.reshape(values.shape[:-1] + (3 * PADW,))


def on_device(
    block_input, segment_ids, norm1_gain, norm1_bias, qkv_weight, conv_kernel, out_weight,
    norm2_gain, norm2_bias, inner_weight, outer_weight, cotangent,
):
    quarter = block_input.shape[2]
    half = quarter * lax.axis_size("heads")
    width = qkv_weight.shape[2]
    heads = width // HEAD_DIM
    group = qkv_weight.shape[0]
    groups = lax.axis_size("batch") * lax.axis_size("seq")
    model = group * groups
    hidden = inner_weight.shape[1]
    head, batch, seq = lax.axis_index("heads"), lax.axis_index("batch"), lax.axis_index("seq")
    own = batch * 2 + seq
    stacks = (groups // 2, group) if pairwise(group) else (1, model // 2)

    ids = segment_ids.reshape(-1)
    docs = jnp.arange(DOCS, dtype=jnp.int32)
    firsts = jnp.sum((ids[None, :] < docs[:, None]).astype(jnp.int32), axis=1) - (seq - 1) * half
    scal = jnp.concatenate([jnp.stack([head, batch, seq]), firsts, jnp.zeros((1,), jnp.int32)]).astype(jnp.int32)

    x_own = block_input.reshape(quarter, model)
    cot_own = cotangent.reshape(quarter, model)

    small = jnp.concatenate([norm1_gain, norm1_bias, norm2_gain, norm2_bias, conv_kernel.reshape(-1)])
    small = jnp.pad(small, (0, -small.shape[0] % 128)).reshape(1, -1)
    if pairwise(group):
        small_all = jnp.stack([small] + [swap(small, "batch", by) for by in range(1, groups // 2)])
        small_all = jnp.concatenate([small_all, swap(small_all, "seq", 1)]).reshape(groups, -1)
        order = jnp.arange(groups)
        rel_of = (order % 2 ^ seq) * (groups // 2) + (order // 2 ^ batch)
        small_all = jnp.sum(
            jnp.where(rel_of[:, None, None] == order[None, :, None], small_all[None].astype(f32), 0.0), axis=1
        )
    else:
        small_all = lax.all_gather(small, ("batch", "seq"), axis=0, tiled=True).astype(f32)
    gain_one, bias_one, gain_two, bias_two = (
        small_all[:, i * group : i * group + group].reshape(1, model) for i in range(4)
    )
    taps = small_all[:, 4 * group : 4 * group + conv_kernel.size].reshape((groups,) + conv_kernel.shape)
    taps = taps.transpose(1, 2, 0, 3).reshape(3, width, KERNEL).transpose(2, 0, 1).reshape(KERNEL, 3 * width)
    taps = pad_heads(taps, width)

    qkv = qkv_weight
    shard = jnp.concatenate(
        [qkv[:, 0, :128], qkv[:, 1, :128], qkv[:, 2, :128], qkv[:, 0, 128:], qkv[:, 1, 128:], qkv[:, 2, 128:],
         jnp.zeros((group, PADW - width), b16)], axis=1,
    )
    w_own, w_other = gather_rows(shard)

    x_pieces = gather_heads(x_own)
    y_pieces = gather_heads(swap(x_own, "seq", 1))

    normed_one, form_one, projected, wpad, query, key, value = call(
        functools.partial(front_body, half, quarter),
        [
            ((half, model), b16), ((half, model), b16), ((half + 16, 3 * PADW), b16), ((model, 3 * PADW), b16),
            ((half, PADW), b16), ((2 * half, PADW), b16), ((2 * half, PADW), b16),
        ],
        scal, *x_pieces, *y_pieces, w_own, w_other, gain_one, bias_one, taps,
        scratch=[pltpu.VMEM((2 * half, model), b16), pltpu.VMEM((2 * half + 16, 3 * PADW), b16)],
        flops=4 * half * model * 3 * width,
    )

    inner_wo = jnp.concatenate(
        [inner_weight, jnp.pad(out_weight.T, ((0, 0), (0, PADW - width)))], axis=1
    )
    first_own, first_other = gather_rows(inner_wo)
    second_own, second_other = gather_rows(outer_weight.T)
    inner_full, wo_own, outer_full = call(
        weights_body,
        [((model, hidden), b16), ((model, PADW), b16), ((model, hidden), b16)],
        scal, first_own, second_own, first_other, second_other,
    )
    wo_pieces = gather_heads(wo_own)
    cot_pieces = gather_heads(cot_own)

    packed, out_t, lse = call(
        functools.partial(attention_body, half, heads),
        [((half + half // 2, 128), b16), ((width, half), f32), ((8, half), f32)],
        scal, query, key, value,
        scratch=[
            pltpu.VMEM((width, 2 * half), b16), pltpu.VMEM((heads, half, PADW), b16),
            pltpu.VMEM((8, half), f32), pltpu.VMEM((8, half), f32),
        ],
        flops=4 * half * half * width,
    )
    packed_pieces = gather_heads(packed)

    normed_two, squared, inner_grad, keep, sent, middle_own = call(
        functools.partial(feed_body, half, quarter),
        [((half, model), b16), ((half, hidden), b16), ((half, hidden), b16),
         ((2 * quarter, model), f32), ((2 * quarter, model), b16), ((quarter, model), f32)],
        scal, *packed_pieces, *wo_pieces, *x_pieces, *cot_pieces, inner_full, outer_full, gain_two, bias_two,
        flops=2 * half * model * (model + 3 * hidden),
    )
    dn_here, dn_far = scatter_heads(keep, sent)
    middle_grad, branch, sums_two = call(
        norm_back_body,
        [((quarter, model), f32), ((quarter, model), b16), ((8, model), f32)],
        scal, dn_here, dn_far, middle_own, cot_own, gain_two,
    )
    branch_pieces = gather_heads(branch)

    keep, sent, in_keep, in_send, ff_keep, ff_send = call(
        functools.partial(feed_grads_body, half, quarter),
        [((2 * quarter, model), f32), ((2 * quarter, model), b16)]
        + [(stacks + (hidden,), d) for d in (f32, b16, f32, b16)],
        scal, *cot_pieces, normed_two, squared, inner_grad, outer_full,
        scratch=[pltpu.VMEM((half, model), b16), pltpu.VMEM((model, hidden), f32)],
        flops=6 * half * model * hidden,
    )
    out_here, out_far = scatter_heads(keep, sent)
    block_output = (middle_own + out_here + out_far.astype(f32)).astype(b16)
    inner_out = scatter_rows(in_keep, in_send)
    outer_out = scatter_rows(ff_keep, ff_send)

    remote, query_t, dout, row_dot, kt, pj_keep, pj_send = call(
        functools.partial(remote_back_body, half, quarter, heads),
        [((half, 384), b16), ((width, half), f32), ((half, PADW), b16), ((8, half), f32), ((width, 2 * half), b16),
         (stacks + (width,), f32), (stacks + (width,), b16)],
        scal, *branch_pieces, wo_own, query, key, value, out_t, lse,
        scratch=[
            pltpu.VMEM((heads, half, PADW), b16), pltpu.VMEM((heads, half, PADW), b16),
            pltpu.VMEM((KB, PADW), f32), pltpu.VMEM((KB, PADW), f32),
            pltpu.VMEM((width, model), f32), pltpu.VMEM((model, width), f32),
        ],
        flops=10 * half * half * width,
    )
    remote_in = lax.ppermute(remote, "seq", [(1, 0)])
    proj_out = scatter_rows(pj_keep, pj_send)

    dq, dk, dv, front = call(
        functools.partial(local_back_body, half, heads),
        [((half, PADW), f32), ((half, PADW), f32), ((half, PADW), f32), ((8, 3 * PADW), f32)],
        scal, query, key, value, dout, lse, row_dot, kt, query_t, taps,
        scratch=[
            pltpu.VMEM((heads, half, PADW), b16), pltpu.VMEM((heads, half, PADW), b16),
            pltpu.VMEM((KB, PADW), f32), pltpu.VMEM((KB, PADW), f32), pltpu.VMEM((width, half), f32),
        ],
        flops=10 * half * half * width,
    )
    front_in = lax.ppermute(front, "seq", [(1, 0)])

    keep, sent, w_keep, w_send, sums = call(
        functools.partial(tail_body, half, quarter),
        [((2 * quarter, model), f32), ((2 * quarter, model), b16),
         (stacks + (640,), f32), (stacks + (640,), b16), ((8, 3 * PADW), f32)],
        scal, dq, dk, dv, remote_in, front_in, projected, normed_one, form_one, wpad, taps,
        scratch=[
            pltpu.VMEM((half + 16, 3 * PADW), b16), pltpu.VMEM((half, 3 * PADW), b16),
            pltpu.VMEM((model, 3 * PADW), f32), pltpu.VMEM((model, 640), f32),
        ],
        flops=4 * half * model * 3 * width,
    )
    norms = jnp.concatenate([sums[0:2], sums_two[0:2]])
    norms = norms + swap(norms, "heads", 1)
    norms = norms + swap(norms, "heads", 2)
    small = jnp.concatenate([norms, sums[4:8]])
    if pairwise(group):
        small = small + swap(small, "seq", 1)
        small = sum([swap(small, "batch", by) for by in range(1, groups // 2)], small)
    else:
        small = lax.psum(small, ("batch", "seq"))

    dn_here, dn_far = scatter_heads(keep, sent)
    qkv_out = scatter_rows(w_keep, w_send)
    input_grad, _, _ = call(
        norm_back_body,
        [((quarter, model), f32), ((quarter, model), b16), ((8, model), f32)],
        scal, dn_here, dn_far, x_own, middle_grad, gain_one,
    )

    qkv_out = jnp.stack(
        [
            jnp.concatenate([qkv_out[:, 0:128], qkv_out[:, 384:448]], axis=1),
            jnp.concatenate([qkv_out[:, 128:256], qkv_out[:, 448:512]], axis=1),
            jnp.concatenate([qkv_out[:, 256:384], qkv_out[:, 512:576]], axis=1),
        ],
        axis=1,
    )
    gains = lax.dynamic_slice_in_dim(small[0:4], own * group, group, 1)
    kernel_out = small[4 : 4 + KERNEL].reshape(KERNEL, 3, PADW)[:, :, :width].reshape(KERNEL, 3, heads, HEAD_DIM)
    kernel_out = kernel_out.transpose(1, 2, 3, 0).reshape(3, heads, HEAD_DIM * KERNEL)
    share = conv_kernel.shape[2]
    kernel_out = lax.dynamic_slice_in_dim(kernel_out, own * share, share, 2)
    return (
        block_output.reshape(block_input.shape),
        input_grad.reshape(block_input.shape),
        gains[0],
        gains[1],
        qkv_out,
        kernel_out,
        proj_out.T,
        gains[2],
        gains[3],
        inner_out,
        outer_out.T,
    )


def solution(mesh):
    return jax.shard_map(
        on_device,
        mesh=mesh,
        in_specs=(
            P("batch", "seq", "heads", None),
            P("batch", None),
            P(("batch", "seq")),
            P(("batch", "seq")),
            P(("batch", "seq"), None, "heads"),
            P(None, "heads", ("batch", "seq")),
            P("heads", ("batch", "seq")),
            P(("batch", "seq")),
            P(("batch", "seq")),
            P(("batch", "seq"), "heads"),
            P("heads", ("batch", "seq")),
            P("batch", "seq", "heads", None),
        ),
        out_specs=(
            P("batch", "seq", "heads", None),
            P("batch", "seq", "heads", None),
            P(("batch", "seq")),
            P(("batch", "seq")),
            P(("batch", "seq"), None, "heads"),
            P(None, "heads", ("batch", "seq")),
            P("heads", ("batch", "seq")),
            P(("batch", "seq")),
            P(("batch", "seq")),
            P(("batch", "seq"), "heads"),
            P("heads", ("batch", "seq")),
        ),
        check_vma=False,
    )
```

```python
import functools

import jax
import jax.numpy as jnp
from jax import lax
from jax.experimental import pallas as pl
from jax.experimental.pallas import tpu as pltpu
from jax.sharding import PartitionSpec as P

HEAD_DIM = 64
KERNEL = 3
DOCS = 4
PADW = 256
QB = 512
KB = 256

epsilon = 1e-05
masked_score = -1e30
f32 = jnp.float32
b16 = jnp.bfloat16

VMEM = pl.BlockSpec(memory_space=pltpu.VMEM)
SMEM = pl.BlockSpec(memory_space=pltpu.SMEM)


def after(value, *others):
    return lax.optimization_barrier((value,) + others)[0]


def swap(shard, axis, by):
    return lax.ppermute(shard, axis, [(i, i ^ by) for i in range(lax.axis_size(axis))])


def gather_heads(shard):
    far = swap(shard, "heads", 2)
    near = swap(shard, "heads", 1)
    return [shard, near, far, swap(far, "heads", 1)]


def pairwise(group):
    return group % 32 == 0


def gather_batch(shard):
    if not pairwise(shard.shape[0]):
        return (shard,)
    return (shard,) + tuple(swap(shard, "batch", by) for by in range(1, lax.axis_size("batch")))


def gather_seq(shards):
    rows, columns = shards[0].shape
    if not pairwise(rows):
        whole = lax.all_gather(shards[0], ("batch", "seq"), axis=0, tiled=True)
        return tuple(whole.reshape(2, 1, -1, columns))
    stack = jnp.stack(shards)
    return stack, swap(stack, "seq", 1)


def scatter_seq(sent):
    return sent if sent.shape[0] == 1 else swap(sent, "seq", 1)


def join_seq(*parts):
    if parts[0][0].shape[0] == 1:
        whole = [jnp.concatenate([keep[0].astype(b16), sent[0]]) for keep, sent in parts]
        return None, jnp.concatenate(whole, axis=-1)
    total = jnp.concatenate([keep.astype(f32) + got.astype(f32) for keep, got in parts], axis=-1)
    return total[0], total[1:].astype(b16)


def scatter_batch(own, rest, more, *others):
    if own is None:
        total = lax.psum_scatter(rest, ("batch", "seq"), scatter_dimension=0, tiled=True).astype(f32)
        return total, None if more is None else lax.psum(more, "batch")
    count = own.shape[0]
    payloads = [rest[by] for by in range(rest.shape[0])]
    if more is not None:
        tail = jnp.pad(more, ((0, 0), (0, own.shape[1] - more.shape[1]))).astype(b16)
        payloads = [jnp.concatenate([payload, tail]) for payload in payloads]
    pieces = [swap(payload, "batch", by + 1) for by, payload in enumerate(payloads)]
    for piece in after(pieces, *others):
        own = own + piece[:count].astype(f32)
        if more is not None:
            more = more + piece[count:, : more.shape[1]].astype(f32)
    return own, more


def scatter_far(keep, got, rows):
    far = (keep[rows:].astype(f32) + got[rows:].astype(f32)).astype(b16)
    here = keep[:rows].astype(f32) + got[:rows].astype(f32)
    return here, swap(far, "heads", 2)


def call(body, outs, *args, scratch=(), flops=0, limit=16, plain=False):
    in_specs = [pl.BlockSpec()] * len(args) if plain else [SMEM] + [VMEM] * (len(args) - 1)
    return pl.pallas_call(
        body,
        out_shape=[jax.ShapeDtypeStruct(*o) for o in outs],
        in_specs=in_specs,
        out_specs=[VMEM] * len(outs),
        scratch_shapes=list(scratch),
        compiler_params=pltpu.CompilerParams(vmem_limit_bytes=limit << 20),
        cost_estimate=pl.CostEstimate(
            flops=flops,
            transcendentals=0,
            bytes_accessed=sum(a.size * a.dtype.itemsize for a in args),
        ),
    )(*args)


def dot(a, b, ca=1, cb=0):
    return lax.dot_general(a, b, (((ca,), (cb,)), ((), ())), preferred_element_type=f32)


def edges(scal):
    return [scal[3 + d] for d in range(DOCS)]


def doc_start(pos, bounds):
    start = bounds[0] + jnp.zeros_like(pos)
    for edge in bounds[1:]:
        start = jnp.where(pos >= edge, edge, start)
    return start


def lanes_like(shape):
    return lax.broadcasted_iota(jnp.int32, shape, 1)


def half_roll(block):
    return pltpu.roll(block, 64, 1)


def norm_rows(values):
    average = jnp.mean(values, axis=-1, keepdims=True)
    centered = values - average
    inverse = lax.rsqrt(jnp.mean(centered * centered, axis=-1, keepdims=True) + epsilon)
    return centered * inverse, inverse


def group_rows(stack, rel, rel_seq, scal):
    count = stack.shape[1]
    if stack.shape[0] == 1:
        return slice(rel_seq * count, rel_seq * count + count)
    return pl.ds(pl.multiple_of(((scal[1] ^ rel) * 2 + (scal[2] ^ rel_seq)) * count, 32), count)


def ds(start, size):
    return pl.ds(pl.multiple_of(start, size), size)


def shard_body(heads, qkv, out_w, small, kernel, shard, rows):
    for part in range(3):
        shard[:, part * 128 : part * 128 + 128] = qkv[part, :, 0:128]
    thirds = [qkv[part, :, 128:192].astype(f32) for part in range(3)]
    turned = out_w[...].astype(f32).T
    shard[:, 384:512] = jnp.concatenate(thirds[:2], axis=1).astype(b16)
    shard[:, 512:640] = jnp.concatenate([thirds[2], turned[:, 0:64]], axis=1).astype(b16)
    shard[:, 640:768] = turned[:, 64:192].astype(b16)
    rows[...] = jnp.zeros_like(rows)
    count = kernel.shape[2]
    rows[0:4, 0 : small.shape[1]] = small[...].astype(f32)
    for part in range(3):
        rows[4 + part * heads : 4 + part * heads + heads, 0:count] = kernel[part].astype(f32)
    shard[:, 768:896] = rows[...].T[: shard.shape[0]].astype(b16)


def small_rows(scal, stacks, heads, norms, taps, columns, features):
    count = features.shape[0] // (2 * stacks[0].shape[0])
    for rel_seq, stack in enumerate(stacks):
        for rel in range(stack.shape[0]):
            block = stack[rel, :, 768:896].astype(f32)
            columns[group_rows(stack, rel, rel_seq, scal), :] = block
            group = (scal[1] ^ rel) * 2 + (scal[2] ^ rel_seq)
            features[pl.ds(pl.multiple_of(group * count, 8), count), :] = block[0:count]
    norms[...] = columns[...].T[0:8]
    taps[...] = jnp.zeros_like(taps)
    low = lanes_like((1, 128)) < 64
    for tap in range(KERNEL):
        turned = features[pl.ds(tap, HEAD_DIM, stride=KERNEL), :].T
        turned = jnp.concatenate([turned, jnp.zeros_like(turned)], axis=1)
        for part in range(3):
            one, two, three = (turned[4 + part * heads + i : 5 + part * heads + i] for i in range(3))
            taps[4 + tap : 5 + tap, part * PADW : part * PADW + 128] = jnp.where(low, one, half_roll(two))
            taps[4 + tap : 5 + tap, part * PADW + 128 : part * PADW + 256] = jnp.where(low, three, 0.0)


def front_body(half, quarter, heads, paired, scal, *refs):
    pieces, refs = refs[:4], refs[4:]
    w_own, w_other, cot = refs[:3]
    refs = refs[3:]
    if not paired:
        norms_in, taps_in, refs = refs[0], refs[1], refs[2:]
    normed, form, projected, wpad, query, key, value, extra, norms, taps = refs[:10]
    rows_in, proj, columns, features, wo = refs[10:]
    head = scal[0]
    if paired:
        small_rows(scal, (w_own, w_other), heads, norms, taps, columns, features)
    else:
        norms[...] = norms_in[...]
        taps[...] = taps_in[...]
    gain, bias = norms[0:1, :], norms[1:2, :]
    low = lanes_like((w_own.shape[1], 128)) < 64
    for rel_seq, stack in enumerate((w_own, w_other)):
        for rel in range(stack.shape[0]):
            rows = group_rows(stack, rel, rel_seq, scal)
            for part in range(3):
                wpad[rows, part * 256 : part * 256 + 128] = stack[rel, :, part * 128 : part * 128 + 128]
            shared = stack[rel, :, 384:512].astype(f32)
            wpad[rows, 128:256] = jnp.where(low, shared, 0.0).astype(b16)
            wpad[rows, 384:512] = jnp.where(low, half_roll(shared), 0.0).astype(b16)
            mid = stack[rel, :, 512:640].astype(f32)
            last = half_roll(stack[rel, :, 640:768].astype(f32))
            wpad[rows, 640:768] = jnp.where(low, mid, 0.0).astype(b16)
            wo[rows, 0:128] = jnp.where(low, half_roll(mid), last)
            wo[rows, 128:256] = last
    extra[0:quarter, :] = cot[...]
    width = heads * HEAD_DIM
    extra[quarter : quarter + width, :] = wo[...].T[0:width].astype(b16)
    for index, piece in enumerate(pieces):
        base = (head ^ index) * quarter
        rows_in[ds(half + base, quarter), :] = piece[0:quarter, :]
        rows_in[ds(base, quarter), :] = piece[quarter : 2 * quarter, :]
    proj[0:16, :] = jnp.zeros((16, proj.shape[1]), b16)

    def project(block, own):
        base = block * quarter
        hat, _ = norm_rows(rows_in[ds(base, quarter), :].astype(f32))
        rounded = (hat * gain + bias).astype(b16)
        proj[pl.ds(pl.multiple_of(base + 16, 16), quarter), :] = dot(rounded, wpad[...]).astype(b16)
        if own:
            rows = ds(base - half, quarter)
            normed[rows, :] = rounded
            form[rows, :] = hat.astype(b16)

    @pl.loop(0, 4)
    def _(block):
        project(block, False)

    @pl.loop(4, 8)
    def _(block):
        project(block, True)

    projected[...] = proj[half : 2 * half + 16, :]
    bounds = edges(scal)

    def convolve(block, own):
        base = block * quarter
        pos = base + lax.broadcasted_iota(jnp.int32, (quarter, 1), 0)
        start = doc_start(pos, bounds)
        for part, out in enumerate((query, key, value)):
            if part == 0 and not own:
                continue
            cols = slice(part * PADW, part * PADW + PADW)
            rows = proj[pl.ds(pl.multiple_of(base, 16), quarter + 16), cols].astype(f32)
            mixed = taps[4:5, cols] * rows[16:]
            for back in range(1, KERNEL):
                earlier = pltpu.roll(rows, back, 0)[16:]
                mixed = mixed + jnp.where(pos - back >= start, taps[4 + back : 5 + back, cols] * earlier, 0.0)
            mixed = mixed.astype(b16)
            if part == 0:
                out[ds(base - half, quarter), :] = mixed * jnp.asarray(HEAD_DIM**-0.5, b16)
            else:
                out[ds(base, quarter), :] = mixed

    @pl.loop(0, 4)
    def _(block):
        convolve(block, False)

    @pl.loop(4, 8)
    def _(block):
        convolve(block, True)


def masked_queries(query, slots, heads):
    lane = lanes_like(query.shape) // HEAD_DIM
    for head in range(heads):
        slots[head] = jnp.where(lane == head, query[...], jnp.zeros((), b16))


def attention_body(half, heads, scal, query, key, value, packed, out_t, lse, vt, qm, peak, total):
    bounds = edges(scal)
    masked_queries(query, qm, heads)

    @pl.loop(0, 2 * half // 256)
    def _(block):
        turned = value[ds(block * 256, 256), :].astype(f32).T
        vt[:, ds(block * 256, 256)] = turned[: heads * HEAD_DIM].astype(b16)

    out_t[...] = jnp.zeros_like(out_t)
    peak[...] = jnp.full_like(peak, masked_score)
    total[...] = jnp.zeros_like(total)
    for block in range(half // QB):
        first = half + block * QB
        cols = slice(block * QB, block * QB + QB)
        pos = first + lanes_like((1, QB))
        start = doc_start(pos, bounds)
        low = doc_start(jnp.int32(first), bounds) // KB

        @pl.loop(low, (first + QB) // KB)
        def _(kb):
            keys = key[ds(kb * KB, KB), :]
            key_pos = kb * KB + lax.broadcasted_iota(jnp.int32, (KB, 1), 0)
            allowed = (key_pos >= start) & (key_pos <= pos)
            for head in range(heads):
                rows = slice(head * HEAD_DIM, head * HEAD_DIM + HEAD_DIM)
                one = slice(head, head + 1)
                scores = dot(keys, qm[head, cols, :], 1, 1)
                scores = jnp.where(allowed, scores, masked_score)
                old = peak[one, cols]
                new = jnp.maximum(old, jnp.max(scores, axis=0, keepdims=True))
                weights = jnp.exp(scores - new)
                shrink = jnp.exp(old - new)
                peak[one, cols] = new
                total[one, cols] = shrink * total[one, cols] + jnp.sum(weights, axis=0, keepdims=True)
                out_t[rows, cols] = shrink * out_t[rows, cols] + dot(
                    vt[rows, ds(kb * KB, KB)], weights.astype(b16)
                )

    for head in range(heads):
        rows = slice(head * HEAD_DIM, head * HEAD_DIM + HEAD_DIM)
        out_t[rows, :] = out_t[rows, :] / total[head : head + 1, :]
    lse[...] = peak[...] + jnp.log(jnp.maximum(total[...], 1e-30))
    for block in range(half // 256):
        cols = slice(block * 256, block * 256 + 256)
        packed[cols, :] = out_t[0:128, cols].T.astype(b16)
    for block in range(half // 512):
        cols = slice(block * 256, block * 256 + 256)
        later = slice(half // 2 + block * 256, half // 2 + block * 256 + 256)
        both = jnp.concatenate([out_t[128:192, cols], out_t[128:192, later]], axis=0)
        packed[half + block * 256 : half + block * 256 + 256, :] = both.T.astype(b16)


def back_blocks(half, heads, scal, first_kb, last_kb, refs, finish):
    key, value, qm, dom, lse, row_dot, kt, query_t, key_sum, value_sum = refs
    bounds = edges(scal)

    @pl.loop(first_kb, last_kb)
    def _(kb):
        key_sum[...] = jnp.zeros_like(key_sum)
        value_sum[...] = jnp.zeros_like(value_sum)
        for block in range(half // QB):
            first = half + block * QB
            cols = slice(block * QB, block * QB + QB)
            low = doc_start(jnp.int32(first), bounds)

            @pl.when((kb * KB + KB > low) & (kb * KB < first + QB))
            def _():
                pos = first + lanes_like((1, QB))
                start = doc_start(pos, bounds)
                keys = key[ds(kb * KB, KB), :]
                values = value[ds(kb * KB, KB), :]
                key_pos = kb * KB + lax.broadcasted_iota(jnp.int32, (KB, 1), 0)
                allowed = (key_pos >= start) & (key_pos <= pos)
                for head in range(heads):
                    rows = slice(head * HEAD_DIM, head * HEAD_DIM + HEAD_DIM)
                    one = slice(head, head + 1)
                    own_q = qm[head, cols, :]
                    own_g = dom[head, cols, :]
                    scores = jnp.where(allowed, dot(keys, own_q, 1, 1) - lse[one, cols], masked_score)
                    weights = jnp.exp(scores)
                    grads = weights * (dot(values, own_g, 1, 1) - row_dot[one, cols])
                    grads = grads.astype(b16)
                    value_sum[...] += dot(weights.astype(b16), own_g)
                    key_sum[...] += dot(grads, own_q)
                    query_t[rows, cols] += dot(kt[rows, ds(kb * KB, KB)], grads)

        finish(kb, key_sum[...], value_sum[...])


def spread_groups(source, scal, keep, sent, cols=slice(None)):
    for rel_seq, out in enumerate((keep, sent)):
        for rel in range(out.shape[0]):
            out[rel, :, cols] = source[group_rows(out, rel, rel_seq, scal), :].astype(out.dtype)


def branch_body(quarter, heads, scal, *refs):
    branches = refs[:4]
    extra, out_t, dout, row_dot, keep, sent, proj_grad, turned = refs[4:]
    head = scal[0]
    width = heads * HEAD_DIM
    weights = jnp.concatenate([extra[quarter:, :], jnp.zeros((PADW - width, extra.shape[1]), b16)], axis=0)
    proj_grad[...] = jnp.zeros_like(proj_grad)
    row_dot[...] = jnp.zeros_like(row_dot)
    for rel, branch in enumerate(branches):
        base = (head ^ rel) * quarter
        grad = dot(branch[...], weights, 1, 1).astype(b16)
        dout[ds(base, quarter), :] = grad
        attended = out_t[:, ds(base, quarter)]
        product = grad.astype(f32).T[:width] * attended
        for one in range(heads):
            row_dot[one : one + 1, ds(base, quarter)] = jnp.sum(
                product[one * HEAD_DIM : one * HEAD_DIM + HEAD_DIM], axis=0, keepdims=True
            )
        proj_grad[...] += dot(attended.astype(b16), branch[...])
    turned[...] = proj_grad[...].T
    spread_groups(turned, scal, keep, sent)


def remote_back_body(half, heads, scal, *refs):
    query, key, value, dout, lse, row_dot = refs[:6]
    remote, query_t, kt = refs[6:9]
    qm, dom, key_sum, value_sum = refs[9:]
    width = heads * HEAD_DIM
    masked_queries(query, qm, heads)
    masked_queries(dout, dom, heads)

    @pl.loop(0, 2 * half // 256)
    def _(block):
        kt[:, ds(block * 256, 256)] = key[ds(block * 256, 256), :].astype(f32).T[:width].astype(b16)

    query_t[...] = jnp.zeros_like(query_t)

    def finish(kb, dk, dv):
        rows = ds(kb * KB, KB)
        remote[rows, 0:128] = dk[:, 0:128].astype(b16)
        remote[rows, 128:256] = dv[:, 0:128].astype(b16)
        remote[rows, 256:384] = (dk[:, 128:256] + half_roll(dv[:, 128:256])).astype(b16)

    back_blocks(
        half, heads, scal, 0, half // KB,
        (key, value, qm, dom, lse, row_dot, kt, query_t, key_sum, value_sum), finish,
    )


def local_back_body(half, heads, scal, *refs):
    query, key, value, dout, lse, row_dot, kt, query_in, taps = refs[:9]
    dq, dk_out, dv_out, front = refs[9:13]
    qm, dom, key_sum, value_sum, query_t = refs[13:]
    masked_queries(query, qm, heads)
    masked_queries(dout, dom, heads)
    query_t[...] = query_in[...]

    def finish(kb, dk, dv):
        rows = ds(kb * KB - half, KB)
        dk_out[rows, :] = dk
        dv_out[rows, :] = dv

    back_blocks(
        half, heads, scal, half // KB, 2 * half // KB,
        (key, value, qm, dom, lse, row_dot, kt, query_t, key_sum, value_sum), finish,
    )
    width = heads * HEAD_DIM
    scale = HEAD_DIM**-0.5
    for block in range(half // 256):
        cols = slice(block * 256, block * 256 + 256)
        turned = (query_t[:, cols] * scale).T
        dq[cols, 0:128] = turned[:, 0:128].astype(b16)
        dq[cols, 128:256] = jnp.concatenate(
            [turned[:, 128:width], jnp.zeros((256, PADW - width), f32)], axis=1
        ).astype(b16)
    bounds = edges(scal)
    pos = half + lax.broadcasted_iota(jnp.int32, (8, 1), 0)
    start = doc_start(pos, bounds)
    for part, grads in enumerate((dq, dk_out, dv_out)):
        cols = slice(part * PADW, part * PADW + PADW)
        rounded = grads[0:16, :].astype(b16).astype(f32)[0:8]
        result = jnp.zeros((8, PADW), f32)
        for back in range(1, KERNEL):
            moved = pltpu.roll(jnp.where(pos - back >= start, taps[4 + back : 5 + back, cols] * rounded, 0.0), 8 - back, 0)
            place = lax.broadcasted_iota(jnp.int32, (8, 1), 0)
            result = result + jnp.where(place >= 8 - back, moved, 0.0)
        front[:, cols] = result


def weights_body(scal, *refs):
    own, other, inner, outer = refs
    width = inner.shape[1]
    for rel_seq, stack in enumerate((own, other)):
        for rel in range(stack.shape[0]):
            rows = group_rows(stack, rel, rel_seq, scal)
            inner[rows, :] = stack[rel, :, :width]
            outer[rows, :] = stack[rel, :, width:]


def feed_body(half, quarter, scal, *refs):
    attended, extras, inputs = refs[0:4], refs[4:8], refs[8:12]
    inner, outer, norms = refs[12:15]
    normed, squared, inner_grad, keep, sent, middle_own = refs[15:]
    head = scal[0]
    for rel in range(4):
        base = (head ^ rel) * quarter
        late = base >= half // 2
        middle = inputs[rel][0:quarter, :].astype(f32)
        for part in range(4):
            left = attended[part][ds(base, quarter), :]
            right = attended[part][ds(half + lax.rem(base, half // 2), quarter), :].astype(f32)
            right = jnp.where(late, half_roll(right), right).astype(b16)
            both = jnp.concatenate([left, right], axis=1)
            weights = extras[part][quarter:, :]
            middle = middle + dot(both[:, : weights.shape[0]], weights)
        if rel == 0:
            middle_own[...] = middle
        hat, _ = norm_rows(middle)
        rounded = (hat * norms[2:3, :] + norms[3:4, :]).astype(b16)
        rows = slice(rel * quarter, rel * quarter + quarter)
        normed[rows, :] = rounded
        positive = jnp.maximum(dot(rounded, inner[...]), 0.0)
        squared[rows, :] = (positive * positive).astype(b16)
        grads = (dot(extras[rel][0:quarter, :], outer[...]) * 2.0 * positive).astype(b16)
        inner_grad[rows, :] = grads
        part = dot(grads, inner[...], 1, 1)
        place = slice((rel // 2) * quarter, (rel // 2) * quarter + quarter)
        if rel % 2 == 0:
            keep[place, :] = part
        else:
            sent[place, :] = part.astype(b16)


def feed_grads_body(half, quarter, scal, *refs):
    extras = refs[0:4]
    normed, squared, inner_grad, outer = refs[4:8]
    keep, sent, kept, away = refs[8:12]
    cot, total = refs[12:]
    width = total.shape[1]
    for rel in range(4):
        rows = slice(rel * quarter, rel * quarter + quarter)
        cot[rows, :] = extras[rel][0:quarter, :]
        part = dot(squared[rows, :], outer[...], 1, 1)
        place = slice((rel // 2) * quarter, (rel // 2) * quarter + quarter)
        if rel % 2 == 0:
            keep[place, :] = part
        else:
            sent[place, :] = part.astype(b16)
    for place, left, right in ((0, normed, inner_grad), (width, cot, squared)):
        for tile in range(total.shape[0] // 256):
            cols = slice(tile * 256, tile * 256 + 256)
            total[cols, :] = dot(left[:, cols], right[...], 0, 0)
        spread_groups(total, scal, kept, away, slice(place, place + width))


def norm_back_body(row, scal, part, got, values, skip, norms, grad_in, rounded, sums):
    del scal
    grad = part[...] + got[0 : part.shape[0], :].astype(f32)
    hat, inverse = norm_rows(values[...].astype(f32))
    scaled = grad * norms[row : row + 1, :]
    back = inverse * (
        scaled
        - jnp.mean(scaled, axis=-1, keepdims=True)
        - hat * jnp.mean(scaled * hat, axis=-1, keepdims=True)
    )
    result = skip[...].astype(f32) + back
    grad_in[...] = result
    rounded[...] = result.astype(b16)
    sums[...] = jnp.zeros_like(sums)
    sums[0:1, :] = jnp.sum(grad * hat, axis=0, keepdims=True)
    sums[1:2, :] = jnp.sum(grad, axis=0, keepdims=True)


def tail_body(half, quarter, scal, *refs):
    dq, dk, dv, remote, front, projected, normed, taps = refs[:8]
    proj_grad, w_keep, w_send, sums = refs[8:12]
    mixed, total, dense = refs[12:]
    bounds = edges(scal)
    low = lanes_like((quarter, 128)) < 64
    sums[...] = jnp.zeros_like(sums)
    for block in range(half // quarter):
        rows = slice(block * quarter, block * quarter + quarter)
        shared = remote[rows, 256:384].astype(f32)
        mixed[rows, 0:256] = dq[rows, :]
        mixed[rows, 256:384] = (dk[rows, 0:128] + remote[rows, 0:128].astype(f32)).astype(b16)
        mixed[rows, 384:512] = (dk[rows, 128:256] + jnp.where(low, shared, 0.0)).astype(b16)
        mixed[rows, 512:640] = (dv[rows, 0:128] + remote[rows, 128:256].astype(f32)).astype(b16)
        mixed[rows, 640:768] = (dv[rows, 128:256] + jnp.where(low, half_roll(shared), 0.0)).astype(b16)
    mixed[half : half + 16, :] = jnp.zeros((16, mixed.shape[1]), b16)

    @pl.loop(0, half // quarter)
    def _(block):
        base = block * quarter
        pos = half + base + lax.broadcasted_iota(jnp.int32, (quarter + 16, 1), 0)
        start = doc_start(pos, bounds)
        for part in range(3):
            cols = slice(part * PADW, part * PADW + PADW)
            grads = mixed[pl.ds(pl.multiple_of(base, 16), quarter + 16), cols].astype(f32)
            values = projected[pl.ds(pl.multiple_of(base, 16), quarter + 16), cols].astype(f32)
            here = grads[:quarter]
            result = taps[4:5, cols] * here
            sums[4:5, cols] += jnp.sum(here * values[16:], axis=0, keepdims=True)
            for back in range(1, KERNEL):
                same = pos - back >= start
                held = jnp.where(same, grads, 0.0)
                ahead = pltpu.roll(held, quarter + 16 - back, 0)[:quarter]
                result = result + taps[4 + back : 5 + back, cols] * ahead
                earlier = pltpu.roll(values, back, 0)[16:]
                sums[4 + back : 5 + back, cols] += jnp.sum(held[:quarter] * earlier, axis=0, keepdims=True)
            proj_grad[ds(base, quarter), cols] = result.astype(b16)

        @pl.when(block == half // quarter - 1)
        def _():
            added = jnp.concatenate([jnp.zeros((8, front.shape[1]), f32), front[...]], axis=0)
            tail_pos = 2 * half - 16 + lax.broadcasted_iota(jnp.int32, (32, 1), 0)
            tail_start = doc_start(tail_pos, bounds)
            grads = mixed[half - 16 : half + 16, :].astype(f32)
            result = taps[4:5, :] * grads[:16]
            for back in range(1, KERNEL):
                held = jnp.where(tail_pos - back >= tail_start, grads, 0.0)
                result = result + taps[4 + back : 5 + back, :] * pltpu.roll(held, 32 - back, 0)[:16]
            proj_grad[half - 16 : half, :] = (result + added).astype(b16)

    for tile in range(total.shape[0] // 256):
        rows = slice(tile * 256, tile * 256 + 256)
        total[rows, :] = dot(normed[:, rows], proj_grad[...], 0, 0)
        for part in range(3):
            dense[rows, part * 128 : part * 128 + 128] = total[rows, part * 256 : part * 256 + 128]
        dense[rows, 384:512] = total[rows, 128:256] + half_roll(total[rows, 384:512])
        dense[rows, 512:640] = total[rows, 640:768]
    spread_groups(dense, scal, w_keep, w_send)


def tail_norm_body(quarter, scal, proj_grad, wpad, form, second, keep, sent, sums):
    head = scal[0]
    sums[...] = jnp.zeros_like(sums)
    sums[2:4, :] = second[0:2, :]
    for rel in (1, 3, 0, 2):
        base = (head ^ rel) * quarter
        part = dot(proj_grad[ds(base, quarter), :], wpad[...], 1, 1)
        sums[0:1, :] += jnp.sum(part * form[ds(base, quarter), :].astype(f32), axis=0, keepdims=True)
        sums[1:2, :] += jnp.sum(part, axis=0, keepdims=True)
        place = slice((rel // 2) * quarter, (rel // 2) * quarter + quarter)
        if rel % 2 == 0:
            keep[place, :] = part
        else:
            sent[place, :] = part.astype(b16)
    keep[2 * quarter :, :] = sums[...]
    sent[2 * quarter :, :] = sums[...].astype(b16)


def pad_heads(values, width):
    shaped = values.reshape(values.shape[:-1] + (3, width))
    padded = jnp.pad(shaped, [(0, 0)] * (shaped.ndim - 1) + [(0, PADW - width)])
    return padded.reshape(values.shape[:-1] + (3 * PADW,))


def gather_small(norms, conv_kernel, model, width):
    norms = lax.all_gather(norms, ("batch", "seq"), axis=0, tiled=True).astype(f32).T
    taps = lax.all_gather(conv_kernel, ("batch", "seq"), axis=2, tiled=True).astype(f32)
    taps = taps.reshape(3, width, KERNEL).transpose(2, 0, 1).reshape(KERNEL, 3 * width)
    return jnp.pad(norms, ((0, 4), (0, 0))), jnp.pad(pad_heads(taps, width), ((4, 1), (0, 0)))


def on_device(
    block_input, segment_ids, norm1_gain, norm1_bias, qkv_weight, conv_kernel, out_weight,
    norm2_gain, norm2_bias, inner_weight, outer_weight, cotangent,
):
    quarter = block_input.shape[2]
    half = quarter * lax.axis_size("heads")
    width = qkv_weight.shape[2]
    heads = width // HEAD_DIM
    group = qkv_weight.shape[0]
    groups = lax.axis_size("batch") * lax.axis_size("seq")
    model = group * groups
    hidden = inner_weight.shape[1]
    head, batch, seq = lax.axis_index("heads"), lax.axis_index("batch"), lax.axis_index("seq")
    own = batch * 2 + seq
    stacks = (groups // 2, group) if pairwise(group) else (1, model // 2)

    ids = segment_ids.reshape(-1)
    docs = jnp.arange(DOCS, dtype=jnp.int32)
    firsts = jnp.sum((ids[None, :] < docs[:, None]).astype(jnp.int32), axis=1) - (seq - 1) * half
    scal = jnp.concatenate([jnp.stack([head, batch, seq]), firsts, jnp.zeros((1,), jnp.int32)]).astype(jnp.int32)

    x_own = block_input.reshape(quarter, model)
    cot_own = cotangent.reshape(quarter, model)

    share = conv_kernel.shape[2]

    x_other = swap(x_own, "seq", 1)
    x_pieces = gather_heads(jnp.concatenate([x_own, x_other]))

    paired = pairwise(group)
    qkv = qkv_weight
    small = [norm1_gain, norm1_bias, norm2_gain, norm2_bias]
    small_args = []
    if paired:
        (shard,) = call(
            functools.partial(shard_body, heads), [((group, 896), b16)],
            qkv.transpose(1, 0, 2), out_weight, jnp.stack(small), conv_kernel,
            scratch=[pltpu.VMEM((128, 128), f32)], limit=4, plain=True,
        )
    else:
        small_args = gather_small(jnp.stack(small, axis=1), conv_kernel, model, width)
        shard = jnp.concatenate(
            [qkv[:, 0, :128], qkv[:, 1, :128], qkv[:, 2, :128], qkv[:, 0, 128:], qkv[:, 1, 128:], qkv[:, 2, 128:],
             out_weight.T, jnp.zeros((group, 128), b16)], axis=1,
        )
    shards = gather_batch(shard)
    w_own, w_other = gather_seq(shards)

    feed_shards = gather_batch(after(jnp.concatenate([inner_weight, outer_weight.T], axis=1), shards))

    normed_one, form_one, projected, wpad, query, key, value, extra, norms, taps = call(
        functools.partial(front_body, half, quarter, heads, paired),
        [
            ((half, model), b16), ((half, model), b16), ((half + 16, 3 * PADW), b16), ((model, 3 * PADW), b16),
            ((half, PADW), b16), ((2 * half, PADW), b16), ((2 * half, PADW), b16), ((quarter + width, model), b16),
            ((8, model), f32), ((8, 3 * PADW), f32),
        ],
        scal, *x_pieces, w_own, w_other, cot_own, *small_args,
        scratch=[
            pltpu.VMEM((2 * half, model), b16), pltpu.VMEM((2 * half + 16, 3 * PADW), b16),
            pltpu.VMEM((model, 128), f32), pltpu.VMEM((KERNEL * HEAD_DIM, 128), f32), pltpu.VMEM((model, PADW), f32),
        ],
        flops=4 * half * model * 3 * width, limit=12,
    )

    feed_own, feed_other = gather_seq(after(feed_shards, query))
    extra_pieces = gather_heads(extra)

    packed, out_t, lse = call(
        functools.partial(attention_body, half, heads),
        [((half + half // 2, 128), b16), ((width, half), f32), ((8, half), f32)],
        scal, query, key, value,
        scratch=[
            pltpu.VMEM((width, 2 * half), b16), pltpu.VMEM((heads, half, PADW), b16),
            pltpu.VMEM((8, half), f32), pltpu.VMEM((8, half), f32),
        ],
        flops=4 * half * half * width, limit=7,
    )
    packed_pieces = gather_heads(packed)
    feed_own, feed_other, _ = lax.optimization_barrier((feed_own, feed_other, packed))
    inner_full, outer_full = call(
        weights_body, [((model, hidden), b16), ((model, hidden), b16)], scal, feed_own, feed_other, limit=4,
    )

    normed_two, squared, inner_grad, keep, sent, middle_own = call(
        functools.partial(feed_body, half, quarter),
        [((half, model), b16), ((half, hidden), b16), ((half, hidden), b16),
         ((2 * quarter, model), f32), ((2 * quarter, model), b16), ((quarter, model), f32)],
        scal, *packed_pieces, *extra_pieces, *x_pieces, inner_full, outer_full, norms,
        flops=2 * half * model * (model + 3 * hidden), limit=12,
    )
    got = swap(sent, "heads", 1)
    out_keep, out_sent, ff_keep, ff_send = call(
        functools.partial(feed_grads_body, half, quarter),
        [((2 * quarter, model), f32), ((2 * quarter, model), b16),
         (stacks + (2 * hidden,), b16), (stacks + (2 * hidden,), b16)],
        scal, *extra_pieces, normed_two, squared, inner_grad, outer_full,
        scratch=[pltpu.VMEM((half, model), b16), pltpu.VMEM((model, hidden), f32)],
        flops=6 * half * model * hidden, limit=10,
    )
    ff_got = scatter_seq(ff_send)
    dn_here, dn_far = scatter_far(keep, after(got, ff_send), quarter)
    middle_grad, branch, sums_two = call(
        functools.partial(norm_back_body, 2),
        [((quarter, model), f32), ((quarter, model), b16), ((8, model), f32)],
        scal, dn_here, dn_far, middle_own, cot_own, norms, limit=6,
    )
    branch_pieces = gather_heads(branch)
    out_got = swap(after(out_sent, branch), "heads", 1)

    dout, row_dot, pj_keep, pj_send = call(
        functools.partial(branch_body, quarter, heads),
        [((half, PADW), b16), ((8, half), f32), (stacks + (width,), f32), (stacks + (width,), b16)],
        scal, *branch_pieces, extra, out_t,
        scratch=[pltpu.VMEM((width, model), f32), pltpu.VMEM((model, width), f32)],
        flops=4 * half * model * width, limit=6,
    )
    pj_got = scatter_seq(pj_send)
    out_here, out_far = scatter_far(out_keep, after(out_got, dout), quarter)
    remote, query_t, kt = call(
        functools.partial(remote_back_body, half, heads),
        [((half, 384), b16), ((width, half), f32), ((width, 2 * half), b16)],
        scal, query, key, value, dout, lse, row_dot,
        scratch=[
            pltpu.VMEM((heads, half, PADW), b16), pltpu.VMEM((heads, half, PADW), b16),
            pltpu.VMEM((KB, PADW), f32), pltpu.VMEM((KB, PADW), f32),
        ],
        flops=10 * half * half * width, limit=8,
    )
    remote_in = lax.ppermute(remote, "seq", [(1, 0)])

    dq, dk, dv, front = call(
        functools.partial(local_back_body, half, heads),
        [((half, PADW), b16), ((half, PADW), f32), ((half, PADW), f32), ((8, 3 * PADW), f32)],
        scal, query, key, value, dout, lse, row_dot, kt, query_t, taps,
        scratch=[
            pltpu.VMEM((heads, half, PADW), b16), pltpu.VMEM((heads, half, PADW), b16),
            pltpu.VMEM((KB, PADW), f32), pltpu.VMEM((KB, PADW), f32), pltpu.VMEM((width, half), f32),
        ],
        flops=10 * half * half * width, limit=8,
    )
    front_in = lax.ppermute(front, "seq", [(1, 0)])
    ff_got, pj_got = after((ff_got, pj_got), dq)
    ff_own, ff_rest = join_seq((ff_keep, ff_got), (pj_keep, pj_got))

    proj_grad, w_keep, w_send, sums_taps = call(
        functools.partial(tail_body, half, quarter),
        [((half, 3 * PADW), b16), (stacks + (640,), f32), (stacks + (640,), b16), ((8, 3 * PADW), f32)],
        scal, dq, dk, dv, remote_in, front_in, projected, normed_one, taps,
        scratch=[
            pltpu.VMEM((half + 16, 3 * PADW), b16), pltpu.VMEM((model, 3 * PADW), f32), pltpu.VMEM((model, 640), f32),
        ],
        flops=2 * half * model * 3 * width, limit=12,
    )
    w_got = scatter_seq(w_send)
    keep, sent, sums = call(
        functools.partial(tail_norm_body, quarter),
        [((2 * quarter + 8, model), f32), ((2 * quarter + 8, model), b16), ((8, model), f32)],
        scal, proj_grad, wpad, form_one, sums_two,
        flops=2 * half * model * 3 * width, limit=8,
    )
    got = swap(sent, "heads", 1)
    dn_here, dn_far = scatter_far(keep, got, quarter)
    ff_out, _ = scatter_batch(ff_own, ff_rest, None, sent)

    small = sums + got[2 * quarter :].astype(f32) + dn_far[quarter:].astype(f32)
    small = jnp.concatenate([small[0:4], sums_taps[4:8]])
    small = small + swap(small, "seq", 1)
    cut = small.shape[1] // 2
    small = jnp.concatenate([small[:, :cut], small[:, cut:]])
    qkv_own, qkv_rest = join_seq((w_keep, w_got))
    qkv_out, small = scatter_batch(qkv_own, qkv_rest, small)
    small = jnp.concatenate([small[:8], small[8:]], axis=1)
    input_grad, _, _ = call(
        functools.partial(norm_back_body, 0),
        [((quarter, model), f32), ((quarter, model), b16), ((8, model), f32)],
        scal, dn_here, dn_far, x_own, middle_grad, norms, limit=6,
    )
    block_output = (middle_own + out_here + out_far.astype(f32)).astype(b16)

    qkv_out = jnp.stack(
        [
            jnp.concatenate([qkv_out[:, 0:128], qkv_out[:, 384:448]], axis=1),
            jnp.concatenate([qkv_out[:, 128:256], qkv_out[:, 448:512]], axis=1),
            jnp.concatenate([qkv_out[:, 256:384], qkv_out[:, 512:576]], axis=1),
        ],
        axis=1,
    )
    gains = lax.dynamic_slice_in_dim(small[0:4], own * group, group, 1)
    kernel_out = small[4 : 4 + KERNEL].reshape(KERNEL, 3, PADW)[:, :, :width].reshape(KERNEL, 3, heads, HEAD_DIM)
    kernel_out = kernel_out.transpose(1, 2, 3, 0).reshape(3, heads, HEAD_DIM * KERNEL)
    kernel_out = lax.dynamic_slice_in_dim(kernel_out, own * share, share, 2)
    return (
        block_output.reshape(block_input.shape),
        input_grad.reshape(block_input.shape),
        gains[0],
        gains[1],
        qkv_out,
        kernel_out,
        ff_out[:, 2 * hidden :].T,
        gains[2],
        gains[3],
        ff_out[:, :hidden],
        ff_out[:, hidden : 2 * hidden].T,
    )


def solution(mesh):
    return jax.shard_map(
        on_device,
        mesh=mesh,
        in_specs=(
            P("batch", "seq", "heads", None),
            P("batch", None),
            P(("batch", "seq")),
            P(("batch", "seq")),
            P(("batch", "seq"), None, "heads"),
            P(None, "heads", ("batch", "seq")),
            P("heads", ("batch", "seq")),
            P(("batch", "seq")),
            P(("batch", "seq")),
            P(("batch", "seq"), "heads"),
            P("heads", ("batch", "seq")),
            P("batch", "seq", "heads", None),
        ),
        out_specs=(
            P("batch", "seq", "heads", None),
            P("batch", "seq", "heads", None),
            P(("batch", "seq")),
            P(("batch", "seq")),
            P(("batch", "seq"), None, "heads"),
            P(None, "heads", ("batch", "seq")),
            P("heads", ("batch", "seq")),
            P(("batch", "seq")),
            P(("batch", "seq")),
            P(("batch", "seq"), "heads"),
            P("heads", ("batch", "seq")),
        ),
        check_vma=False,
    )
```

```python
import functools

import jax
import jax.numpy as jnp
from jax import lax
from jax.experimental import pallas as pl
from jax.experimental.pallas import tpu as pltpu
from jax.sharding import PartitionSpec as P

HEAD_DIM = 64
KERNEL = 3
DOCS = 4
PADW = 256
QB = 512
QF = 256
KB = 256

epsilon = 1e-05
masked_score = -1e30
f32 = jnp.float32
b16 = jnp.bfloat16

VMEM = pl.BlockSpec(memory_space=pltpu.VMEM)
SMEM = pl.BlockSpec(memory_space=pltpu.SMEM)


def after(value, *others):
    return lax.optimization_barrier((value,) + others)[0]


def swap(shard, axis, by):
    return lax.ppermute(shard, axis, [(i, i ^ by) for i in range(lax.axis_size(axis))])


def gather_heads(shard):
    far = swap(shard, "heads", 2)
    near = swap(shard, "heads", 1)
    return [shard, near, far, swap(far, "heads", 1)]


def gather_cores(shard, far):
    both = jnp.concatenate([shard, far])
    return [both, swap(both, "heads", 1)]


def pairwise(group):
    return group % 32 == 0


def gather_batch(shard):
    if not pairwise(shard.shape[0]):
        return (shard,)
    return (shard,) + tuple(swap(shard, "batch", by) for by in range(1, lax.axis_size("batch")))


def gather_batch_steps(shard):
    if not pairwise(shard.shape[0]) or lax.axis_size("batch") != 4:
        shards = gather_batch(shard)
        return shards, shards[-1]
    far = swap(shard, "batch", 2)
    near = swap(jnp.concatenate([shard, far]), "batch", 1)
    rows = shard.shape[0]
    return (shard, near[:rows], far, near[rows:]), far


def gather_seq(shards):
    rows, columns = shards[0].shape
    if not pairwise(rows):
        whole = lax.all_gather(shards[0], ("batch", "seq"), axis=0, tiled=True)
        return tuple(whole.reshape(2, 1, -1, columns))
    stack = jnp.stack(shards)
    return stack, swap(stack, "seq", 1)


def scatter_seq(sent):
    return sent if sent.shape[0] == 1 else swap(sent, "seq", 1)


def join_seq(*parts):
    if parts[0][0].shape[0] == 1:
        whole = [jnp.concatenate([keep[0].astype(b16), sent[0]]) for keep, sent in parts]
        return None, jnp.concatenate(whole, axis=-1)
    total = jnp.concatenate([keep.astype(f32) + got.astype(f32) for keep, got in parts], axis=-1)
    return total[0], total[1:].astype(b16)


def scatter_batch(own, rest, more, *others):
    if own is None:
        total = lax.psum_scatter(rest, ("batch", "seq"), scatter_dimension=0, tiled=True).astype(f32)
        return total, None if more is None else lax.psum(more, "batch")
    count = own.shape[0]
    payloads = [rest[by] for by in range(rest.shape[0])]
    if more is not None:
        tail = jnp.pad(more, ((0, 0), (0, own.shape[1] - more.shape[1]))).astype(b16)
        payloads = [jnp.concatenate([payload, tail]) for payload in payloads]
    pieces = [swap(payload, "batch", by + 1) for by, payload in enumerate(payloads)]
    for piece in after(pieces, *others) if others else pieces:
        own = own + piece[:count].astype(f32)
        if more is not None:
            more = more + piece[count:, : more.shape[1]].astype(f32)
    return own, more


def scatter_far(keep, got, rows):
    far = (keep[rows : 2 * rows].astype(f32) + got[rows : 2 * rows].astype(f32)).astype(b16)
    here = keep[:rows].astype(f32) + got[:rows].astype(f32)
    return here, swap(far, "heads", 2)


def call(body, outs, *args, scratch=(), flops=0, limit=16, plain=False):
    in_specs = [pl.BlockSpec(memory_space=pl.ANY)] * len(args) if plain else [SMEM] + [VMEM] * (len(args) - 1)
    return pl.pallas_call(
        body,
        out_shape=[jax.ShapeDtypeStruct(*o) for o in outs],
        in_specs=in_specs,
        out_specs=[VMEM] * len(outs),
        scratch_shapes=list(scratch),
        compiler_params=pltpu.CompilerParams(vmem_limit_bytes=limit << 20),
        cost_estimate=pl.CostEstimate(flops=flops // 16, transcendentals=0, bytes_accessed=0),
    )(*args)


def dot(a, b, ca=1, cb=0):
    return lax.dot_general(a, b, (((ca,), (cb,)), ((), ())), preferred_element_type=f32)


def edges(scal):
    return [scal[3 + d] for d in range(DOCS)]


def doc_start(pos, bounds):
    start = bounds[0] + jnp.zeros_like(pos)
    for edge in bounds[1:]:
        start = jnp.where(pos >= edge, edge, start)
    return start


def lanes_like(shape):
    return lax.broadcasted_iota(jnp.int32, shape, 1)


def half_roll(block):
    return pltpu.roll(block, 64, 1)


def norm_rows(values):
    average = jnp.mean(values, axis=-1, keepdims=True)
    centered = values - average
    inverse = lax.rsqrt(jnp.mean(centered * centered, axis=-1, keepdims=True) + epsilon)
    return centered * inverse, inverse


def group_rows(stack, rel, rel_seq, scal):
    return some_rows(stack.shape[1], stack.shape[0] > 1, rel, rel_seq, scal)


def some_rows(count, paired, rel, rel_seq, scal):
    if not paired:
        return slice(rel_seq * count, rel_seq * count + count)
    return pl.ds(pl.multiple_of(((scal[1] ^ rel) * 2 + (scal[2] ^ rel_seq)) * count, 32), count)


def ds(start, size):
    return pl.ds(pl.multiple_of(start, size), size)


def shard_body(heads, *refs):
    sources, shard, (qkv, out_w, small, kernel), rows, sems = refs[:4], refs[4], refs[5:9], refs[9], refs[10]
    copies = [
        pltpu.make_async_copy(source, target, sems.at[index])
        for index, (source, target) in enumerate(zip(sources, (qkv, out_w, small, kernel)))
    ]
    for copy in copies:
        copy.start()
    for copy in copies:
        copy.wait()
    for part in range(3):
        shard[:, part * 128 : part * 128 + 128] = qkv[part, :, 0:128]
    thirds = [qkv[part, :, 128:192].astype(f32) for part in range(3)]
    turned = out_w[...].astype(f32).T
    shard[:, 384:512] = jnp.concatenate(thirds[:2], axis=1).astype(b16)
    shard[:, 512:640] = jnp.concatenate([thirds[2], turned[:, 0:64]], axis=1).astype(b16)
    shard[:, 640:768] = turned[:, 64:192].astype(b16)
    rows[...] = jnp.zeros_like(rows)
    count = kernel.shape[2]
    rows[0:4, 0 : small.shape[1]] = small[...].astype(f32)
    for part in range(3):
        rows[4 + part * heads : 4 + part * heads + heads, 0:count] = kernel[part].astype(f32)
    shard[:, 768:896] = rows[...].T[: shard.shape[0]].astype(b16)


def small_rows(scal, stacks, heads, norms, taps, columns, features):
    count = features.shape[0] // (2 * stacks[0].shape[0])
    for rel_seq, stack in enumerate(stacks):
        for rel in range(stack.shape[0]):
            block = stack[rel, :, 768:896].astype(f32)
            columns[group_rows(stack, rel, rel_seq, scal), :] = block
            group = (scal[1] ^ rel) * 2 + (scal[2] ^ rel_seq)
            features[pl.ds(pl.multiple_of(group * count, 8), count), :] = block[0:count]
    norms[...] = columns[...].T[0:8]
    taps[...] = jnp.zeros_like(taps)
    low = lanes_like((1, 128)) < 64
    for tap in range(KERNEL):
        turned = features[pl.ds(tap, HEAD_DIM, stride=KERNEL), :].T
        turned = jnp.concatenate([turned, jnp.zeros_like(turned)], axis=1)
        for part in range(3):
            one, two, three = (turned[4 + part * heads + i : 5 + part * heads + i] for i in range(3))
            taps[4 + tap : 5 + tap, part * PADW : part * PADW + 128] = jnp.where(low, one, half_roll(two))
            taps[4 + tap : 5 + tap, part * PADW + 128 : part * PADW + 256] = jnp.where(low, three, 0.0)


def norm_body(half, quarter, scal, *refs):
    pieces, hats, form = refs[:4], refs[4], refs[5]
    head = scal[0]
    for side in range(2):
        for rel in range(4):
            base = (head ^ rel) * quarter
            piece = pieces[2 * side + rel % 2]
            hat, _ = norm_rows(piece[rel // 2 * quarter : rel // 2 * quarter + quarter, :].astype(f32))
            if side == 0:
                hats[ds(half + base, quarter), :] = hat
                form[ds(base, quarter), :] = hat.astype(b16)
            else:
                hats[ds(base, quarter), :] = hat


def front_body(half, quarter, heads, paired, scal, *refs):
    hats, w_own, w_other, cot = refs[:4]
    refs = refs[1:]
    refs = refs[3:]
    if not paired:
        norms_in, taps_in, refs = refs[0], refs[1], refs[2:]
    normed, projected, wpad, query, key, value, extra, norms, taps = refs[:9]
    proj, columns, features, wo = refs[9:]
    if paired:
        small_rows(scal, (w_own, w_other), heads, norms, taps, columns, features)
    else:
        norms[...] = norms_in[...]
        taps[...] = taps_in[...]
    gain, bias = norms[0:1, :], norms[1:2, :]
    low = lanes_like((w_own.shape[1], 128)) < 64
    for rel_seq, stack in enumerate((w_own, w_other)):
        for rel in range(stack.shape[0]):
            rows = group_rows(stack, rel, rel_seq, scal)
            for part in range(3):
                wpad[rows, part * 256 : part * 256 + 128] = stack[rel, :, part * 128 : part * 128 + 128]
            shared = stack[rel, :, 384:512].astype(f32)
            wpad[rows, 128:256] = jnp.where(low, shared, 0.0).astype(b16)
            wpad[rows, 384:512] = jnp.where(low, half_roll(shared), 0.0).astype(b16)
            mid = stack[rel, :, 512:640].astype(f32)
            last = half_roll(stack[rel, :, 640:768].astype(f32))
            wpad[rows, 640:768] = jnp.where(low, mid, 0.0).astype(b16)
            wo[rows, 0:128] = jnp.where(low, half_roll(mid), last)
            wo[rows, 128:256] = last
    extra[0:quarter, :] = cot[...]
    width = heads * HEAD_DIM
    extra[quarter : quarter + width, :] = wo[...].T[0:width].astype(b16)
    proj[0:16, :] = jnp.zeros((16, proj.shape[1]), b16)

    def project(block, own):
        base = block * quarter
        rounded = (hats[ds(base, quarter), :] * gain + bias).astype(b16)
        proj[pl.ds(pl.multiple_of(base + 16, 16), quarter), :] = dot(rounded, wpad[...]).astype(b16)
        if own:
            rows = ds(base - half, quarter)
            normed[rows, :] = rounded

    @pl.loop(0, 4)
    def _(block):
        project(block, False)

    @pl.loop(4, 8)
    def _(block):
        project(block, True)

    projected[...] = proj[half : 2 * half + 16, :]
    bounds = edges(scal)

    def convolve(block, own):
        base = block * quarter
        pos = base + lax.broadcasted_iota(jnp.int32, (quarter, 1), 0)
        start = doc_start(pos, bounds)
        for part, out in enumerate((query, key, value)):
            if part == 0 and not own:
                continue
            cols = slice(part * PADW, part * PADW + PADW)
            rows = proj[pl.ds(pl.multiple_of(base, 16), quarter + 16), cols].astype(f32)
            mixed = taps[4:5, cols] * rows[16:]
            for back in range(1, KERNEL):
                earlier = pltpu.roll(rows, back, 0)[16:]
                mixed = mixed + jnp.where(pos - back >= start, taps[4 + back : 5 + back, cols] * earlier, 0.0)
            mixed = mixed.astype(b16)
            if part == 0:
                out[ds(base - half, quarter), :] = mixed * jnp.asarray(HEAD_DIM**-0.5, b16)
            else:
                out[ds(base, quarter), :] = mixed

    @pl.loop(0, 4)
    def _(block):
        convolve(block, False)

    @pl.loop(4, 8)
    def _(block):
        convolve(block, True)


def masked_queries(query, slots, heads):
    lane = lanes_like(query.shape) // HEAD_DIM
    for head in range(heads):
        slots[head] = jnp.where(lane == head, query[...], jnp.zeros((), b16))


def attention_body(half, heads, scal, query, key, value, packed, out_t, lse, vt, qm, peak, total):
    bounds = edges(scal)
    masked_queries(query, qm, heads)

    @pl.loop(0, 2 * half // 256)
    def _(block):
        turned = value[ds(block * 256, 256), :].astype(f32).T
        vt[:, ds(block * 256, 256)] = turned[: heads * HEAD_DIM].astype(b16)

    out_t[...] = jnp.zeros_like(out_t)
    peak[...] = jnp.full_like(peak, masked_score)
    total[...] = jnp.zeros_like(total)
    for block in range(half // QF):
        first = half + block * QF
        cols = slice(block * QF, block * QF + QF)
        pos = first + lanes_like((1, QF))
        start = doc_start(pos, bounds)
        low = doc_start(jnp.int32(first), bounds) // KB

        @pl.loop(low, (first + QF) // KB)
        def _(kb):
            keys = key[ds(kb * KB, KB), :]
            key_pos = kb * KB + lax.broadcasted_iota(jnp.int32, (KB, 1), 0)
            allowed = (key_pos >= start) & (key_pos <= pos)
            for head in range(heads):
                rows = slice(head * HEAD_DIM, head * HEAD_DIM + HEAD_DIM)
                one = slice(head, head + 1)
                scores = dot(keys, qm[head, cols, :], 1, 1)
                scores = jnp.where(allowed, scores, masked_score)
                old = peak[one, cols]
                new = jnp.maximum(old, jnp.max(scores, axis=0, keepdims=True))
                weights = jnp.exp(scores - new)
                shrink = jnp.exp(old - new)
                peak[one, cols] = new
                total[one, cols] = shrink * total[one, cols] + jnp.sum(weights, axis=0, keepdims=True)
                out_t[rows, cols] = shrink * out_t[rows, cols] + dot(
                    vt[rows, ds(kb * KB, KB)], weights.astype(b16)
                )

    for head in range(heads):
        rows = slice(head * HEAD_DIM, head * HEAD_DIM + HEAD_DIM)
        out_t[rows, :] = out_t[rows, :] / total[head : head + 1, :]
    lse[...] = peak[...] + jnp.log(jnp.maximum(total[...], 1e-30))
    for block in range(half // 256):
        cols = slice(block * 256, block * 256 + 256)
        packed[cols, :] = out_t[0:128, cols].T.astype(b16)
    for block in range(half // 512):
        cols = slice(block * 256, block * 256 + 256)
        later = slice(half // 2 + block * 256, half // 2 + block * 256 + 256)
        both = jnp.concatenate([out_t[128:192, cols], out_t[128:192, later]], axis=0)
        packed[half + block * 256 : half + block * 256 + 256, :] = both.T.astype(b16)


def back_blocks(half, heads, scal, first_kb, last_kb, refs, finish):
    key, value, qm, dom, lse, row_dot, kt, query_t, key_sum, value_sum = refs
    bounds = edges(scal)

    @pl.loop(first_kb, last_kb)
    def _(kb):
        key_sum[...] = jnp.zeros_like(key_sum)
        value_sum[...] = jnp.zeros_like(value_sum)
        for block in range(half // QB):
            first = half + block * QB
            cols = slice(block * QB, block * QB + QB)
            low = doc_start(jnp.int32(first), bounds)

            @pl.when((kb * KB + KB > low) & (kb * KB < first + QB))
            def _():
                pos = first + lanes_like((1, QB))
                start = doc_start(pos, bounds)
                keys = key[ds(kb * KB, KB), :]
                values = value[ds(kb * KB, KB), :]
                key_pos = kb * KB + lax.broadcasted_iota(jnp.int32, (KB, 1), 0)
                allowed = (key_pos >= start) & (key_pos <= pos)
                for head in range(heads):
                    rows = slice(head * HEAD_DIM, head * HEAD_DIM + HEAD_DIM)
                    one = slice(head, head + 1)
                    own_q = qm[head, cols, :]
                    own_g = dom[head, cols, :]
                    scores = jnp.where(allowed, dot(keys, own_q, 1, 1) - lse[one, cols], masked_score)
                    weights = jnp.exp(scores)
                    grads = weights * (dot(values, own_g, 1, 1) - row_dot[one, cols])
                    grads = grads.astype(b16)
                    value_sum[...] += dot(weights.astype(b16), own_g)
                    key_sum[...] += dot(grads, own_q)
                    query_t[rows, cols] += dot(kt[rows, ds(kb * KB, KB)], grads)

        finish(kb, key_sum[...], value_sum[...])


def spread_groups(source, scal, keep, sent, cols=slice(None)):
    for rel_seq, out in enumerate((keep, sent)):
        for rel in range(out.shape[0]):
            out[rel, :, cols] = source[group_rows(out, rel, rel_seq, scal), :].astype(out.dtype)


def branch_body(quarter, heads, scal, *refs):
    branches = refs[:4]
    extra, out_t, dout, row_dot, keep, sent, proj_grad, turned = refs[4:]
    head = scal[0]
    width = heads * HEAD_DIM
    weights = jnp.concatenate([extra[quarter:, :], jnp.zeros((PADW - width, extra.shape[1]), b16)], axis=0)
    proj_grad[...] = jnp.zeros_like(proj_grad)
    row_dot[...] = jnp.zeros_like(row_dot)
    for rel, branch in enumerate(branches):
        base = (head ^ rel) * quarter
        grad = dot(branch[...], weights, 1, 1).astype(b16)
        dout[ds(base, quarter), :] = grad
        attended = out_t[:, ds(base, quarter)]
        product = grad.astype(f32).T[:width] * attended
        for one in range(heads):
            row_dot[one : one + 1, ds(base, quarter)] = jnp.sum(
                product[one * HEAD_DIM : one * HEAD_DIM + HEAD_DIM], axis=0, keepdims=True
            )
        proj_grad[...] += dot(attended.astype(b16), branch[...])
    turned[...] = proj_grad[...].T
    spread_groups(turned, scal, keep, sent)


def remote_back_body(half, heads, scal, *refs):
    query, key, value, dout, lse, row_dot = refs[:6]
    remote, query_t, kt = refs[6:9]
    qm, dom, key_sum, value_sum = refs[9:]
    width = heads * HEAD_DIM
    masked_queries(query, qm, heads)
    masked_queries(dout, dom, heads)

    @pl.loop(0, 2 * half // 256)
    def _(block):
        kt[:, ds(block * 256, 256)] = key[ds(block * 256, 256), :].astype(f32).T[:width].astype(b16)

    query_t[...] = jnp.zeros_like(query_t)

    def finish(kb, dk, dv):
        rows = ds(kb * KB, KB)
        remote[rows, 0:128] = dk[:, 0:128].astype(b16)
        remote[rows, 128:256] = dv[:, 0:128].astype(b16)
        remote[rows, 256:384] = (dk[:, 128:256] + half_roll(dv[:, 128:256])).astype(b16)

    back_blocks(
        half, heads, scal, 0, half // KB,
        (key, value, qm, dom, lse, row_dot, kt, query_t, key_sum, value_sum), finish,
    )


def local_back_body(half, heads, scal, *refs):
    query, key, value, dout, lse, row_dot, kt, query_in, taps = refs[:9]
    dq, dk_out, dv_out, front = refs[9:13]
    qm, dom, key_sum, value_sum, query_t = refs[13:]
    masked_queries(query, qm, heads)
    masked_queries(dout, dom, heads)
    query_t[...] = query_in[...]

    def finish(kb, dk, dv):
        rows = ds(kb * KB - half, KB)
        dk_out[rows, :] = dk.astype(b16)
        dv_out[rows, :] = dv.astype(b16)

    back_blocks(
        half, heads, scal, half // KB, 2 * half // KB,
        (key, value, qm, dom, lse, row_dot, kt, query_t, key_sum, value_sum), finish,
    )
    width = heads * HEAD_DIM
    scale = HEAD_DIM**-0.5
    for block in range(half // 256):
        cols = slice(block * 256, block * 256 + 256)
        turned = (query_t[:, cols] * scale).T
        dq[cols, 0:128] = turned[:, 0:128].astype(b16)
        dq[cols, 128:256] = jnp.concatenate(
            [turned[:, 128:width], jnp.zeros((256, PADW - width), f32)], axis=1
        ).astype(b16)
    bounds = edges(scal)
    pos = half + lax.broadcasted_iota(jnp.int32, (8, 1), 0)
    start = doc_start(pos, bounds)
    for part, grads in enumerate((dq, dk_out, dv_out)):
        cols = slice(part * PADW, part * PADW + PADW)
        rounded = grads[0:16, :].astype(b16).astype(f32)[0:8]
        result = jnp.zeros((8, PADW), f32)
        for back in range(1, KERNEL):
            moved = pltpu.roll(jnp.where(pos - back >= start, taps[4 + back : 5 + back, cols] * rounded, 0.0), 8 - back, 0)
            place = lax.broadcasted_iota(jnp.int32, (8, 1), 0)
            result = result + jnp.where(place >= 8 - back, moved, 0.0)
        front[:, cols] = result


def weights_body(scal, *refs):
    own, other, inner, outer = refs
    width = inner.shape[1]
    for rel_seq, stack in enumerate((own, other)):
        for rel in range(stack.shape[0]):
            rows = group_rows(stack, rel, rel_seq, scal)
            inner[rows, :] = stack[rel, :, :width]
            outer[rows, :] = stack[rel, :, width:]


def feed_body(half, quarter, scal, *refs):
    attended, extras, inputs = refs[0:4], refs[4:8], refs[8:10]
    inner, outer, norms = refs[10:13]
    normed, squared, inner_grad, keep, sent, middle_own = refs[13:]
    head = scal[0]
    for rel in range(4):
        base = (head ^ rel) * quarter
        late = base >= half // 2
        middle = inputs[rel % 2][rel // 2 * quarter : rel // 2 * quarter + quarter, :].astype(f32)
        for part in range(4):
            left = attended[part][ds(base, quarter), :]
            right = attended[part][ds(half + lax.rem(base, half // 2), quarter), :].astype(f32)
            right = jnp.where(late, half_roll(right), right).astype(b16)
            both = jnp.concatenate([left, right], axis=1)
            weights = extras[part][quarter:, :]
            middle = middle + dot(both[:, : weights.shape[0]], weights)
        if rel == 0:
            middle_own[...] = middle
        hat, _ = norm_rows(middle)
        rounded = (hat * norms[2:3, :] + norms[3:4, :]).astype(b16)
        rows = slice(rel * quarter, rel * quarter + quarter)
        normed[rows, :] = rounded
        positive = jnp.maximum(dot(rounded, inner[...]), 0.0)
        squared[rows, :] = (positive * positive).astype(b16)
        grads = (dot(extras[rel][0:quarter, :], outer[...]) * 2.0 * positive).astype(b16)
        inner_grad[rows, :] = grads
        part = dot(grads, inner[...], 1, 1)
        place = slice((rel // 2) * quarter, (rel // 2) * quarter + quarter)
        if rel % 2 == 0:
            keep[place, :] = part
        else:
            sent[place, :] = part.astype(b16)


def outer_grads_body(quarter, scal, *refs):
    extras, squared, total, cot = refs[0:4], refs[4], refs[5], refs[6]
    for rel in range(4):
        cot[rel * quarter : rel * quarter + quarter, :] = extras[rel][0:quarter, :]
    for tile in range(total.shape[0] // 256):
        cols = slice(tile * 256, tile * 256 + 256)
        total[cols, :] = dot(cot[:, cols], squared[...], 0, 0)


def feed_grads_body(quarter, scal, *refs):
    normed, squared, inner_grad, outer, outer_total = refs[:5]
    keep, sent, kept, away, total = refs[5:]
    width = total.shape[1]
    for rel in range(4):
        rows = slice(rel * quarter, rel * quarter + quarter)
        part = dot(squared[rows, :], outer[...], 1, 1)
        place = slice((rel // 2) * quarter, (rel // 2) * quarter + quarter)
        if rel % 2 == 0:
            keep[place, :] = part
        else:
            sent[place, :] = part.astype(b16)
    for tile in range(total.shape[0] // 256):
        cols = slice(tile * 256, tile * 256 + 256)
        total[cols, :] = dot(normed[:, cols], inner_grad[...], 0, 0)
    spread_groups(total, scal, kept, away, slice(0, width))
    spread_groups(outer_total, scal, kept, away, slice(width, 2 * width))


def norm_back_body(row, scal, part, got, values, skip, norms, grad_in, rounded, sums):
    del scal
    grad = part[...] + got[0 : part.shape[0], :].astype(f32)
    hat, inverse = norm_rows(values[...].astype(f32))
    scaled = grad * norms[row : row + 1, :]
    back = inverse * (
        scaled
        - jnp.mean(scaled, axis=-1, keepdims=True)
        - hat * jnp.mean(scaled * hat, axis=-1, keepdims=True)
    )
    result = skip[...].astype(f32) + back
    grad_in[...] = result
    rounded[...] = result.astype(b16)
    sums[...] = jnp.zeros_like(sums)
    sums[0:1, :] = jnp.sum(grad * hat, axis=0, keepdims=True)
    sums[1:2, :] = jnp.sum(grad, axis=0, keepdims=True)


def tail_body(half, quarter, scal, *refs):
    dq, dk, dv, remote, front, projected, normed, taps = refs[:8]
    proj_grad, w_keep, w_send, sums = refs[8:12]
    mixed, total, dense = refs[12:]
    bounds = edges(scal)
    low = lanes_like((quarter, 128)) < 64
    sums[...] = jnp.zeros_like(sums)
    for block in range(half // quarter):
        rows = slice(block * quarter, block * quarter + quarter)
        shared = remote[rows, 256:384].astype(f32)
        mixed[rows, 0:256] = dq[rows, :]
        mixed[rows, 256:384] = (dk[rows, 0:128].astype(f32) + remote[rows, 0:128].astype(f32)).astype(b16)
        mixed[rows, 384:512] = (dk[rows, 128:256].astype(f32) + jnp.where(low, shared, 0.0)).astype(b16)
        mixed[rows, 512:640] = (dv[rows, 0:128].astype(f32) + remote[rows, 128:256].astype(f32)).astype(b16)
        mixed[rows, 640:768] = (dv[rows, 128:256].astype(f32) + jnp.where(low, half_roll(shared), 0.0)).astype(b16)
    mixed[half : half + 16, :] = jnp.zeros((16, mixed.shape[1]), b16)

    @pl.loop(0, half // quarter)
    def _(block):
        base = block * quarter
        pos = half + base + lax.broadcasted_iota(jnp.int32, (quarter + 16, 1), 0)
        start = doc_start(pos, bounds)
        for part in range(3):
            cols = slice(part * PADW, part * PADW + PADW)
            grads = mixed[pl.ds(pl.multiple_of(base, 16), quarter + 16), cols].astype(f32)
            values = projected[pl.ds(pl.multiple_of(base, 16), quarter + 16), cols].astype(f32)
            here = grads[:quarter]
            result = taps[4:5, cols] * here
            sums[4:5, cols] += jnp.sum(here * values[16:], axis=0, keepdims=True)
            for back in range(1, KERNEL):
                same = pos - back >= start
                held = jnp.where(same, grads, 0.0)
                ahead = pltpu.roll(held, quarter + 16 - back, 0)[:quarter]
                result = result + taps[4 + back : 5 + back, cols] * ahead
                earlier = pltpu.roll(values, back, 0)[16:]
                sums[4 + back : 5 + back, cols] += jnp.sum(held[:quarter] * earlier, axis=0, keepdims=True)
            proj_grad[ds(base, quarter), cols] = result.astype(b16)

        @pl.when(block == half // quarter - 1)
        def _():
            added = jnp.concatenate([jnp.zeros((8, front.shape[1]), f32), front[...]], axis=0)
            tail_pos = 2 * half - 16 + lax.broadcasted_iota(jnp.int32, (32, 1), 0)
            tail_start = doc_start(tail_pos, bounds)
            grads = mixed[half - 16 : half + 16, :].astype(f32)
            result = taps[4:5, :] * grads[:16]
            for back in range(1, KERNEL):
                held = jnp.where(tail_pos - back >= tail_start, grads, 0.0)
                result = result + taps[4 + back : 5 + back, :] * pltpu.roll(held, 32 - back, 0)[:16]
            proj_grad[half - 16 : half, :] = (result + added).astype(b16)

    for tile in range(total.shape[0] // 256):
        rows = slice(tile * 256, tile * 256 + 256)
        total[rows, :] = dot(normed[:, rows], proj_grad[...], 0, 0)
        for part in range(3):
            dense[rows, part * 128 : part * 128 + 128] = total[rows, part * 256 : part * 256 + 128]
        dense[rows, 384:512] = total[rows, 128:256] + half_roll(total[rows, 384:512])
        dense[rows, 512:640] = total[rows, 640:768]
    spread_groups(dense, scal, w_keep, w_send)


def tail_norm_body(quarter, scal, proj_grad, wpad, form, second, keep, sent, sums):
    head = scal[0]
    sums[...] = jnp.zeros_like(sums)
    sums[2:4, :] = second[0:2, :]
    for rel in (1, 3, 0, 2):
        base = (head ^ rel) * quarter
        part = dot(proj_grad[ds(base, quarter), :], wpad[...], 1, 1)
        sums[0:1, :] += jnp.sum(part * form[ds(base, quarter), :].astype(f32), axis=0, keepdims=True)
        sums[1:2, :] += jnp.sum(part, axis=0, keepdims=True)
        place = slice((rel // 2) * quarter, (rel // 2) * quarter + quarter)
        if rel % 2 == 0:
            keep[place, :] = part
        else:
            sent[place, :] = part.astype(b16)
    keep[2 * quarter :, :] = sums[...]
    sent[2 * quarter :, :] = sums[...].astype(b16)


def pad_heads(values, width):
    shaped = values.reshape(values.shape[:-1] + (3, width))
    padded = jnp.pad(shaped, [(0, 0)] * (shaped.ndim - 1) + [(0, PADW - width)])
    return padded.reshape(values.shape[:-1] + (3 * PADW,))


def gather_small(norms, conv_kernel, model, width):
    norms = lax.all_gather(norms, ("batch", "seq"), axis=0, tiled=True).astype(f32).T
    taps = lax.all_gather(conv_kernel, ("batch", "seq"), axis=2, tiled=True).astype(f32)
    taps = taps.reshape(3, width, KERNEL).transpose(2, 0, 1).reshape(KERNEL, 3 * width)
    return jnp.pad(norms, ((0, 4), (0, 0))), jnp.pad(pad_heads(taps, width), ((4, 1), (0, 0)))


def on_device(
    block_input, segment_ids, norm1_gain, norm1_bias, qkv_weight, conv_kernel, out_weight,
    norm2_gain, norm2_bias, inner_weight, outer_weight, cotangent,
):
    quarter = block_input.shape[2]
    half = quarter * lax.axis_size("heads")
    width = qkv_weight.shape[2]
    heads = width // HEAD_DIM
    group = qkv_weight.shape[0]
    groups = lax.axis_size("batch") * lax.axis_size("seq")
    model = group * groups
    hidden = inner_weight.shape[1]
    head, batch, seq = lax.axis_index("heads"), lax.axis_index("batch"), lax.axis_index("seq")
    own = batch * 2 + seq
    stacks = (groups // 2, group) if pairwise(group) else (1, model // 2)

    ids = segment_ids.reshape(-1)
    docs = jnp.arange(DOCS, dtype=jnp.int32)
    firsts = jnp.sum((ids[None, :] < docs[:, None]).astype(jnp.int32), axis=1) - (seq - 1) * half
    scal = jnp.concatenate([jnp.stack([head, batch, seq]), firsts, jnp.zeros((1,), jnp.int32)]).astype(jnp.int32)

    x_own = block_input.reshape(quarter, model)
    cot_own = cotangent.reshape(quarter, model)

    share = conv_kernel.shape[2]

    paired = pairwise(group)
    qkv = qkv_weight
    small = [norm1_gain, norm1_bias, norm2_gain, norm2_bias]
    small_args = []
    if paired:
        (shard,) = call(
            functools.partial(shard_body, heads), [((group, 896), b16)],
            qkv.transpose(1, 0, 2), out_weight, jnp.stack(small), conv_kernel,
            scratch=[
                pltpu.VMEM((3, group, width), b16), pltpu.VMEM(out_weight.shape, b16), pltpu.VMEM((4, group), b16),
                pltpu.VMEM(conv_kernel.shape, b16), pltpu.VMEM((128, 128), f32), pltpu.SemaphoreType.DMA((4,)),
            ],
            limit=4, plain=True,
        )
    else:
        small_args = gather_small(jnp.stack(small, axis=1), conv_kernel, model, width)
        shard = jnp.concatenate(
            [qkv[:, 0, :128], qkv[:, 1, :128], qkv[:, 2, :128], qkv[:, 0, 128:], qkv[:, 1, 128:], qkv[:, 2, 128:],
             out_weight.T, jnp.zeros((group, 128), b16)], axis=1,
        )
    shards, first_shard = gather_batch_steps(shard)
    far_seq = [(2 * h + t, 2 * (h ^ 2) + (t ^ 1)) for h in range(lax.axis_size("heads")) for t in range(2)]
    x_other, x_far, x_far_other = after(
        (swap(x_own, "seq", 1), swap(x_own, "heads", 2), lax.ppermute(x_own, ("heads", "seq"), far_seq)), first_shard
    )
    x_pieces = gather_cores(x_own, x_far)
    y_pieces = gather_cores(x_other, x_far_other)
    hats, form_one = call(
        functools.partial(norm_body, half, quarter),
        [((2 * half, model), f32), ((half, model), b16)],
        scal, *x_pieces, *y_pieces, flops=2 * half * model, limit=6,
    )
    w_own, w_other = gather_seq(shards)
    w_other = after(w_other, hats)

    feed_shards = gather_batch(after(jnp.concatenate([inner_weight, outer_weight.T], axis=1), shards))

    normed_one, projected, wpad, query, key, value, extra, norms, taps = call(
        functools.partial(front_body, half, quarter, heads, paired),
        [
            ((half, model), b16), ((half + 16, 3 * PADW), b16), ((model, 3 * PADW), b16),
            ((half, PADW), b16), ((2 * half, PADW), b16), ((2 * half, PADW), b16), ((quarter + width, model), b16),
            ((8, model), f32), ((8, 3 * PADW), f32),
        ],
        scal, hats, w_own, w_other, cot_own, *small_args,
        scratch=[
            pltpu.VMEM((2 * half + 16, 3 * PADW), b16),
            pltpu.VMEM((model, 128), f32), pltpu.VMEM((KERNEL * HEAD_DIM, 128), f32), pltpu.VMEM((model, PADW), f32),
        ],
        flops=4 * half * model * 3 * width, limit=12,
    )

    feed_own, feed_other = gather_seq(after(feed_shards, query))
    extra_pieces = gather_heads(extra)

    packed, out_t, lse = call(
        functools.partial(attention_body, half, heads),
        [((half + half // 2, 128), b16), ((width, half), f32), ((8, half), f32)],
        scal, query, key, value,
        scratch=[
            pltpu.VMEM((width, 2 * half), b16), pltpu.VMEM((heads, half, PADW), b16),
            pltpu.VMEM((8, half), f32), pltpu.VMEM((8, half), f32),
        ],
        flops=4 * half * half * width, limit=7,
    )
    packed_pieces = gather_heads(packed)
    feed_own, feed_other, _ = lax.optimization_barrier((feed_own, feed_other, packed))
    inner_full, outer_full = call(
        weights_body, [((model, hidden), b16), ((model, hidden), b16)], scal, feed_own, feed_other, limit=4,
    )

    normed_two, squared, inner_grad, keep, sent, middle_own = call(
        functools.partial(feed_body, half, quarter),
        [((half, model), b16), ((half, hidden), b16), ((half, hidden), b16),
         ((2 * quarter, model), f32), ((2 * quarter, model), b16), ((quarter, model), f32)],
        scal, *packed_pieces, *extra_pieces, *x_pieces, inner_full, outer_full, norms,
        flops=2 * half * model * (model + 3 * hidden), limit=12,
    )
    got = swap(sent, "heads", 1)
    (outer_total,) = call(
        functools.partial(outer_grads_body, quarter), [((model, hidden), f32)],
        scal, *extra_pieces, squared,
        scratch=[pltpu.VMEM((half, model), b16)], flops=2 * half * model * hidden, limit=8,
    )
    got = after(got, outer_total)
    dn_here, dn_far = scatter_far(keep, got, quarter)
    out_keep, out_sent, ff_keep, ff_send = call(
        functools.partial(feed_grads_body, quarter),
        [((2 * quarter, model), f32), ((2 * quarter, model), b16),
         (stacks + (2 * hidden,), b16), (stacks + (2 * hidden,), b16)],
        scal, after(normed_two, got), squared, inner_grad, outer_full, outer_total,
        scratch=[pltpu.VMEM((model, hidden), f32)],
        flops=4 * half * model * hidden, limit=8,
    )
    dn_far = after(dn_far, out_sent)
    ff_got = scatter_seq(ff_send)
    middle_grad, branch, sums_two = call(
        functools.partial(norm_back_body, 2),
        [((quarter, model), f32), ((quarter, model), b16), ((8, model), f32)],
        scal, dn_here, dn_far, middle_own, cot_own, norms, limit=6,
    )
    branch_pieces = gather_heads(branch)
    out_got = swap(after(out_sent, branch), "heads", 1)

    dout, row_dot, pj_keep, pj_send = call(
        functools.partial(branch_body, quarter, heads),
        [((half, PADW), b16), ((8, half), f32), (stacks + (width,), f32), (stacks + (width,), b16)],
        scal, *branch_pieces, extra, out_t,
        scratch=[pltpu.VMEM((width, model), f32), pltpu.VMEM((model, width), f32)],
        flops=4 * half * model * width, limit=6,
    )
    out_here, out_far = scatter_far(out_keep, after(out_got, dout), quarter)
    remote, query_t, kt = call(
        functools.partial(remote_back_body, half, heads),
        [((half, 384), b16), ((width, half), f32), ((width, 2 * half), b16)],
        scal, query, key, value, dout, lse, row_dot,
        scratch=[
            pltpu.VMEM((heads, half, PADW), b16), pltpu.VMEM((heads, half, PADW), b16),
            pltpu.VMEM((KB, PADW), f32), pltpu.VMEM((KB, PADW), f32),
        ],
        flops=10 * half * half * width, limit=8,
    )
    remote_in = lax.ppermute(remote, "seq", [(1, 0)])
    ff_own, ff_rest = join_seq((ff_keep, after(ff_got, remote)))

    dq, dk, dv, front = call(
        functools.partial(local_back_body, half, heads),
        [((half, PADW), b16), ((half, PADW), b16), ((half, PADW), b16), ((8, 3 * PADW), f32)],
        scal, query, key, value, dout, lse, row_dot, kt, after(query_t, ff_rest), taps,
        scratch=[
            pltpu.VMEM((heads, half, PADW), b16), pltpu.VMEM((heads, half, PADW), b16),
            pltpu.VMEM((KB, PADW), f32), pltpu.VMEM((KB, PADW), f32), pltpu.VMEM((width, half), f32),
        ],
        flops=10 * half * half * width, limit=8,
    )
    front_in = lax.ppermute(front, "seq", [(1, 0)])
    pj_got = scatter_seq(after(pj_send, ff_rest))
    remote_in = after(remote_in, dq)
    front_in = after(front_in, pj_got)
    block_output = (middle_own + out_here + after(out_far, dq).astype(f32)).astype(b16)

    proj_grad, w_keep, w_send, sums_taps = call(
        functools.partial(tail_body, half, quarter),
        [((half, 3 * PADW), b16), (stacks + (640,), f32), (stacks + (640,), b16), ((8, 3 * PADW), f32)],
        scal, dq, dk, dv, remote_in, front_in, projected, normed_one, taps,
        scratch=[
            pltpu.VMEM((half + 16, 3 * PADW), b16), pltpu.VMEM((model, 3 * PADW), f32), pltpu.VMEM((model, 640), f32),
        ],
        flops=2 * half * model * 3 * width, limit=12,
    )
    w_got = scatter_seq(w_send)
    keep, sent, sums = call(
        functools.partial(tail_norm_body, quarter),
        [((2 * quarter + 8, model), f32), ((2 * quarter + 8, model), b16), ((8, model), f32)],
        scal, proj_grad, wpad, form_one, sums_two,
        flops=2 * half * model * 3 * width, limit=8,
    )
    got = swap(sent, "heads", 1)
    dn_here, dn_far = scatter_far(keep, got, quarter)
    small = sums + got[2 * quarter :].astype(f32)
    small = jnp.concatenate([small[0:4], sums_taps[4:8]])
    small = small + swap(small, "seq", 1)
    ff_out, _ = scatter_batch(ff_own, ff_rest, None, small)
    cut = small.shape[1] // 2
    small = jnp.concatenate([small[:, :cut], small[:, cut:]])
    qkv_own, qkv_rest = join_seq((w_keep, w_got), (pj_keep, pj_got))
    qkv_out, small = scatter_batch(qkv_own, qkv_rest, small)
    pj_out = qkv_out[:, 640:]
    small = jnp.concatenate([small[:8], small[8:]], axis=1)
    input_grad, _, _ = call(
        functools.partial(norm_back_body, 0),
        [((quarter, model), f32), ((quarter, model), b16), ((8, model), f32)],
        scal, dn_here, dn_far, x_own, middle_grad, norms, limit=6,
    )
    qkv_out = jnp.stack(
        [
            jnp.concatenate([qkv_out[:, 0:128], qkv_out[:, 384:448]], axis=1),
            jnp.concatenate([qkv_out[:, 128:256], qkv_out[:, 448:512]], axis=1),
            jnp.concatenate([qkv_out[:, 256:384], qkv_out[:, 512:576]], axis=1),
        ],
        axis=1,
    )
    gains = lax.dynamic_slice_in_dim(small[0:4], own * group, group, 1)
    gains = gains + swap(gains, "heads", 2)
    kernel_out = small[4 : 4 + KERNEL].reshape(KERNEL, 3, PADW)[:, :, :width].reshape(KERNEL, 3, heads, HEAD_DIM)
    kernel_out = kernel_out.transpose(1, 2, 3, 0).reshape(3, heads, HEAD_DIM * KERNEL)
    kernel_out = lax.dynamic_slice_in_dim(kernel_out, own * share, share, 2)
    return (
        block_output.reshape(block_input.shape),
        input_grad.reshape(block_input.shape),
        gains[0],
        gains[1],
        qkv_out,
        kernel_out,
        pj_out.T,
        gains[2],
        gains[3],
        ff_out[:, :hidden],
        ff_out[:, hidden : 2 * hidden].T,
    )


def solution(mesh):
    return jax.shard_map(
        on_device,
        mesh=mesh,
        in_specs=(
            P("batch", "seq", "heads", None),
            P("batch", None),
            P(("batch", "seq")),
            P(("batch", "seq")),
            P(("batch", "seq"), None, "heads"),
            P(None, "heads", ("batch", "seq")),
            P("heads", ("batch", "seq")),
            P(("batch", "seq")),
            P(("batch", "seq")),
            P(("batch", "seq"), "heads"),
            P("heads", ("batch", "seq")),
            P("batch", "seq", "heads", None),
        ),
        out_specs=(
            P("batch", "seq", "heads", None),
            P("batch", "seq", "heads", None),
            P(("batch", "seq")),
            P(("batch", "seq")),
            P(("batch", "seq"), None, "heads"),
            P(None, "heads", ("batch", "seq")),
            P("heads", ("batch", "seq")),
            P(("batch", "seq")),
            P(("batch", "seq")),
            P(("batch", "seq"), "heads"),
            P("heads", ("batch", "seq")),
        ),
        check_vma=False,
    )
```

```python
import functools

import jax
import jax.numpy as jnp
from jax import lax
from jax.experimental import pallas as pl
from jax.experimental.pallas import tpu as pltpu
from jax.sharding import PartitionSpec as P

HEAD_DIM = 64
KERNEL = 3
DOCS = 4
PADW = 256
QB = 512
QF = 256
KB = 256

epsilon = 1e-05
masked_score = -1e30
f32 = jnp.float32
b16 = jnp.bfloat16

VMEM = pl.BlockSpec(memory_space=pltpu.VMEM)
SMEM = pl.BlockSpec(memory_space=pltpu.SMEM)
HBM = pl.BlockSpec(memory_space=pl.ANY)


def after(value, *others):
    return lax.optimization_barrier((value,) + others)[0]


def swap(shard, axis, by):
    return lax.ppermute(shard, axis, [(i, i ^ by) for i in range(lax.axis_size(axis))])


def gather_heads(shard):
    far = swap(shard, "heads", 2)
    near = swap(shard, "heads", 1)
    return [shard, near, far, swap(far, "heads", 1)]


def gather_cores(shard, far):
    both = jnp.concatenate([shard, far])
    return [both, swap(both, "heads", 1)]


def pairwise(group):
    return group % 32 == 0


def gather_batch(shard):
    if not pairwise(shard.shape[0]):
        return (shard,)
    return (shard,) + tuple(swap(shard, "batch", by) for by in range(1, lax.axis_size("batch")))


def gather_batch_steps(shard):
    if not pairwise(shard.shape[0]) or lax.axis_size("batch") != 4:
        shards = gather_batch(shard)
        return shards, shards[-1]
    far = swap(shard, "batch", 2)
    near = swap(jnp.concatenate([shard, far]), "batch", 1)
    rows = shard.shape[0]
    return (shard, near[:rows], far, near[rows:]), far


def gather_seq(shards):
    rows, columns = shards[0].shape
    if not pairwise(rows):
        whole = lax.all_gather(shards[0], ("batch", "seq"), axis=0, tiled=True)
        return tuple(whole.reshape(2, 1, -1, columns))
    stack = jnp.stack(shards)
    return stack, swap(stack, "seq", 1)


def scatter_seq(sent):
    return sent if sent.shape[0] == 1 else swap(sent, "seq", 1)


def join_seq(*parts):
    if parts[0][0].shape[0] == 1:
        whole = [jnp.concatenate([keep[0].astype(b16), sent[0]]) for keep, sent in parts]
        return None, jnp.concatenate(whole, axis=-1)
    total = jnp.concatenate([keep.astype(f32) + got.astype(f32) for keep, got in parts], axis=-1)
    return total[0], total[1:].astype(b16)


def scatter_batch(own, rest, more, *others):
    if own is None:
        total = lax.psum_scatter(rest, ("batch", "seq"), scatter_dimension=0, tiled=True).astype(f32)
        return total, None if more is None else lax.psum(more, "batch")
    count = own.shape[0]
    payloads = [rest[by] for by in range(rest.shape[0])]
    if more is not None:
        tail = jnp.pad(more, ((0, 0), (0, own.shape[1] - more.shape[1]))).astype(b16)
        payloads = [jnp.concatenate([payload, tail]) for payload in payloads]
    pieces = [swap(payload, "batch", by + 1) for by, payload in enumerate(payloads)]
    for piece in after(pieces, *others) if others else pieces:
        own = own + piece[:count].astype(f32)
        if more is not None:
            more = more + piece[count:, : more.shape[1]].astype(f32)
    return own, more


def scatter_far(keep, got, rows):
    far = (keep[rows : 2 * rows].astype(f32) + got[rows : 2 * rows].astype(f32)).astype(b16)
    here = keep[:rows].astype(f32) + got[:rows].astype(f32)
    return here, swap(far, "heads", 2)


def call(body, outs, *args, scratch=(), flops=0, limit=16, plain=False, away=()):
    in_specs = [HBM] * len(args) if plain else [SMEM] + [VMEM] * (len(args) - 1)
    return pl.pallas_call(
        body,
        out_shape=[jax.ShapeDtypeStruct(*o) for o in outs],
        in_specs=in_specs,
        out_specs=[HBM if index in away else VMEM for index in range(len(outs))],
        scratch_shapes=list(scratch),
        compiler_params=pltpu.CompilerParams(vmem_limit_bytes=limit << 20),
        cost_estimate=pl.CostEstimate(flops=flops // 16, transcendentals=0, bytes_accessed=0),
    )(*args)


def dot(a, b, ca=1, cb=0):
    return lax.dot_general(a, b, (((ca,), (cb,)), ((), ())), preferred_element_type=f32)


def edges(scal):
    return [scal[3 + d] for d in range(DOCS)]


def doc_start(pos, bounds):
    start = bounds[0] + jnp.zeros_like(pos)
    for edge in bounds[1:]:
        start = jnp.where(pos >= edge, edge, start)
    return start


def lanes_like(shape):
    return lax.broadcasted_iota(jnp.int32, shape, 1)


def half_roll(block):
    return pltpu.roll(block, 64, 1)


def norm_rows(values):
    average = jnp.mean(values, axis=-1, keepdims=True)
    centered = values - average
    inverse = lax.rsqrt(jnp.mean(centered * centered, axis=-1, keepdims=True) + epsilon)
    return centered * inverse, inverse


def group_rows(stack, rel, rel_seq, scal):
    return some_rows(stack.shape[1], stack.shape[0] > 1, rel, rel_seq, scal)


def some_rows(count, paired, rel, rel_seq, scal):
    if not paired:
        return slice(rel_seq * count, rel_seq * count + count)
    return pl.ds(pl.multiple_of(((scal[1] ^ rel) * 2 + (scal[2] ^ rel_seq)) * count, 32), count)


def ds(start, size):
    return pl.ds(pl.multiple_of(start, size), size)


def shard_body(heads, *refs):
    sources, shard, (qkv, out_w, small, kernel), rows, sems = refs[:4], refs[4], refs[5:9], refs[9], refs[10]
    copies = [
        pltpu.make_async_copy(source, target, sems.at[index])
        for index, (source, target) in enumerate(zip(sources, (qkv, out_w, small, kernel)))
    ]
    for copy in copies:
        copy.start()
    for copy in copies:
        copy.wait()
    for part in range(3):
        shard[:, part * 128 : part * 128 + 128] = qkv[part, :, 0:128]
    thirds = [qkv[part, :, 128:192].astype(f32) for part in range(3)]
    turned = out_w[...].astype(f32).T
    shard[:, 384:512] = jnp.concatenate(thirds[:2], axis=1).astype(b16)
    shard[:, 512:640] = jnp.concatenate([thirds[2], turned[:, 0:64]], axis=1).astype(b16)
    shard[:, 640:768] = turned[:, 64:192].astype(b16)
    rows[...] = jnp.zeros_like(rows)
    count = kernel.shape[2]
    rows[0:4, 0 : small.shape[1]] = small[...].astype(f32)
    for part in range(3):
        rows[4 + part * heads : 4 + part * heads + heads, 0:count] = kernel[part].astype(f32)
    shard[:, 768:896] = rows[...].T[: shard.shape[0]].astype(b16)


def small_rows(scal, stacks, heads, norms, taps, columns, features):
    count = features.shape[0] // (2 * stacks[0].shape[0])
    for rel_seq, stack in enumerate(stacks):
        for rel in range(stack.shape[0]):
            block = stack[rel, :, 768:896].astype(f32)
            columns[group_rows(stack, rel, rel_seq, scal), :] = block
            group = (scal[1] ^ rel) * 2 + (scal[2] ^ rel_seq)
            features[pl.ds(pl.multiple_of(group * count, 8), count), :] = block[0:count]
    norms[...] = columns[...].T[0:8]
    taps[...] = jnp.zeros_like(taps)
    low = lanes_like((1, 128)) < 64
    for tap in range(KERNEL):
        turned = features[pl.ds(tap, HEAD_DIM, stride=KERNEL), :].T
        turned = jnp.concatenate([turned, jnp.zeros_like(turned)], axis=1)
        for part in range(3):
            one, two, three = (turned[4 + part * heads + i : 5 + part * heads + i] for i in range(3))
            taps[4 + tap : 5 + tap, part * PADW : part * PADW + 128] = jnp.where(low, one, half_roll(two))
            taps[4 + tap : 5 + tap, part * PADW + 128 : part * PADW + 256] = jnp.where(low, three, 0.0)


def norm_body(half, quarter, scal, *refs):
    pieces, hats, form_out, form, sem = refs[:4], *refs[4:]
    head = scal[0]
    for side in range(2):
        for rel in range(4):
            base = (head ^ rel) * quarter
            piece = pieces[2 * side + rel % 2]
            hat, _ = norm_rows(piece[rel // 2 * quarter : rel // 2 * quarter + quarter, :].astype(f32))
            if side == 0:
                hats[ds(half + base, quarter), :] = hat
                form[ds(base, quarter), :] = hat.astype(b16)
            else:
                hats[ds(base, quarter), :] = hat
        if side == 0:
            copy = pltpu.make_async_copy(form, form_out, sem)
            copy.start()
    copy.wait()


def front_body(half, quarter, heads, paired, scal, *refs):
    hats, w_own, w_other, cot = refs[:4]
    refs = refs[1:]
    refs = refs[3:]
    if not paired:
        norms_in, taps_in, refs = refs[0], refs[1], refs[2:]
    normed, projected, wpad, query, key, value, extra, norms, taps = refs[:9]
    normed_out, projected_out, wpad_out = normed, projected, wpad
    proj, columns, features, wo, normed, wpad, sems = refs[9:]
    if paired:
        small_rows(scal, (w_own, w_other), heads, norms, taps, columns, features)
    else:
        norms[...] = norms_in[...]
        taps[...] = taps_in[...]
    gain, bias = norms[0:1, :], norms[1:2, :]
    low = lanes_like((w_own.shape[1], 128)) < 64
    for rel_seq, stack in enumerate((w_own, w_other)):
        for rel in range(stack.shape[0]):
            rows = group_rows(stack, rel, rel_seq, scal)
            for part in range(3):
                wpad[rows, part * 256 : part * 256 + 128] = stack[rel, :, part * 128 : part * 128 + 128]
            shared = stack[rel, :, 384:512].astype(f32)
            wpad[rows, 128:256] = jnp.where(low, shared, 0.0).astype(b16)
            wpad[rows, 384:512] = jnp.where(low, half_roll(shared), 0.0).astype(b16)
            mid = stack[rel, :, 512:640].astype(f32)
            last = half_roll(stack[rel, :, 640:768].astype(f32))
            wpad[rows, 640:768] = jnp.where(low, mid, 0.0).astype(b16)
            wo[rows, 0:128] = jnp.where(low, half_roll(mid), last)
            wo[rows, 128:256] = last
    extra[0:quarter, :] = cot[...]
    width = heads * HEAD_DIM
    extra[quarter : quarter + width, :] = wo[...].T[0:width].astype(b16)
    proj[0:16, :] = jnp.zeros((16, proj.shape[1]), b16)

    def project(block, own):
        base = block * quarter
        rounded = (hats[ds(base, quarter), :] * gain + bias).astype(b16)
        proj[pl.ds(pl.multiple_of(base + 16, 16), quarter), :] = dot(rounded, wpad[...]).astype(b16)
        if own:
            rows = ds(base - half, quarter)
            normed[rows, :] = rounded

    @pl.loop(0, 4)
    def _(block):
        project(block, False)

    @pl.loop(4, 8)
    def _(block):
        project(block, True)

    copies = [
        pltpu.make_async_copy(wpad, wpad_out, sems.at[0]),
        pltpu.make_async_copy(normed, normed_out, sems.at[1]),
        pltpu.make_async_copy(proj.at[half : 2 * half + 16, :], projected_out, sems.at[2]),
    ]
    for copy in copies:
        copy.start()
    bounds = edges(scal)

    def convolve(block, own):
        base = block * quarter
        pos = base + lax.broadcasted_iota(jnp.int32, (quarter, 1), 0)
        start = doc_start(pos, bounds)
        for part, out in enumerate((query, key, value)):
            if part == 0 and not own:
                continue
            cols = slice(part * PADW, part * PADW + PADW)
            rows = proj[pl.ds(pl.multiple_of(base, 16), quarter + 16), cols].astype(f32)
            mixed = taps[4:5, cols] * rows[16:]
            for back in range(1, KERNEL):
                earlier = pltpu.roll(rows, back, 0)[16:]
                mixed = mixed + jnp.where(pos - back >= start, taps[4 + back : 5 + back, cols] * earlier, 0.0)
            mixed = mixed.astype(b16)
            if part == 0:
                out[ds(base - half, quarter), :] = mixed * jnp.asarray(HEAD_DIM**-0.5, b16)
            else:
                out[ds(base, quarter), :] = mixed

    @pl.loop(0, 4)
    def _(block):
        convolve(block, False)

    @pl.loop(4, 8)
    def _(block):
        convolve(block, True)

    for copy in copies:
        copy.wait()


def masked_queries(query, slots, heads):
    lane = lanes_like(query.shape) // HEAD_DIM
    for head in range(heads):
        slots[head] = jnp.where(lane == head, query[...], jnp.zeros((), b16))


def attention_body(half, heads, scal, query, key, value, packed, out_t, lse, vt, qm, peak, total):
    bounds = edges(scal)
    masked_queries(query, qm, heads)

    @pl.loop(0, 2 * half // 256)
    def _(block):
        turned = value[ds(block * 256, 256), :].astype(f32).T
        vt[:, ds(block * 256, 256)] = turned[: heads * HEAD_DIM].astype(b16)

    out_t[...] = jnp.zeros_like(out_t)
    peak[...] = jnp.full_like(peak, masked_score)
    total[...] = jnp.zeros_like(total)
    for block in range(half // QF):
        first = half + block * QF
        cols = slice(block * QF, block * QF + QF)
        pos = first + lanes_like((1, QF))
        start = doc_start(pos, bounds)
        low = doc_start(jnp.int32(first), bounds) // KB

        @pl.loop(low, (first + QF) // KB)
        def _(kb):
            keys = key[ds(kb * KB, KB), :]
            key_pos = kb * KB + lax.broadcasted_iota(jnp.int32, (KB, 1), 0)
            allowed = (key_pos >= start) & (key_pos <= pos)
            for head in range(heads):
                rows = slice(head * HEAD_DIM, head * HEAD_DIM + HEAD_DIM)
                one = slice(head, head + 1)
                scores = dot(keys, qm[head, cols, :], 1, 1)
                scores = jnp.where(allowed, scores, masked_score)
                old = peak[one, cols]
                new = jnp.maximum(old, jnp.max(scores, axis=0, keepdims=True))
                weights = jnp.exp(scores - new)
                shrink = jnp.exp(old - new)
                peak[one, cols] = new
                total[one, cols] = shrink * total[one, cols] + jnp.sum(weights, axis=0, keepdims=True)
                out_t[rows, cols] = shrink * out_t[rows, cols] + dot(
                    vt[rows, ds(kb * KB, KB)], weights.astype(b16)
                )

    for head in range(heads):
        rows = slice(head * HEAD_DIM, head * HEAD_DIM + HEAD_DIM)
        out_t[rows, :] = out_t[rows, :] / total[head : head + 1, :]
    lse[...] = peak[...] + jnp.log(jnp.maximum(total[...], 1e-30))
    for block in range(half // 256):
        cols = slice(block * 256, block * 256 + 256)
        packed[cols, :] = out_t[0:128, cols].T.astype(b16)
    for block in range(half // 512):
        cols = slice(block * 256, block * 256 + 256)
        later = slice(half // 2 + block * 256, half // 2 + block * 256 + 256)
        both = jnp.concatenate([out_t[128:192, cols], out_t[128:192, later]], axis=0)
        packed[half + block * 256 : half + block * 256 + 256, :] = both.T.astype(b16)


def back_blocks(half, heads, scal, first_kb, last_kb, refs, finish):
    key, value, qm, dom, lse, row_dot, kt, query_t, key_sum, value_sum = refs
    bounds = edges(scal)

    @pl.loop(first_kb, last_kb)
    def _(kb):
        key_sum[...] = jnp.zeros_like(key_sum)
        value_sum[...] = jnp.zeros_like(value_sum)
        for block in range(half // QB):
            first = half + block * QB
            cols = slice(block * QB, block * QB + QB)
            low = doc_start(jnp.int32(first), bounds)

            @pl.when((kb * KB + KB > low) & (kb * KB < first + QB))
            def _():
                pos = first + lanes_like((1, QB))
                start = doc_start(pos, bounds)
                keys = key[ds(kb * KB, KB), :]
                values = value[ds(kb * KB, KB), :]
                key_pos = kb * KB + lax.broadcasted_iota(jnp.int32, (KB, 1), 0)
                allowed = (key_pos >= start) & (key_pos <= pos)
                for head in range(heads):
                    rows = slice(head * HEAD_DIM, head * HEAD_DIM + HEAD_DIM)
                    one = slice(head, head + 1)
                    own_q = qm[head, cols, :]
                    own_g = dom[head, cols, :]
                    scores = jnp.where(allowed, dot(keys, own_q, 1, 1) - lse[one, cols], masked_score)
                    weights = jnp.exp(scores)
                    grads = weights * (dot(values, own_g, 1, 1) - row_dot[one, cols])
                    grads = grads.astype(b16)
                    value_sum[...] += dot(weights.astype(b16), own_g)
                    key_sum[...] += dot(grads, own_q)
                    query_t[rows, cols] += dot(kt[rows, ds(kb * KB, KB)], grads)

        finish(kb, key_sum[...], value_sum[...])


def spread_groups(source, scal, keep, sent, cols=slice(None)):
    for rel_seq, out in enumerate((keep, sent)):
        for rel in range(out.shape[0]):
            out[rel, :, cols] = source[group_rows(out, rel, rel_seq, scal), :].astype(out.dtype)


def branch_body(quarter, heads, scal, *refs):
    branches = refs[:4]
    extra, out_t, dout, row_dot, keep, sent, proj_grad, turned = refs[4:]
    head = scal[0]
    width = heads * HEAD_DIM
    weights = jnp.concatenate([extra[quarter:, :], jnp.zeros((PADW - width, extra.shape[1]), b16)], axis=0)
    proj_grad[...] = jnp.zeros_like(proj_grad)
    row_dot[...] = jnp.zeros_like(row_dot)
    for rel, branch in enumerate(branches):
        base = (head ^ rel) * quarter
        grad = dot(branch[...], weights, 1, 1).astype(b16)
        dout[ds(base, quarter), :] = grad
        attended = out_t[:, ds(base, quarter)]
        product = grad.astype(f32).T[:width] * attended
        for one in range(heads):
            row_dot[one : one + 1, ds(base, quarter)] = jnp.sum(
                product[one * HEAD_DIM : one * HEAD_DIM + HEAD_DIM], axis=0, keepdims=True
            )
        proj_grad[...] += dot(attended.astype(b16), branch[...])
    turned[...] = proj_grad[...].T
    spread_groups(turned, scal, keep, sent)


def remote_back_body(half, heads, scal, *refs):
    query, key, value, dout, lse, row_dot = refs[:6]
    remote, query_t, kt = refs[6:9]
    qm, dom, key_sum, value_sum = refs[9:]
    width = heads * HEAD_DIM
    masked_queries(query, qm, heads)
    masked_queries(dout, dom, heads)

    @pl.loop(0, 2 * half // 256)
    def _(block):
        kt[:, ds(block * 256, 256)] = key[ds(block * 256, 256), :].astype(f32).T[:width].astype(b16)

    query_t[...] = jnp.zeros_like(query_t)

    def finish(kb, dk, dv):
        rows = ds(kb * KB, KB)
        remote[rows, 0:128] = dk[:, 0:128].astype(b16)
        remote[rows, 128:256] = dv[:, 0:128].astype(b16)
        remote[rows, 256:384] = (dk[:, 128:256] + half_roll(dv[:, 128:256])).astype(b16)

    back_blocks(
        half, heads, scal, 0, half // KB,
        (key, value, qm, dom, lse, row_dot, kt, query_t, key_sum, value_sum), finish,
    )


def local_back_body(half, heads, scal, *refs):
    query, key, value, dout, lse, row_dot, kt, query_in, taps = refs[:9]
    dq, dk_out, dv_out, front = refs[9:13]
    qm, dom, key_sum, value_sum, query_t = refs[13:]
    masked_queries(query, qm, heads)
    masked_queries(dout, dom, heads)
    query_t[...] = query_in[...]

    def finish(kb, dk, dv):
        rows = ds(kb * KB - half, KB)
        dk_out[rows, :] = dk.astype(b16)
        dv_out[rows, :] = dv.astype(b16)

    back_blocks(
        half, heads, scal, half // KB, 2 * half // KB,
        (key, value, qm, dom, lse, row_dot, kt, query_t, key_sum, value_sum), finish,
    )
    width = heads * HEAD_DIM
    scale = HEAD_DIM**-0.5
    for block in range(half // 256):
        cols = slice(block * 256, block * 256 + 256)
        turned = (query_t[:, cols] * scale).T
        dq[cols, 0:128] = turned[:, 0:128].astype(b16)
        dq[cols, 128:256] = jnp.concatenate(
            [turned[:, 128:width], jnp.zeros((256, PADW - width), f32)], axis=1
        ).astype(b16)
    bounds = edges(scal)
    pos = half + lax.broadcasted_iota(jnp.int32, (8, 1), 0)
    start = doc_start(pos, bounds)
    for part, grads in enumerate((dq, dk_out, dv_out)):
        cols = slice(part * PADW, part * PADW + PADW)
        rounded = grads[0:16, :].astype(b16).astype(f32)[0:8]
        result = jnp.zeros((8, PADW), f32)
        for back in range(1, KERNEL):
            moved = pltpu.roll(jnp.where(pos - back >= start, taps[4 + back : 5 + back, cols] * rounded, 0.0), 8 - back, 0)
            place = lax.broadcasted_iota(jnp.int32, (8, 1), 0)
            result = result + jnp.where(place >= 8 - back, moved, 0.0)
        front[:, cols] = result


def weights_body(scal, *refs):
    own, other, inner, outer = refs
    width = inner.shape[1]
    for rel_seq, stack in enumerate((own, other)):
        for rel in range(stack.shape[0]):
            rows = group_rows(stack, rel, rel_seq, scal)
            inner[rows, :] = stack[rel, :, :width]
            outer[rows, :] = stack[rel, :, width:]


def feed_body(half, quarter, scal, *refs):
    attended, extras, inputs = refs[0:4], refs[4:8], refs[8:10]
    inner, outer, norms = refs[10:13]
    normed, squared, inner_grad, keep, sent, middle_own = refs[13:]
    head = scal[0]
    for rel in range(4):
        base = (head ^ rel) * quarter
        late = base >= half // 2
        middle = inputs[rel % 2][rel // 2 * quarter : rel // 2 * quarter + quarter, :].astype(f32)
        for part in range(4):
            left = attended[part][ds(base, quarter), :]
            right = attended[part][ds(half + lax.rem(base, half // 2), quarter), :].astype(f32)
            right = jnp.where(late, half_roll(right), right).astype(b16)
            both = jnp.concatenate([left, right], axis=1)
            weights = extras[part][quarter:, :]
            middle = middle + dot(both[:, : weights.shape[0]], weights)
        if rel == 0:
            middle_own[...] = middle
        hat, _ = norm_rows(middle)
        rounded = (hat * norms[2:3, :] + norms[3:4, :]).astype(b16)
        rows = slice(rel * quarter, rel * quarter + quarter)
        normed[rows, :] = rounded
        positive = jnp.maximum(dot(rounded, inner[...]), 0.0)
        squared[rows, :] = (positive * positive).astype(b16)
        grads = (dot(extras[rel][0:quarter, :], outer[...]) * 2.0 * positive).astype(b16)
        inner_grad[rows, :] = grads
        part = dot(grads, inner[...], 1, 1)
        place = slice((rel // 2) * quarter, (rel // 2) * quarter + quarter)
        if rel % 2 == 0:
            keep[place, :] = part
        else:
            sent[place, :] = part.astype(b16)


def outer_grads_body(quarter, scal, *refs):
    extras, squared, total, cot = refs[0:4], refs[4], refs[5], refs[6]
    for rel in range(4):
        cot[rel * quarter : rel * quarter + quarter, :] = extras[rel][0:quarter, :]
    for tile in range(total.shape[0] // 256):
        cols = slice(tile * 256, tile * 256 + 256)
        total[cols, :] = dot(cot[:, cols], squared[...], 0, 0)


def feed_grads_body(quarter, scal, *refs):
    normed, squared, inner_grad, outer, outer_total = refs[:5]
    keep, sent, kept, away, total = refs[5:]
    width = total.shape[1]
    for rel in range(4):
        rows = slice(rel * quarter, rel * quarter + quarter)
        part = dot(squared[rows, :], outer[...], 1, 1)
        place = slice((rel // 2) * quarter, (rel // 2) * quarter + quarter)
        if rel % 2 == 0:
            keep[place, :] = part
        else:
            sent[place, :] = part.astype(b16)
    for tile in range(total.shape[0] // 256):
        cols = slice(tile * 256, tile * 256 + 256)
        total[cols, :] = dot(normed[:, cols], inner_grad[...], 0, 0)
    spread_groups(total, scal, kept, away, slice(0, width))
    spread_groups(outer_total, scal, kept, away, slice(width, 2 * width))


def norm_back_body(row, scal, part, got, values, skip, norms, grad_in, rounded, sums):
    del scal
    grad = part[...] + got[0 : part.shape[0], :].astype(f32)
    hat, inverse = norm_rows(values[...].astype(f32))
    scaled = grad * norms[row : row + 1, :]
    back = inverse * (
        scaled
        - jnp.mean(scaled, axis=-1, keepdims=True)
        - hat * jnp.mean(scaled * hat, axis=-1, keepdims=True)
    )
    result = skip[...].astype(f32) + back
    grad_in[...] = result
    rounded[...] = result.astype(b16)
    sums[...] = jnp.zeros_like(sums)
    sums[0:1, :] = jnp.sum(grad * hat, axis=0, keepdims=True)
    sums[1:2, :] = jnp.sum(grad, axis=0, keepdims=True)


def tail_body(half, quarter, scal, *refs):
    dq, dk, dv, remote, front, projected, normed, taps = refs[:8]
    proj_grad, w_keep, w_send, sums = refs[8:12]
    mixed, total, dense = refs[12:]
    bounds = edges(scal)
    low = lanes_like((quarter, 128)) < 64
    sums[...] = jnp.zeros_like(sums)
    for block in range(half // quarter):
        rows = slice(block * quarter, block * quarter + quarter)
        shared = remote[rows, 256:384].astype(f32)
        mixed[rows, 0:256] = dq[rows, :]
        mixed[rows, 256:384] = (dk[rows, 0:128].astype(f32) + remote[rows, 0:128].astype(f32)).astype(b16)
        mixed[rows, 384:512] = (dk[rows, 128:256].astype(f32) + jnp.where(low, shared, 0.0)).astype(b16)
        mixed[rows, 512:640] = (dv[rows, 0:128].astype(f32) + remote[rows, 128:256].astype(f32)).astype(b16)
        mixed[rows, 640:768] = (dv[rows, 128:256].astype(f32) + jnp.where(low, half_roll(shared), 0.0)).astype(b16)
    mixed[half : half + 16, :] = jnp.zeros((16, mixed.shape[1]), b16)

    @pl.loop(0, half // quarter)
    def _(block):
        base = block * quarter
        pos = half + base + lax.broadcasted_iota(jnp.int32, (quarter + 16, 1), 0)
        start = doc_start(pos, bounds)
        for part in range(3):
            cols = slice(part * PADW, part * PADW + PADW)
            grads = mixed[pl.ds(pl.multiple_of(base, 16), quarter + 16), cols].astype(f32)
            values = projected[pl.ds(pl.multiple_of(base, 16), quarter + 16), cols].astype(f32)
            here = grads[:quarter]
            result = taps[4:5, cols] * here
            sums[4:5, cols] += jnp.sum(here * values[16:], axis=0, keepdims=True)
            for back in range(1, KERNEL):
                same = pos - back >= start
                held = jnp.where(same, grads, 0.0)
                ahead = pltpu.roll(held, quarter + 16 - back, 0)[:quarter]
                result = result + taps[4 + back : 5 + back, cols] * ahead
                earlier = pltpu.roll(values, back, 0)[16:]
                sums[4 + back : 5 + back, cols] += jnp.sum(held[:quarter] * earlier, axis=0, keepdims=True)
            proj_grad[ds(base, quarter), cols] = result.astype(b16)

        @pl.when(block == half // quarter - 1)
        def _():
            added = jnp.concatenate([jnp.zeros((8, front.shape[1]), f32), front[...]], axis=0)
            tail_pos = 2 * half - 16 + lax.broadcasted_iota(jnp.int32, (32, 1), 0)
            tail_start = doc_start(tail_pos, bounds)
            grads = mixed[half - 16 : half + 16, :].astype(f32)
            result = taps[4:5, :] * grads[:16]
            for back in range(1, KERNEL):
                held = jnp.where(tail_pos - back >= tail_start, grads, 0.0)
                result = result + taps[4 + back : 5 + back, :] * pltpu.roll(held, 32 - back, 0)[:16]
            proj_grad[half - 16 : half, :] = (result + added).astype(b16)

    for tile in range(total.shape[0] // 256):
        rows = slice(tile * 256, tile * 256 + 256)
        total[rows, :] = dot(normed[:, rows], proj_grad[...], 0, 0)
        for part in range(3):
            dense[rows, part * 128 : part * 128 + 128] = total[rows, part * 256 : part * 256 + 128]
        dense[rows, 384:512] = total[rows, 128:256] + half_roll(total[rows, 384:512])
        dense[rows, 512:640] = total[rows, 640:768]
    spread_groups(dense, scal, w_keep, w_send)


def tail_norm_body(quarter, scal, proj_grad, wpad, form, second, keep, sent, sums):
    head = scal[0]
    sums[...] = jnp.zeros_like(sums)
    sums[2:4, :] = second[0:2, :]
    for rel in (1, 3, 0, 2):
        base = (head ^ rel) * quarter
        part = dot(proj_grad[ds(base, quarter), :], wpad[...], 1, 1)
        sums[0:1, :] += jnp.sum(part * form[ds(base, quarter), :].astype(f32), axis=0, keepdims=True)
        sums[1:2, :] += jnp.sum(part, axis=0, keepdims=True)
        place = slice((rel // 2) * quarter, (rel // 2) * quarter + quarter)
        if rel % 2 == 0:
            keep[place, :] = part
        else:
            sent[place, :] = part.astype(b16)
    keep[2 * quarter :, :] = sums[...]
    sent[2 * quarter :, :] = sums[...].astype(b16)


def pad_heads(values, width):
    shaped = values.reshape(values.shape[:-1] + (3, width))
    padded = jnp.pad(shaped, [(0, 0)] * (shaped.ndim - 1) + [(0, PADW - width)])
    return padded.reshape(values.shape[:-1] + (3 * PADW,))


def gather_small(norms, conv_kernel, model, width):
    norms = lax.all_gather(norms, ("batch", "seq"), axis=0, tiled=True).astype(f32).T
    taps = lax.all_gather(conv_kernel, ("batch", "seq"), axis=2, tiled=True).astype(f32)
    taps = taps.reshape(3, width, KERNEL).transpose(2, 0, 1).reshape(KERNEL, 3 * width)
    return jnp.pad(norms, ((0, 4), (0, 0))), jnp.pad(pad_heads(taps, width), ((4, 1), (0, 0)))


def on_device(
    block_input, segment_ids, norm1_gain, norm1_bias, qkv_weight, conv_kernel, out_weight,
    norm2_gain, norm2_bias, inner_weight, outer_weight, cotangent,
):
    quarter = block_input.shape[2]
    half = quarter * lax.axis_size("heads")
    width = qkv_weight.shape[2]
    heads = width // HEAD_DIM
    group = qkv_weight.shape[0]
    groups = lax.axis_size("batch") * lax.axis_size("seq")
    model = group * groups
    hidden = inner_weight.shape[1]
    head, batch, seq = lax.axis_index("heads"), lax.axis_index("batch"), lax.axis_index("seq")
    own = batch * 2 + seq
    stacks = (groups // 2, group) if pairwise(group) else (1, model // 2)

    ids = segment_ids.reshape(-1)
    docs = jnp.arange(DOCS, dtype=jnp.int32)
    firsts = jnp.sum((ids[None, :] < docs[:, None]).astype(jnp.int32), axis=1) - (seq - 1) * half
    scal = jnp.concatenate([jnp.stack([head, batch, seq]), firsts, jnp.zeros((1,), jnp.int32)]).astype(jnp.int32)

    x_own = block_input.reshape(quarter, model)
    cot_own = cotangent.reshape(quarter, model)

    share = conv_kernel.shape[2]

    paired = pairwise(group)
    qkv = qkv_weight
    small = [norm1_gain, norm1_bias, norm2_gain, norm2_bias]
    small_args = []
    if paired:
        (shard,) = call(
            functools.partial(shard_body, heads), [((group, 896), b16)],
            qkv.transpose(1, 0, 2), out_weight, jnp.stack(small), conv_kernel,
            scratch=[
                pltpu.VMEM((3, group, width), b16), pltpu.VMEM(out_weight.shape, b16), pltpu.VMEM((4, group), b16),
                pltpu.VMEM(conv_kernel.shape, b16), pltpu.VMEM((128, 128), f32), pltpu.SemaphoreType.DMA((4,)),
            ],
            limit=4, plain=True,
        )
    else:
        small_args = gather_small(jnp.stack(small, axis=1), conv_kernel, model, width)
        shard = jnp.concatenate(
            [qkv[:, 0, :128], qkv[:, 1, :128], qkv[:, 2, :128], qkv[:, 0, 128:], qkv[:, 1, 128:], qkv[:, 2, 128:],
             out_weight.T, jnp.zeros((group, 128), b16)], axis=1,
        )
    shards, first_shard = gather_batch_steps(shard)
    far_seq = [(2 * h + t, 2 * (h ^ 2) + (t ^ 1)) for h in range(lax.axis_size("heads")) for t in range(2)]
    x_other, x_far, x_far_other = after(
        (swap(x_own, "seq", 1), swap(x_own, "heads", 2), lax.ppermute(x_own, ("heads", "seq"), far_seq)), first_shard
    )
    x_pieces = gather_cores(x_own, x_far)
    y_pieces = gather_cores(x_other, x_far_other)
    hats, form_one = call(
        functools.partial(norm_body, half, quarter),
        [((2 * half, model), f32), ((half, model), b16)],
        scal, *x_pieces, *y_pieces, flops=2 * half * model, limit=8, away=(1,),
        scratch=[pltpu.VMEM((half, model), b16), pltpu.SemaphoreType.DMA],
    )
    w_own, w_other = gather_seq(shards)
    w_other = after(w_other, hats)

    feed_shards = gather_batch(after(jnp.concatenate([inner_weight, outer_weight.T], axis=1), shards))

    normed_one, projected, wpad, query, key, value, extra, norms, taps = call(
        functools.partial(front_body, half, quarter, heads, paired),
        [
            ((half, model), b16), ((half + 16, 3 * PADW), b16), ((model, 3 * PADW), b16),
            ((half, PADW), b16), ((2 * half, PADW), b16), ((2 * half, PADW), b16), ((quarter + width, model), b16),
            ((8, model), f32), ((8, 3 * PADW), f32),
        ],
        scal, hats, w_own, w_other, cot_own, *small_args,
        scratch=[
            pltpu.VMEM((2 * half + 16, 3 * PADW), b16),
            pltpu.VMEM((model, 128), f32), pltpu.VMEM((KERNEL * HEAD_DIM, 128), f32), pltpu.VMEM((model, PADW), f32),
            pltpu.VMEM((half, model), b16), pltpu.VMEM((model, 3 * PADW), b16), pltpu.SemaphoreType.DMA((3,)),
        ],
        flops=4 * half * model * 3 * width, limit=14, away=(0, 1, 2),
    )

    feed_own, feed_other = gather_seq(after(feed_shards, query))
    extra_pieces = gather_heads(extra)

    packed, out_t, lse = call(
        functools.partial(attention_body, half, heads),
        [((half + half // 2, 128), b16), ((width, half), f32), ((8, half), f32)],
        scal, query, key, value,
        scratch=[
            pltpu.VMEM((width, 2 * half), b16), pltpu.VMEM((heads, half, PADW), b16),
            pltpu.VMEM((8, half), f32), pltpu.VMEM((8, half), f32),
        ],
        flops=4 * half * half * width, limit=7,
    )
    packed_pieces = gather_heads(packed)
    feed_own, feed_other, _ = lax.optimization_barrier((feed_own, feed_other, packed))
    inner_full, outer_full = call(
        weights_body, [((model, hidden), b16), ((model, hidden), b16)], scal, feed_own, feed_other, limit=4,
    )

    normed_two, squared, inner_grad, keep, sent, middle_own = call(
        functools.partial(feed_body, half, quarter),
        [((half, model), b16), ((half, hidden), b16), ((half, hidden), b16),
         ((2 * quarter, model), f32), ((2 * quarter, model), b16), ((quarter, model), f32)],
        scal, *packed_pieces, *extra_pieces, *x_pieces, inner_full, outer_full, norms,
        flops=2 * half * model * (model + 3 * hidden), limit=12,
    )
    got = swap(sent, "heads", 1)
    (outer_total,) = call(
        functools.partial(outer_grads_body, quarter), [((model, hidden), f32)],
        scal, *extra_pieces, squared,
        scratch=[pltpu.VMEM((half, model), b16)], flops=2 * half * model * hidden, limit=8,
    )
    got = after(got, outer_total)
    dn_here, dn_far = scatter_far(keep, got, quarter)
    out_keep, out_sent, ff_keep, ff_send = call(
        functools.partial(feed_grads_body, quarter),
        [((2 * quarter, model), f32), ((2 * quarter, model), b16),
         (stacks + (2 * hidden,), b16), (stacks + (2 * hidden,), b16)],
        scal, after(normed_two, got), squared, inner_grad, outer_full, outer_total,
        scratch=[pltpu.VMEM((model, hidden), f32)],
        flops=4 * half * model * hidden, limit=8,
    )
    dn_far = after(dn_far, out_sent)
    ff_got = scatter_seq(ff_send)
    middle_grad, branch, sums_two = call(
        functools.partial(norm_back_body, 2),
        [((quarter, model), f32), ((quarter, model), b16), ((8, model), f32)],
        scal, dn_here, dn_far, middle_own, cot_own, norms, limit=6,
    )
    branch_pieces = gather_heads(branch)
    out_got = swap(after(out_sent, branch), "heads", 1)

    dout, row_dot, pj_keep, pj_send = call(
        functools.partial(branch_body, quarter, heads),
        [((half, PADW), b16), ((8, half), f32), (stacks + (width,), f32), (stacks + (width,), b16)],
        scal, *branch_pieces, extra, out_t,
        scratch=[pltpu.VMEM((width, model), f32), pltpu.VMEM((model, width), f32)],
        flops=4 * half * model * width, limit=6,
    )
    pj_got = scatter_seq(pj_send)
    out_here, out_far = scatter_far(out_keep, after(out_got, dout), quarter)
    remote, query_t, kt = call(
        functools.partial(remote_back_body, half, heads),
        [((half, 384), b16), ((width, half), f32), ((width, 2 * half), b16)],
        scal, query, key, value, dout, lse, row_dot,
        scratch=[
            pltpu.VMEM((heads, half, PADW), b16), pltpu.VMEM((heads, half, PADW), b16),
            pltpu.VMEM((KB, PADW), f32), pltpu.VMEM((KB, PADW), f32),
        ],
        flops=10 * half * half * width, limit=8,
    )
    remote_in = lax.ppermute(remote, "seq", [(1, 0)])
    ff_got, pj_got = after((ff_got, pj_got), remote)
    ff_own, ff_rest = join_seq((ff_keep, ff_got))

    dq, dk, dv, front = call(
        functools.partial(local_back_body, half, heads),
        [((half, PADW), b16), ((half, PADW), b16), ((half, PADW), b16), ((8, 3 * PADW), f32)],
        scal, query, key, value, dout, lse, row_dot, kt, after(query_t, ff_rest, pj_got), taps,
        scratch=[
            pltpu.VMEM((heads, half, PADW), b16), pltpu.VMEM((heads, half, PADW), b16),
            pltpu.VMEM((KB, PADW), f32), pltpu.VMEM((KB, PADW), f32), pltpu.VMEM((width, half), f32),
        ],
        flops=10 * half * half * width, limit=8,
    )
    front_in = lax.ppermute(front, "seq", [(1, 0)])
    remote_in = after(remote_in, dq)
    block_output = (middle_own + out_here + after(out_far, dq).astype(f32)).astype(b16)

    proj_grad, w_keep, w_send, sums_taps = call(
        functools.partial(tail_body, half, quarter),
        [((half, 3 * PADW), b16), (stacks + (640,), f32), (stacks + (640,), b16), ((8, 3 * PADW), f32)],
        scal, dq, dk, dv, remote_in, front_in, projected, normed_one, taps,
        scratch=[
            pltpu.VMEM((half + 16, 3 * PADW), b16), pltpu.VMEM((model, 3 * PADW), f32), pltpu.VMEM((model, 640), f32),
        ],
        flops=2 * half * model * 3 * width, limit=12,
    )
    w_got = scatter_seq(w_send)
    keep, sent, sums = call(
        functools.partial(tail_norm_body, quarter),
        [((2 * quarter + 8, model), f32), ((2 * quarter + 8, model), b16), ((8, model), f32)],
        scal, proj_grad, wpad, form_one, sums_two,
        flops=2 * half * model * 3 * width, limit=8,
    )
    got = swap(sent, "heads", 1)
    dn_here, dn_far = scatter_far(keep, got, quarter)
    small = sums + got[2 * quarter :].astype(f32)
    small = jnp.concatenate([small[0:4], sums_taps[4:8]])
    small = small + swap(small, "seq", 1)
    ff_out, _ = scatter_batch(ff_own, ff_rest, None, small)
    small = jnp.concatenate([small[0:4] + swap(small[0:4], "heads", 2), small[4:8]])
    qkv_own, qkv_rest = join_seq((w_keep, after(w_got, small)), (pj_keep, pj_got))
    cut = small.shape[1] // 2
    small = jnp.concatenate([small[:, :cut], small[:, cut:]])
    input_grad, _, _ = call(
        functools.partial(norm_back_body, 0),
        [((quarter, model), f32), ((quarter, model), b16), ((8, model), f32)],
        scal, dn_here, dn_far, x_own, middle_grad, norms, limit=6,
    )
    qkv_out, small = scatter_batch(qkv_own, qkv_rest, small, input_grad)
    pj_out = qkv_out[:, 640:]
    small = jnp.concatenate([small[:8], small[8:]], axis=1)

    qkv_out = jnp.stack(
        [
            jnp.concatenate([qkv_out[:, 0:128], qkv_out[:, 384:448]], axis=1),
            jnp.concatenate([qkv_out[:, 128:256], qkv_out[:, 448:512]], axis=1),
            jnp.concatenate([qkv_out[:, 256:384], qkv_out[:, 512:576]], axis=1),
        ],
        axis=1,
    )
    gains = lax.dynamic_slice_in_dim(small[0:4], own * group, group, 1)
    kernel_out = small[4 : 4 + KERNEL].reshape(KERNEL, 3, PADW)[:, :, :width].reshape(KERNEL, 3, heads, HEAD_DIM)
    kernel_out = kernel_out.transpose(1, 2, 3, 0).reshape(3, heads, HEAD_DIM * KERNEL)
    kernel_out = lax.dynamic_slice_in_dim(kernel_out, own * share, share, 2)
    return (
        block_output.reshape(block_input.shape),
        input_grad.reshape(block_input.shape),
        gains[0],
        gains[1],
        qkv_out,
        kernel_out,
        pj_out.T,
        gains[2],
        gains[3],
        ff_out[:, :hidden],
        ff_out[:, hidden : 2 * hidden].T,
    )


def solution(mesh):
    return jax.shard_map(
        on_device,
        mesh=mesh,
        in_specs=(
            P("batch", "seq", "heads", None),
            P("batch", None),
            P(("batch", "seq")),
            P(("batch", "seq")),
            P(("batch", "seq"), None, "heads"),
            P(None, "heads", ("batch", "seq")),
            P("heads", ("batch", "seq")),
            P(("batch", "seq")),
            P(("batch", "seq")),
            P(("batch", "seq"), "heads"),
            P("heads", ("batch", "seq")),
            P("batch", "seq", "heads", None),
        ),
        out_specs=(
            P("batch", "seq", "heads", None),
            P("batch", "seq", "heads", None),
            P(("batch", "seq")),
            P(("batch", "seq")),
            P(("batch", "seq"), None, "heads"),
            P(None, "heads", ("batch", "seq")),
            P("heads", ("batch", "seq")),
            P(("batch", "seq")),
            P(("batch", "seq")),
            P(("batch", "seq"), "heads"),
            P("heads", ("batch", "seq")),
        ),
        check_vma=False,
    )
```

```python
import functools

import jax
import jax.numpy as jnp
from jax import lax
from jax.experimental import pallas as pl
from jax.experimental.pallas import tpu as pltpu
from jax.sharding import PartitionSpec as P

HEAD_DIM = 64
KERNEL = 3
DOCS = 4
PADW = 256
QB = 512
QF = 256
KB = 256

epsilon = 1e-05
masked_score = -1e30
f32 = jnp.float32
b16 = jnp.bfloat16

VMEM = pl.BlockSpec(memory_space=pltpu.VMEM)
SMEM = pl.BlockSpec(memory_space=pltpu.SMEM)
HBM = pl.BlockSpec(memory_space=pl.ANY)


def after(value, *others):
    return lax.optimization_barrier((value,) + others)[0]


def swap(shard, axis, by):
    return lax.ppermute(shard, axis, [(i, i ^ by) for i in range(lax.axis_size(axis))])


def gather_heads(shard):
    far = swap(shard, "heads", 2)
    near = swap(shard, "heads", 1)
    return [shard, near, far, swap(far, "heads", 1)]


def gather_cores(shard, far):
    both = jnp.concatenate([shard, far])
    return [both, swap(both, "heads", 1)]


def pairwise(group):
    return group % 32 == 0


def gather_batch(shard):
    if not pairwise(shard.shape[0]):
        return (shard,)
    return (shard,) + tuple(swap(shard, "batch", by) for by in range(1, lax.axis_size("batch")))


def gather_batch_steps(shard):
    if not pairwise(shard.shape[0]) or lax.axis_size("batch") != 4:
        shards = gather_batch(shard)
        return shards, shards[-1]
    far = swap(shard, "batch", 2)
    near = swap(jnp.concatenate([shard, far]), "batch", 1)
    rows = shard.shape[0]
    return (shard, near[:rows], far, near[rows:]), far


def gather_seq(shards):
    rows, columns = shards[0].shape
    if not pairwise(rows):
        whole = lax.all_gather(shards[0], ("batch", "seq"), axis=0, tiled=True)
        return tuple(whole.reshape(2, 1, -1, columns))
    stack = jnp.stack(shards)
    return stack, swap(stack, "seq", 1)


def scatter_seq(sent):
    return sent if sent.shape[0] == 1 else swap(sent, "seq", 1)


def join_seq(*parts):
    if parts[0][0].shape[0] == 1:
        whole = [jnp.concatenate([keep[0].astype(b16), sent[0]]) for keep, sent in parts]
        return None, jnp.concatenate(whole, axis=-1)
    total = jnp.concatenate([keep.astype(f32) + got.astype(f32) for keep, got in parts], axis=-1)
    return total[0], total[1:].astype(b16)


def scatter_batch(own, rest, more, *others):
    if own is None:
        total = lax.psum_scatter(rest, ("batch", "seq"), scatter_dimension=0, tiled=True).astype(f32)
        return total, None if more is None else lax.psum(more, "batch")
    count = own.shape[0]
    payloads = [rest[by] for by in range(rest.shape[0])]
    if more is not None:
        tail = jnp.pad(more, ((0, 0), (0, own.shape[1] - more.shape[1]))).astype(b16)
        payloads = [jnp.concatenate([payload, tail]) for payload in payloads]
    pieces = [swap(payload, "batch", by + 1) for by, payload in enumerate(payloads)]
    for piece in after(pieces, *others) if others else pieces:
        own = own + piece[:count].astype(f32)
        if more is not None:
            more = more + piece[count:, : more.shape[1]].astype(f32)
    return own, more


def scatter_far(keep, got, rows):
    far = (keep[rows : 2 * rows].astype(f32) + got[rows : 2 * rows].astype(f32)).astype(b16)
    here = keep[:rows].astype(f32) + got[:rows].astype(f32)
    return here, swap(far, "heads", 2)


def call(body, outs, *args, scratch=(), flops=0, limit=16, plain=False, away=()):
    in_specs = [HBM] * len(args) if plain else [SMEM] + [VMEM] * (len(args) - 1)
    return pl.pallas_call(
        body,
        out_shape=[jax.ShapeDtypeStruct(*o) for o in outs],
        in_specs=in_specs,
        out_specs=[HBM if index in away else VMEM for index in range(len(outs))],
        scratch_shapes=list(scratch),
        compiler_params=pltpu.CompilerParams(vmem_limit_bytes=limit << 20),
        cost_estimate=pl.CostEstimate(flops=flops // 16, transcendentals=0, bytes_accessed=0),
    )(*args)


def dot(a, b, ca=1, cb=0):
    return lax.dot_general(a, b, (((ca,), (cb,)), ((), ())), preferred_element_type=f32)


def edges(scal):
    return [scal[3 + d] for d in range(DOCS)]


def doc_start(pos, bounds):
    start = bounds[0] + jnp.zeros_like(pos)
    for edge in bounds[1:]:
        start = jnp.where(pos >= edge, edge, start)
    return start


def lanes_like(shape):
    return lax.broadcasted_iota(jnp.int32, shape, 1)


def half_roll(block):
    return pltpu.roll(block, 64, 1)


def norm_rows(values):
    average = jnp.mean(values, axis=-1, keepdims=True)
    centered = values - average
    inverse = lax.rsqrt(jnp.mean(centered * centered, axis=-1, keepdims=True) + epsilon)
    return centered * inverse, inverse


def group_rows(stack, rel, rel_seq, scal):
    return some_rows(stack.shape[1], stack.shape[0] > 1, rel, rel_seq, scal)


def some_rows(count, paired, rel, rel_seq, scal):
    if not paired:
        return slice(rel_seq * count, rel_seq * count + count)
    return pl.ds(pl.multiple_of(((scal[1] ^ rel) * 2 + (scal[2] ^ rel_seq)) * count, 32), count)


def ds(start, size):
    return pl.ds(pl.multiple_of(start, size), size)


def shard_body(heads, *refs):
    sources, shard, (qkv, out_w, small, kernel), rows, sems = refs[:4], refs[4], refs[5:9], refs[9], refs[10]
    copies = [
        pltpu.make_async_copy(source, target, sems.at[index])
        for index, (source, target) in enumerate(zip(sources, (qkv, out_w, small, kernel)))
    ]
    for copy in copies:
        copy.start()
    for copy in copies:
        copy.wait()
    for part in range(3):
        shard[:, part * 128 : part * 128 + 128] = qkv[part, :, 0:128]
    thirds = [qkv[part, :, 128:192].astype(f32) for part in range(3)]
    turned = out_w[...].astype(f32).T
    shard[:, 384:512] = jnp.concatenate(thirds[:2], axis=1).astype(b16)
    shard[:, 512:640] = jnp.concatenate([thirds[2], turned[:, 0:64]], axis=1).astype(b16)
    shard[:, 640:768] = turned[:, 64:192].astype(b16)
    rows[...] = jnp.zeros_like(rows)
    count = kernel.shape[2]
    rows[0:4, 0 : small.shape[1]] = small[...].astype(f32)
    for part in range(3):
        rows[4 + part * heads : 4 + part * heads + heads, 0:count] = kernel[part].astype(f32)
    shard[:, 768:896] = rows[...].T[: shard.shape[0]].astype(b16)


def small_rows(scal, stacks, heads, norms, taps, columns, features):
    count = features.shape[0] // (2 * stacks[0].shape[0])
    for rel_seq, stack in enumerate(stacks):
        for rel in range(stack.shape[0]):
            block = stack[rel, :, 768:896].astype(f32)
            columns[group_rows(stack, rel, rel_seq, scal), :] = block
            group = (scal[1] ^ rel) * 2 + (scal[2] ^ rel_seq)
            features[pl.ds(pl.multiple_of(group * count, 8), count), :] = block[0:count]
    norms[...] = columns[...].T[0:8]
    taps[...] = jnp.zeros_like(taps)
    low = lanes_like((1, 128)) < 64
    for tap in range(KERNEL):
        turned = features[pl.ds(tap, HEAD_DIM, stride=KERNEL), :].T
        turned = jnp.concatenate([turned, jnp.zeros_like(turned)], axis=1)
        for part in range(3):
            one, two, three = (turned[4 + part * heads + i : 5 + part * heads + i] for i in range(3))
            taps[4 + tap : 5 + tap, part * PADW : part * PADW + 128] = jnp.where(low, one, half_roll(two))
            taps[4 + tap : 5 + tap, part * PADW + 128 : part * PADW + 256] = jnp.where(low, three, 0.0)


def norm_body(half, quarter, scal, *refs):
    pieces, hats, form_out, form, sem = refs[:4], *refs[4:]
    head = scal[0]
    for side in range(2):
        for rel in range(4):
            base = (head ^ rel) * quarter
            piece = pieces[2 * side + rel % 2]
            hat, _ = norm_rows(piece[rel // 2 * quarter : rel // 2 * quarter + quarter, :].astype(f32))
            if side == 0:
                hats[ds(half + base, quarter), :] = hat
                form[ds(base, quarter), :] = hat.astype(b16)
            else:
                hats[ds(base, quarter), :] = hat
        if side == 0:
            copy = pltpu.make_async_copy(form, form_out, sem)
            copy.start()
    copy.wait()


def front_body(half, quarter, heads, paired, scal, *refs):
    hats, w_own, w_other, cot = refs[:4]
    refs = refs[1:]
    refs = refs[3:]
    if not paired:
        norms_in, taps_in, refs = refs[0], refs[1], refs[2:]
    normed, projected, wpad, query, key, value, extra, norms, taps = refs[:9]
    normed_out, projected_out, wpad_out = normed, projected, wpad
    proj, columns, features, wo, normed, wpad, sems = refs[9:]
    if paired:
        small_rows(scal, (w_own, w_other), heads, norms, taps, columns, features)
    else:
        norms[...] = norms_in[...]
        taps[...] = taps_in[...]
    gain, bias = norms[0:1, :], norms[1:2, :]
    low = lanes_like((w_own.shape[1], 128)) < 64
    for rel_seq, stack in enumerate((w_own, w_other)):
        for rel in range(stack.shape[0]):
            rows = group_rows(stack, rel, rel_seq, scal)
            for part in range(3):
                wpad[rows, part * 256 : part * 256 + 128] = stack[rel, :, part * 128 : part * 128 + 128]
            shared = stack[rel, :, 384:512].astype(f32)
            wpad[rows, 128:256] = jnp.where(low, shared, 0.0).astype(b16)
            wpad[rows, 384:512] = jnp.where(low, half_roll(shared), 0.0).astype(b16)
            mid = stack[rel, :, 512:640].astype(f32)
            last = half_roll(stack[rel, :, 640:768].astype(f32))
            wpad[rows, 640:768] = jnp.where(low, mid, 0.0).astype(b16)
            wo[rows, 0:128] = jnp.where(low, half_roll(mid), last)
            wo[rows, 128:256] = last
    extra[0:quarter, :] = cot[...]
    width = heads * HEAD_DIM
    extra[quarter : quarter + width, :] = wo[...].T[0:width].astype(b16)
    proj[0:16, :] = jnp.zeros((16, proj.shape[1]), b16)

    def project(block, own):
        base = block * quarter
        rounded = (hats[ds(base, quarter), :] * gain + bias).astype(b16)
        proj[pl.ds(pl.multiple_of(base + 16, 16), quarter), :] = dot(rounded, wpad[...]).astype(b16)
        if own:
            rows = ds(base - half, quarter)
            normed[rows, :] = rounded

    @pl.loop(0, 4)
    def _(block):
        project(block, False)

    @pl.loop(4, 8)
    def _(block):
        project(block, True)

    copies = [
        pltpu.make_async_copy(wpad, wpad_out, sems.at[0]),
        pltpu.make_async_copy(normed, normed_out, sems.at[1]),
        pltpu.make_async_copy(proj.at[half : 2 * half + 16, :], projected_out, sems.at[2]),
    ]
    for copy in copies:
        copy.start()
    bounds = edges(scal)

    def convolve(block, own):
        base = block * quarter
        pos = base + lax.broadcasted_iota(jnp.int32, (quarter, 1), 0)
        start = doc_start(pos, bounds)
        for part, out in enumerate((query, key, value)):
            if part == 0 and not own:
                continue
            cols = slice(part * PADW, part * PADW + PADW)
            rows = proj[pl.ds(pl.multiple_of(base, 16), quarter + 16), cols].astype(f32)
            mixed = taps[4:5, cols] * rows[16:]
            for back in range(1, KERNEL):
                earlier = pltpu.roll(rows, back, 0)[16:]
                mixed = mixed + jnp.where(pos - back >= start, taps[4 + back : 5 + back, cols] * earlier, 0.0)
            mixed = mixed.astype(b16)
            if part == 0:
                out[ds(base - half, quarter), :] = mixed * jnp.asarray(HEAD_DIM**-0.5, b16)
            else:
                out[ds(base, quarter), :] = mixed

    @pl.loop(0, 4)
    def _(block):
        convolve(block, False)

    @pl.loop(4, 8)
    def _(block):
        convolve(block, True)

    for copy in copies:
        copy.wait()


def masked_queries(query, slots, heads):
    lane = lanes_like(query.shape) // HEAD_DIM
    for head in range(heads):
        slots[head] = jnp.where(lane == head, query[...], jnp.zeros((), b16))


def attention_body(half, heads, scal, query, key, value, packed, out_t, lse, vt, qm, peak, total):
    bounds = edges(scal)
    masked_queries(query, qm, heads)

    @pl.loop(0, 2 * half // 256)
    def _(block):
        turned = value[ds(block * 256, 256), :].astype(f32).T
        vt[:, ds(block * 256, 256)] = turned[: heads * HEAD_DIM].astype(b16)

    out_t[...] = jnp.zeros_like(out_t)
    peak[...] = jnp.full_like(peak, masked_score)
    total[...] = jnp.zeros_like(total)
    for block in range(half // QF):
        first = half + block * QF
        cols = slice(block * QF, block * QF + QF)
        pos = first + lanes_like((1, QF))
        start = doc_start(pos, bounds)
        low = doc_start(jnp.int32(first), bounds) // KB

        @pl.loop(low, (first + QF) // KB)
        def _(kb):
            keys = key[ds(kb * KB, KB), :]
            key_pos = kb * KB + lax.broadcasted_iota(jnp.int32, (KB, 1), 0)
            allowed = (key_pos >= start) & (key_pos <= pos)
            for head in range(heads):
                rows = slice(head * HEAD_DIM, head * HEAD_DIM + HEAD_DIM)
                one = slice(head, head + 1)
                scores = dot(keys, qm[head, cols, :], 1, 1)
                scores = jnp.where(allowed, scores, masked_score)
                old = peak[one, cols]
                new = jnp.maximum(old, jnp.max(scores, axis=0, keepdims=True))
                weights = jnp.exp(scores - new)
                shrink = jnp.exp(old - new)
                peak[one, cols] = new
                total[one, cols] = shrink * total[one, cols] + jnp.sum(weights, axis=0, keepdims=True)
                out_t[rows, cols] = shrink * out_t[rows, cols] + dot(
                    vt[rows, ds(kb * KB, KB)], weights.astype(b16)
                )

    for head in range(heads):
        rows = slice(head * HEAD_DIM, head * HEAD_DIM + HEAD_DIM)
        out_t[rows, :] = out_t[rows, :] / total[head : head + 1, :]
    lse[...] = peak[...] + jnp.log(jnp.maximum(total[...], 1e-30))
    for block in range(half // 256):
        cols = slice(block * 256, block * 256 + 256)
        packed[cols, :] = out_t[0:128, cols].T.astype(b16)
    for block in range(half // 512):
        cols = slice(block * 256, block * 256 + 256)
        later = slice(half // 2 + block * 256, half // 2 + block * 256 + 256)
        both = jnp.concatenate([out_t[128:192, cols], out_t[128:192, later]], axis=0)
        packed[half + block * 256 : half + block * 256 + 256, :] = both.T.astype(b16)


def back_blocks(half, heads, scal, first_kb, last_kb, refs, finish):
    key, value, qm, dom, lse, row_dot, kt, query_t, key_sum, value_sum = refs
    bounds = edges(scal)

    @pl.loop(first_kb, last_kb)
    def _(kb):
        key_sum[...] = jnp.zeros_like(key_sum)
        value_sum[...] = jnp.zeros_like(value_sum)
        for block in range(half // QB):
            first = half + block * QB
            cols = slice(block * QB, block * QB + QB)
            low = doc_start(jnp.int32(first), bounds)

            @pl.when((kb * KB + KB > low) & (kb * KB < first + QB))
            def _():
                pos = first + lanes_like((1, QB))
                start = doc_start(pos, bounds)
                keys = key[ds(kb * KB, KB), :]
                values = value[ds(kb * KB, KB), :]
                key_pos = kb * KB + lax.broadcasted_iota(jnp.int32, (KB, 1), 0)
                allowed = (key_pos >= start) & (key_pos <= pos)
                for head in range(heads):
                    rows = slice(head * HEAD_DIM, head * HEAD_DIM + HEAD_DIM)
                    one = slice(head, head + 1)
                    own_q = qm[head, cols, :]
                    own_g = dom[head, cols, :]
                    scores = jnp.where(allowed, dot(keys, own_q, 1, 1) - lse[one, cols], masked_score)
                    weights = jnp.exp(scores)
                    grads = weights * (dot(values, own_g, 1, 1) - row_dot[one, cols])
                    grads = grads.astype(b16)
                    value_sum[...] += dot(weights.astype(b16), own_g)
                    key_sum[...] += dot(grads, own_q)
                    query_t[rows, cols] += dot(kt[rows, ds(kb * KB, KB)], grads)

        finish(kb, key_sum[...], value_sum[...])


def spread_groups(source, scal, keep, sent, cols=slice(None)):
    for rel_seq, out in enumerate((keep, sent)):
        for rel in range(out.shape[0]):
            out[rel, :, cols] = source[group_rows(out, rel, rel_seq, scal), :].astype(out.dtype)


def branch_body(quarter, heads, scal, *refs):
    branches = refs[:4]
    extra, out_t, dout, row_dot, keep, sent, proj_grad, turned = refs[4:]
    head = scal[0]
    width = heads * HEAD_DIM
    weights = jnp.concatenate([extra[quarter:, :], jnp.zeros((PADW - width, extra.shape[1]), b16)], axis=0)
    proj_grad[...] = jnp.zeros_like(proj_grad)
    row_dot[...] = jnp.zeros_like(row_dot)
    for rel, branch in enumerate(branches):
        base = (head ^ rel) * quarter
        grad = dot(branch[...], weights, 1, 1).astype(b16)
        dout[ds(base, quarter), :] = grad
        attended = out_t[:, ds(base, quarter)]
        product = grad.astype(f32).T[:width] * attended
        for one in range(heads):
            row_dot[one : one + 1, ds(base, quarter)] = jnp.sum(
                product[one * HEAD_DIM : one * HEAD_DIM + HEAD_DIM], axis=0, keepdims=True
            )
        proj_grad[...] += dot(attended.astype(b16), branch[...])
    turned[...] = proj_grad[...].T
    spread_groups(turned, scal, keep, sent)


def remote_back_body(half, heads, scal, *refs):
    query, key, value, dout, lse, row_dot = refs[:6]
    remote, query_t, kt = refs[6:9]
    qm, dom, key_sum, value_sum = refs[9:]
    width = heads * HEAD_DIM
    masked_queries(query, qm, heads)
    masked_queries(dout, dom, heads)

    @pl.loop(0, 2 * half // 256)
    def _(block):
        kt[:, ds(block * 256, 256)] = key[ds(block * 256, 256), :].astype(f32).T[:width].astype(b16)

    query_t[...] = jnp.zeros_like(query_t)

    def finish(kb, dk, dv):
        rows = ds(kb * KB, KB)
        remote[rows, 0:128] = dk[:, 0:128].astype(b16)
        remote[rows, 128:256] = dv[:, 0:128].astype(b16)
        remote[rows, 256:384] = (dk[:, 128:256] + half_roll(dv[:, 128:256])).astype(b16)

    back_blocks(
        half, heads, scal, 0, half // KB,
        (key, value, qm, dom, lse, row_dot, kt, query_t, key_sum, value_sum), finish,
    )


def local_back_body(half, heads, scal, *refs):
    query, key, value, dout, lse, row_dot, kt, query_in, taps = refs[:9]
    dq, dk_out, dv_out, front = refs[9:13]
    qm, dom, key_sum, value_sum, query_t = refs[13:]
    masked_queries(query, qm, heads)
    masked_queries(dout, dom, heads)
    query_t[...] = query_in[...]

    def finish(kb, dk, dv):
        rows = ds(kb * KB - half, KB)
        dk_out[rows, :] = dk.astype(b16)
        dv_out[rows, :] = dv.astype(b16)

    back_blocks(
        half, heads, scal, half // KB, 2 * half // KB,
        (key, value, qm, dom, lse, row_dot, kt, query_t, key_sum, value_sum), finish,
    )
    width = heads * HEAD_DIM
    scale = HEAD_DIM**-0.5
    for block in range(half // 256):
        cols = slice(block * 256, block * 256 + 256)
        turned = (query_t[:, cols] * scale).T
        dq[cols, 0:128] = turned[:, 0:128].astype(b16)
        dq[cols, 128:256] = jnp.concatenate(
            [turned[:, 128:width], jnp.zeros((256, PADW - width), f32)], axis=1
        ).astype(b16)
    bounds = edges(scal)
    pos = half + lax.broadcasted_iota(jnp.int32, (8, 1), 0)
    start = doc_start(pos, bounds)
    for part, grads in enumerate((dq, dk_out, dv_out)):
        cols = slice(part * PADW, part * PADW + PADW)
        rounded = grads[0:16, :].astype(b16).astype(f32)[0:8]
        result = jnp.zeros((8, PADW), f32)
        for back in range(1, KERNEL):
            moved = pltpu.roll(jnp.where(pos - back >= start, taps[4 + back : 5 + back, cols] * rounded, 0.0), 8 - back, 0)
            place = lax.broadcasted_iota(jnp.int32, (8, 1), 0)
            result = result + jnp.where(place >= 8 - back, moved, 0.0)
        front[:, cols] = result


def weights_body(scal, *refs):
    own, other, inner, outer = refs
    width = inner.shape[1]
    for rel_seq, stack in enumerate((own, other)):
        for rel in range(stack.shape[0]):
            rows = group_rows(stack, rel, rel_seq, scal)
            inner[rows, :] = stack[rel, :, :width]
            outer[rows, :] = stack[rel, :, width:]


def feed_body(half, quarter, scal, *refs):
    attended, extras, inputs = refs[0:4], refs[4:8], refs[8:10]
    inner, outer, norms = refs[10:13]
    normed, squared, inner_grad, keep, sent, middle_own = refs[13:]
    head = scal[0]
    for rel in range(4):
        base = (head ^ rel) * quarter
        late = base >= half // 2
        middle = inputs[rel % 2][rel // 2 * quarter : rel // 2 * quarter + quarter, :].astype(f32)
        for part in range(4):
            left = attended[part][ds(base, quarter), :]
            right = attended[part][ds(half + lax.rem(base, half // 2), quarter), :].astype(f32)
            right = jnp.where(late, half_roll(right), right).astype(b16)
            both = jnp.concatenate([left, right], axis=1)
            weights = extras[part][quarter:, :]
            middle = middle + dot(both[:, : weights.shape[0]], weights)
        if rel == 0:
            middle_own[...] = middle
        hat, _ = norm_rows(middle)
        rounded = (hat * norms[2:3, :] + norms[3:4, :]).astype(b16)
        rows = slice(rel * quarter, rel * quarter + quarter)
        normed[rows, :] = rounded
        positive = jnp.maximum(dot(rounded, inner[...]), 0.0)
        squared[rows, :] = (positive * positive).astype(b16)
        grads = (dot(extras[rel][0:quarter, :], outer[...]) * 2.0 * positive).astype(b16)
        inner_grad[rows, :] = grads
        part = dot(grads, inner[...], 1, 1)
        place = slice((rel // 2) * quarter, (rel // 2) * quarter + quarter)
        if rel % 2 == 0:
            keep[place, :] = part
        else:
            sent[place, :] = part.astype(b16)


def outer_grads_body(quarter, scal, *refs):
    extras, squared, total, cot = refs[0:4], refs[4], refs[5], refs[6]
    for rel in range(4):
        cot[rel * quarter : rel * quarter + quarter, :] = extras[rel][0:quarter, :]
    for tile in range(total.shape[0] // 256):
        cols = slice(tile * 256, tile * 256 + 256)
        total[cols, :] = dot(cot[:, cols], squared[...], 0, 0)


def feed_grads_body(quarter, scal, *refs):
    normed, squared, inner_grad, outer, outer_total = refs[:5]
    keep, sent, kept, away, total = refs[5:]
    width = total.shape[1]
    for rel in range(4):
        rows = slice(rel * quarter, rel * quarter + quarter)
        part = dot(squared[rows, :], outer[...], 1, 1)
        place = slice((rel // 2) * quarter, (rel // 2) * quarter + quarter)
        if rel % 2 == 0:
            keep[place, :] = part
        else:
            sent[place, :] = part.astype(b16)
    for tile in range(total.shape[0] // 256):
        cols = slice(tile * 256, tile * 256 + 256)
        total[cols, :] = dot(normed[:, cols], inner_grad[...], 0, 0)
    spread_groups(total, scal, kept, away, slice(0, width))
    spread_groups(outer_total, scal, kept, away, slice(width, 2 * width))


def norm_back_body(row, scal, part, got, values, skip, norms, grad_in, rounded, sums):
    del scal
    grad = part[...] + got[0 : part.shape[0], :].astype(f32)
    hat, inverse = norm_rows(values[...].astype(f32))
    scaled = grad * norms[row : row + 1, :]
    back = inverse * (
        scaled
        - jnp.mean(scaled, axis=-1, keepdims=True)
        - hat * jnp.mean(scaled * hat, axis=-1, keepdims=True)
    )
    result = skip[...].astype(f32) + back
    grad_in[...] = result
    rounded[...] = result.astype(b16)
    sums[...] = jnp.zeros_like(sums)
    sums[0:1, :] = jnp.sum(grad * hat, axis=0, keepdims=True)
    sums[1:2, :] = jnp.sum(grad, axis=0, keepdims=True)


def tail_body(half, quarter, scal, *refs):
    dq, dk, dv, remote, front, projected, normed, taps = refs[:8]
    proj_grad, w_keep, w_send, sums = refs[8:12]
    mixed, total, dense = refs[12:]
    bounds = edges(scal)
    low = lanes_like((quarter, 128)) < 64
    sums[...] = jnp.zeros_like(sums)
    for block in range(half // quarter):
        rows = slice(block * quarter, block * quarter + quarter)
        shared = remote[rows, 256:384].astype(f32)
        mixed[rows, 0:256] = dq[rows, :]
        mixed[rows, 256:384] = (dk[rows, 0:128].astype(f32) + remote[rows, 0:128].astype(f32)).astype(b16)
        mixed[rows, 384:512] = (dk[rows, 128:256].astype(f32) + jnp.where(low, shared, 0.0)).astype(b16)
        mixed[rows, 512:640] = (dv[rows, 0:128].astype(f32) + remote[rows, 128:256].astype(f32)).astype(b16)
        mixed[rows, 640:768] = (dv[rows, 128:256].astype(f32) + jnp.where(low, half_roll(shared), 0.0)).astype(b16)
    mixed[half : half + 16, :] = jnp.zeros((16, mixed.shape[1]), b16)

    @pl.loop(0, half // quarter)
    def _(block):
        base = block * quarter
        pos = half + base + lax.broadcasted_iota(jnp.int32, (quarter + 16, 1), 0)
        start = doc_start(pos, bounds)
        for part in range(3):
            cols = slice(part * PADW, part * PADW + PADW)
            grads = mixed[pl.ds(pl.multiple_of(base, 16), quarter + 16), cols].astype(f32)
            values = projected[pl.ds(pl.multiple_of(base, 16), quarter + 16), cols].astype(f32)
            here = grads[:quarter]
            result = taps[4:5, cols] * here
            sums[4:5, cols] += jnp.sum(here * values[16:], axis=0, keepdims=True)
            for back in range(1, KERNEL):
                same = pos - back >= start
                held = jnp.where(same, grads, 0.0)
                ahead = pltpu.roll(held, quarter + 16 - back, 0)[:quarter]
                result = result + taps[4 + back : 5 + back, cols] * ahead
                earlier = pltpu.roll(values, back, 0)[16:]
                sums[4 + back : 5 + back, cols] += jnp.sum(held[:quarter] * earlier, axis=0, keepdims=True)
            proj_grad[ds(base, quarter), cols] = result.astype(b16)

        @pl.when(block == half // quarter - 1)
        def _():
            added = jnp.concatenate([jnp.zeros((8, front.shape[1]), f32), front[...]], axis=0)
            tail_pos = 2 * half - 16 + lax.broadcasted_iota(jnp.int32, (32, 1), 0)
            tail_start = doc_start(tail_pos, bounds)
            grads = mixed[half - 16 : half + 16, :].astype(f32)
            result = taps[4:5, :] * grads[:16]
            for back in range(1, KERNEL):
                held = jnp.where(tail_pos - back >= tail_start, grads, 0.0)
                result = result + taps[4 + back : 5 + back, :] * pltpu.roll(held, 32 - back, 0)[:16]
            proj_grad[half - 16 : half, :] = (result + added).astype(b16)

    for tile in range(total.shape[0] // 256):
        rows = slice(tile * 256, tile * 256 + 256)
        total[rows, :] = dot(normed[:, rows], proj_grad[...], 0, 0)
        for part in range(3):
            dense[rows, part * 128 : part * 128 + 128] = total[rows, part * 256 : part * 256 + 128]
        dense[rows, 384:512] = total[rows, 128:256] + half_roll(total[rows, 384:512])
        dense[rows, 512:640] = total[rows, 640:768]
    spread_groups(dense, scal, w_keep, w_send)


def tail_norm_body(quarter, scal, proj_grad, wpad, form, second, keep, sent, sums):
    head = scal[0]
    sums[...] = jnp.zeros_like(sums)
    sums[2:4, :] = second[0:2, :]
    for rel in (1, 3, 0, 2):
        base = (head ^ rel) * quarter
        part = dot(proj_grad[ds(base, quarter), :], wpad[...], 1, 1)
        sums[0:1, :] += jnp.sum(part * form[ds(base, quarter), :].astype(f32), axis=0, keepdims=True)
        sums[1:2, :] += jnp.sum(part, axis=0, keepdims=True)
        place = slice((rel // 2) * quarter, (rel // 2) * quarter + quarter)
        if rel % 2 == 0:
            keep[place, :] = part
        else:
            sent[place, :] = part.astype(b16)
    keep[2 * quarter :, :] = sums[...]
    sent[2 * quarter :, :] = sums[...].astype(b16)


def pad_heads(values, width):
    shaped = values.reshape(values.shape[:-1] + (3, width))
    padded = jnp.pad(shaped, [(0, 0)] * (shaped.ndim - 1) + [(0, PADW - width)])
    return padded.reshape(values.shape[:-1] + (3 * PADW,))


def gather_small(norms, conv_kernel, model, width):
    norms = lax.all_gather(norms, ("batch", "seq"), axis=0, tiled=True).astype(f32).T
    taps = lax.all_gather(conv_kernel, ("batch", "seq"), axis=2, tiled=True).astype(f32)
    taps = taps.reshape(3, width, KERNEL).transpose(2, 0, 1).reshape(KERNEL, 3 * width)
    return jnp.pad(norms, ((0, 4), (0, 0))), jnp.pad(pad_heads(taps, width), ((4, 1), (0, 0)))


def on_device(
    block_input, segment_ids, norm1_gain, norm1_bias, qkv_weight, conv_kernel, out_weight,
    norm2_gain, norm2_bias, inner_weight, outer_weight, cotangent,
):
    quarter = block_input.shape[2]
    half = quarter * lax.axis_size("heads")
    width = qkv_weight.shape[2]
    heads = width // HEAD_DIM
    group = qkv_weight.shape[0]
    groups = lax.axis_size("batch") * lax.axis_size("seq")
    model = group * groups
    hidden = inner_weight.shape[1]
    head, batch, seq = lax.axis_index("heads"), lax.axis_index("batch"), lax.axis_index("seq")
    own = batch * 2 + seq
    stacks = (groups // 2, group) if pairwise(group) else (1, model // 2)

    ids = segment_ids.reshape(-1)
    docs = jnp.arange(DOCS, dtype=jnp.int32)
    firsts = jnp.sum((ids[None, :] < docs[:, None]).astype(jnp.int32), axis=1) - (seq - 1) * half
    scal = jnp.concatenate([jnp.stack([head, batch, seq]), firsts, jnp.zeros((1,), jnp.int32)]).astype(jnp.int32)

    x_own = block_input.reshape(quarter, model)
    cot_own = cotangent.reshape(quarter, model)

    share = conv_kernel.shape[2]

    paired = pairwise(group)
    qkv = qkv_weight
    small = [norm1_gain, norm1_bias, norm2_gain, norm2_bias]
    small_args = []
    if paired:
        (shard,) = call(
            functools.partial(shard_body, heads), [((group, 896), b16)],
            qkv.transpose(1, 0, 2), out_weight, jnp.stack(small), conv_kernel,
            scratch=[
                pltpu.VMEM((3, group, width), b16), pltpu.VMEM(out_weight.shape, b16), pltpu.VMEM((4, group), b16),
                pltpu.VMEM(conv_kernel.shape, b16), pltpu.VMEM((128, 128), f32), pltpu.SemaphoreType.DMA((4,)),
            ],
            limit=4, plain=True,
        )
    else:
        small_args = gather_small(jnp.stack(small, axis=1), conv_kernel, model, width)
        shard = jnp.concatenate(
            [qkv[:, 0, :128], qkv[:, 1, :128], qkv[:, 2, :128], qkv[:, 0, 128:], qkv[:, 1, 128:], qkv[:, 2, 128:],
             out_weight.T, jnp.zeros((group, 128), b16)], axis=1,
        )
    shards, first_shard = gather_batch_steps(shard)
    far_seq = [(2 * h + t, 2 * (h ^ 2) + (t ^ 1)) for h in range(lax.axis_size("heads")) for t in range(2)]
    x_other, x_far, x_far_other = after(
        (swap(x_own, "seq", 1), swap(x_own, "heads", 2), lax.ppermute(x_own, ("heads", "seq"), far_seq)), first_shard
    )
    x_pieces = gather_cores(x_own, x_far)
    y_pieces = gather_cores(x_other, x_far_other)
    hats, form_one = call(
        functools.partial(norm_body, half, quarter),
        [((2 * half, model), f32), ((half, model), b16)],
        scal, *x_pieces, *y_pieces, flops=2 * half * model, limit=8, away=(1,),
        scratch=[pltpu.VMEM((half, model), b16), pltpu.SemaphoreType.DMA],
    )
    w_own, w_other = gather_seq(shards)
    w_other = after(w_other, hats)

    feed_shards = gather_batch(after(jnp.concatenate([inner_weight, outer_weight.T], axis=1), shards))

    normed_one, projected, wpad, query, key, value, extra, norms, taps = call(
        functools.partial(front_body, half, quarter, heads, paired),
        [
            ((half, model), b16), ((half + 16, 3 * PADW), b16), ((model, 3 * PADW), b16),
            ((half, PADW), b16), ((2 * half, PADW), b16), ((2 * half, PADW), b16), ((quarter + width, model), b16),
            ((8, model), f32), ((8, 3 * PADW), f32),
        ],
        scal, hats, w_own, w_other, cot_own, *small_args,
        scratch=[
            pltpu.VMEM((2 * half + 16, 3 * PADW), b16),
            pltpu.VMEM((model, 128), f32), pltpu.VMEM((KERNEL * HEAD_DIM, 128), f32), pltpu.VMEM((model, PADW), f32),
            pltpu.VMEM((half, model), b16), pltpu.VMEM((model, 3 * PADW), b16), pltpu.SemaphoreType.DMA((3,)),
        ],
        flops=4 * half * model * 3 * width, limit=14, away=(0, 1, 2),
    )

    feed_own, feed_other = gather_seq(after(feed_shards, query))
    extra_pieces = gather_heads(extra)

    packed, out_t, lse = call(
        functools.partial(attention_body, half, heads),
        [((half + half // 2, 128), b16), ((width, half), f32), ((8, half), f32)],
        scal, query, key, value,
        scratch=[
            pltpu.VMEM((width, 2 * half), b16), pltpu.VMEM((heads, half, PADW), b16),
            pltpu.VMEM((8, half), f32), pltpu.VMEM((8, half), f32),
        ],
        flops=4 * half * half * width, limit=7,
    )
    packed_pieces = gather_heads(packed)
    feed_own, feed_other, _ = lax.optimization_barrier((feed_own, feed_other, packed))
    inner_full, outer_full = call(
        weights_body, [((model, hidden), b16), ((model, hidden), b16)], scal, feed_own, feed_other, limit=4,
    )

    normed_two, squared, inner_grad, keep, sent, middle_own = call(
        functools.partial(feed_body, half, quarter),
        [((half, model), b16), ((half, hidden), b16), ((half, hidden), b16),
         ((2 * quarter, model), f32), ((2 * quarter, model), b16), ((quarter, model), f32)],
        scal, *packed_pieces, *extra_pieces, *x_pieces, inner_full, outer_full, norms,
        flops=2 * half * model * (model + 3 * hidden), limit=12,
    )
    got = swap(sent, "heads", 1)
    (outer_total,) = call(
        functools.partial(outer_grads_body, quarter), [((model, hidden), f32)],
        scal, *extra_pieces, squared,
        scratch=[pltpu.VMEM((half, model), b16)], flops=2 * half * model * hidden, limit=8,
    )
    got = after(got, outer_total)
    dn_here, dn_far = scatter_far(keep, got, quarter)
    out_keep, out_sent, ff_keep, ff_send = call(
        functools.partial(feed_grads_body, quarter),
        [((2 * quarter, model), f32), ((2 * quarter, model), b16),
         (stacks + (2 * hidden,), b16), (stacks + (2 * hidden,), b16)],
        scal, after(normed_two, got), squared, inner_grad, outer_full, outer_total,
        scratch=[pltpu.VMEM((model, hidden), f32)],
        flops=4 * half * model * hidden, limit=8,
    )
    dn_far = after(dn_far, out_sent)
    ff_got = scatter_seq(ff_send)
    middle_grad, branch, sums_two = call(
        functools.partial(norm_back_body, 2),
        [((quarter, model), f32), ((quarter, model), b16), ((8, model), f32)],
        scal, dn_here, dn_far, middle_own, cot_own, norms, limit=6,
    )
    branch_pieces = gather_heads(branch)
    out_got = swap(after(out_sent, branch), "heads", 1)

    dout, row_dot, pj_keep, pj_send = call(
        functools.partial(branch_body, quarter, heads),
        [((half, PADW), b16), ((8, half), f32), (stacks + (width,), f32), (stacks + (width,), b16)],
        scal, *branch_pieces, extra, out_t,
        scratch=[pltpu.VMEM((width, model), f32), pltpu.VMEM((model, width), f32)],
        flops=4 * half * model * width, limit=6,
    )
    pj_got = scatter_seq(pj_send)
    out_here, out_far = scatter_far(out_keep, after(out_got, dout), quarter)
    remote, query_t, kt = call(
        functools.partial(remote_back_body, half, heads),
        [((half, 384), b16), ((width, half), f32), ((width, 2 * half), b16)],
        scal, query, key, value, dout, lse, row_dot,
        scratch=[
            pltpu.VMEM((heads, half, PADW), b16), pltpu.VMEM((heads, half, PADW), b16),
            pltpu.VMEM((KB, PADW), f32), pltpu.VMEM((KB, PADW), f32),
        ],
        flops=10 * half * half * width, limit=8,
    )
    remote_in = lax.ppermute(remote, "seq", [(1, 0)])
    ff_got, pj_got = after((ff_got, pj_got), remote)
    ff_own, ff_rest = join_seq((ff_keep, ff_got))

    dq, dk, dv, front = call(
        functools.partial(local_back_body, half, heads),
        [((half, PADW), b16), ((half, PADW), b16), ((half, PADW), b16), ((8, 3 * PADW), f32)],
        scal, query, key, value, dout, lse, row_dot, kt, after(query_t, ff_rest, pj_got), taps,
        scratch=[
            pltpu.VMEM((heads, half, PADW), b16), pltpu.VMEM((heads, half, PADW), b16),
            pltpu.VMEM((KB, PADW), f32), pltpu.VMEM((KB, PADW), f32), pltpu.VMEM((width, half), f32),
        ],
        flops=10 * half * half * width, limit=8,
    )
    front_in = lax.ppermute(front, "seq", [(1, 0)])
    remote_in = after(remote_in, dq)
    block_output = (middle_own + out_here + after(out_far, dq).astype(f32)).astype(b16)

    proj_grad, w_keep, w_send, sums_taps = call(
        functools.partial(tail_body, half, quarter),
        [((half, 3 * PADW), b16), (stacks + (640,), f32), (stacks + (640,), b16), ((8, 3 * PADW), f32)],
        scal, dq, dk, dv, remote_in, front_in, projected, normed_one, taps,
        scratch=[
            pltpu.VMEM((half + 16, 3 * PADW), b16), pltpu.VMEM((model, 3 * PADW), f32), pltpu.VMEM((model, 640), f32),
        ],
        flops=2 * half * model * 3 * width, limit=12,
    )
    w_got = scatter_seq(w_send)
    keep, sent, sums = call(
        functools.partial(tail_norm_body, quarter),
        [((2 * quarter + 8, model), f32), ((2 * quarter + 8, model), b16), ((8, model), f32)],
        scal, proj_grad, wpad, form_one, sums_two,
        flops=2 * half * model * 3 * width, limit=8,
    )
    got = swap(sent, "heads", 1)
    dn_here, dn_far = scatter_far(keep, got, quarter)
    small = sums + got[2 * quarter :].astype(f32)
    small = jnp.concatenate([small[0:4], sums_taps[4:8]])
    small = small + swap(small, "seq", 1)
    ff_out, _ = scatter_batch(ff_own, ff_rest, None, small)
    small = jnp.concatenate([small[0:4] + swap(small[0:4], "heads", 2), small[4:8]])
    qkv_own, qkv_rest = join_seq((w_keep[..., : 3 * width], after(w_got, small)[..., : 3 * width]), (pj_keep, pj_got))
    cut = small.shape[1] // 2
    small = jnp.concatenate([small[:, :cut], small[:, cut:]])
    input_grad, _, _ = call(
        functools.partial(norm_back_body, 0),
        [((quarter, model), f32), ((quarter, model), b16), ((8, model), f32)],
        scal, dn_here, dn_far, x_own, middle_grad, norms, limit=6,
    )
    qkv_out, small = scatter_batch(qkv_own, qkv_rest, small, input_grad)
    pj_out = qkv_out[:, 3 * width :]
    small = jnp.concatenate([small[:8], small[8:]], axis=1)

    qkv_out = jnp.stack(
        [
            jnp.concatenate([qkv_out[:, 0:128], qkv_out[:, 384:448]], axis=1),
            jnp.concatenate([qkv_out[:, 128:256], qkv_out[:, 448:512]], axis=1),
            jnp.concatenate([qkv_out[:, 256:384], qkv_out[:, 512:576]], axis=1),
        ],
        axis=1,
    )
    gains = lax.dynamic_slice_in_dim(small[0:4], own * group, group, 1)
    kernel_out = small[4 : 4 + KERNEL].reshape(KERNEL, 3, PADW)[:, :, :width].reshape(KERNEL, 3, heads, HEAD_DIM)
    kernel_out = kernel_out.transpose(1, 2, 3, 0).reshape(3, heads, HEAD_DIM * KERNEL)
    kernel_out = lax.dynamic_slice_in_dim(kernel_out, own * share, share, 2)
    return (
        block_output.reshape(block_input.shape),
        input_grad.reshape(block_input.shape),
        gains[0],
        gains[1],
        qkv_out,
        kernel_out,
        pj_out.T,
        gains[2],
        gains[3],
        ff_out[:, :hidden],
        ff_out[:, hidden : 2 * hidden].T,
    )


def solution(mesh):
    return jax.shard_map(
        on_device,
        mesh=mesh,
        in_specs=(
            P("batch", "seq", "heads", None),
            P("batch", None),
            P(("batch", "seq")),
            P(("batch", "seq")),
            P(("batch", "seq"), None, "heads"),
            P(None, "heads", ("batch", "seq")),
            P("heads", ("batch", "seq")),
            P(("batch", "seq")),
            P(("batch", "seq")),
            P(("batch", "seq"), "heads"),
            P("heads", ("batch", "seq")),
            P("batch", "seq", "heads", None),
        ),
        out_specs=(
            P("batch", "seq", "heads", None),
            P("batch", "seq", "heads", None),
            P(("batch", "seq")),
            P(("batch", "seq")),
            P(("batch", "seq"), None, "heads"),
            P(None, "heads", ("batch", "seq")),
            P("heads", ("batch", "seq")),
            P(("batch", "seq")),
            P(("batch", "seq")),
            P(("batch", "seq"), "heads"),
            P("heads", ("batch", "seq")),
        ),
        check_vma=False,
    )
```

```python
import functools

import jax
import jax.numpy as jnp
from jax import lax
from jax.experimental import pallas as pl
from jax.experimental.pallas import tpu as pltpu
from jax.sharding import PartitionSpec as P

HEAD_DIM = 64
KERNEL = 3
DOCS = 4
PADW = 256
QB = 512
QF = 256
KB = 256

epsilon = 1e-05
masked_score = -1e30
f32 = jnp.float32
b16 = jnp.bfloat16

VMEM = pl.BlockSpec(memory_space=pltpu.VMEM)
SMEM = pl.BlockSpec(memory_space=pltpu.SMEM)


def after(value, *others):
    return lax.optimization_barrier((value,) + others)[0]


def swap(shard, axis, by):
    return lax.ppermute(shard, axis, [(i, i ^ by) for i in range(lax.axis_size(axis))])


def gather_heads(shard):
    far = swap(shard, "heads", 2)
    near = swap(shard, "heads", 1)
    return [shard, near, far, swap(far, "heads", 1)]


def gather_cores(shard, far):
    both = jnp.concatenate([shard, far])
    return [both, swap(both, "heads", 1)]


def pairwise(group):
    return group % 32 == 0


def gather_batch(shard):
    if not pairwise(shard.shape[0]):
        return (shard,)
    return (shard,) + tuple(swap(shard, "batch", by) for by in range(1, lax.axis_size("batch")))


def gather_batch_steps(shard):
    if not pairwise(shard.shape[0]) or lax.axis_size("batch") != 4:
        shards = gather_batch(shard)
        return shards, shards[-1]
    far = swap(shard, "batch", 2)
    near = swap(jnp.concatenate([shard, far]), "batch", 1)
    rows = shard.shape[0]
    return (shard, near[:rows], far, near[rows:]), far


def gather_seq(shards):
    rows, columns = shards[0].shape
    if not pairwise(rows):
        whole = lax.all_gather(shards[0], ("batch", "seq"), axis=0, tiled=True)
        return tuple(whole.reshape(2, 1, -1, columns))
    stack = jnp.stack(shards)
    return stack, swap(stack, "seq", 1)


def scatter_seq(sent):
    return sent if sent.shape[0] == 1 else swap(sent, "seq", 1)


def join_seq(*parts):
    if parts[0][0].shape[0] == 1:
        whole = [jnp.concatenate([keep[0].astype(b16), sent[0]]) for keep, sent in parts]
        return None, jnp.concatenate(whole, axis=-1)
    total = jnp.concatenate([keep.astype(f32) + got.astype(f32) for keep, got in parts], axis=-1)
    return total[0], total[1:].astype(b16)


def scatter_batch(own, rest, more, *others):
    if own is None:
        total = lax.psum_scatter(rest, ("batch", "seq"), scatter_dimension=0, tiled=True).astype(f32)
        return total, None if more is None else lax.psum(more, "batch")
    count = own.shape[0]
    payloads = [rest[by] for by in range(rest.shape[0])]
    if more is not None:
        tail = jnp.pad(more, ((0, 0), (0, own.shape[1] - more.shape[1]))).astype(b16)
        payloads = [jnp.concatenate([payload, tail]) for payload in payloads]
    pieces = [swap(payload, "batch", by + 1) for by, payload in enumerate(payloads)]
    for piece in after(pieces, *others) if others else pieces:
        own = own + piece[:count].astype(f32)
        if more is not None:
            more = more + piece[count:, : more.shape[1]].astype(f32)
    return own, more


def scatter_far(keep, got, rows):
    far = (keep[rows : 2 * rows].astype(f32) + got[rows : 2 * rows].astype(f32)).astype(b16)
    here = keep[:rows].astype(f32) + got[:rows].astype(f32)
    return here, swap(far, "heads", 2)


def call(body, outs, *args, scratch=(), flops=0, limit=16, plain=False):
    in_specs = [pl.BlockSpec(memory_space=pl.ANY)] * len(args) if plain else [SMEM] + [VMEM] * (len(args) - 1)
    return pl.pallas_call(
        body,
        out_shape=[jax.ShapeDtypeStruct(*o) for o in outs],
        in_specs=in_specs,
        out_specs=[VMEM] * len(outs),
        scratch_shapes=list(scratch),
        compiler_params=pltpu.CompilerParams(vmem_limit_bytes=limit << 20),
        cost_estimate=pl.CostEstimate(flops=flops // 16, transcendentals=0, bytes_accessed=0),
    )(*args)


def dot(a, b, ca=1, cb=0):
    return lax.dot_general(a, b, (((ca,), (cb,)), ((), ())), preferred_element_type=f32)


def edges(scal):
    return [scal[3 + d] for d in range(DOCS)]


def doc_start(pos, bounds):
    start = bounds[0] + jnp.zeros_like(pos)
    for edge in bounds[1:]:
        start = jnp.where(pos >= edge, edge, start)
    return start


def lanes_like(shape):
    return lax.broadcasted_iota(jnp.int32, shape, 1)


def half_roll(block):
    return pltpu.roll(block, 64, 1)


def norm_rows(values):
    average = jnp.mean(values, axis=-1, keepdims=True)
    centered = values - average
    inverse = lax.rsqrt(jnp.mean(centered * centered, axis=-1, keepdims=True) + epsilon)
    return centered * inverse, inverse


def group_rows(stack, rel, rel_seq, scal):
    return some_rows(stack.shape[1], stack.shape[0] > 1, rel, rel_seq, scal)


def some_rows(count, paired, rel, rel_seq, scal):
    if not paired:
        return slice(rel_seq * count, rel_seq * count + count)
    return pl.ds(pl.multiple_of(((scal[1] ^ rel) * 2 + (scal[2] ^ rel_seq)) * count, 32), count)


def ds(start, size):
    return pl.ds(pl.multiple_of(start, size), size)


def shard_body(heads, *refs):
    sources, shard, (qkv, out_w, small, kernel), rows, sems = refs[:4], refs[4], refs[5:9], refs[9], refs[10]
    copies = [
        pltpu.make_async_copy(source, target, sems.at[index])
        for index, (source, target) in enumerate(zip(sources, (qkv, out_w, small, kernel)))
    ]
    for copy in copies:
        copy.start()
    for copy in copies:
        copy.wait()
    for part in range(3):
        shard[:, part * 128 : part * 128 + 128] = qkv[part, :, 0:128]
    thirds = [qkv[part, :, 128:192].astype(f32) for part in range(3)]
    turned = out_w[...].astype(f32).T
    shard[:, 384:512] = jnp.concatenate(thirds[:2], axis=1).astype(b16)
    shard[:, 512:640] = jnp.concatenate([thirds[2], turned[:, 0:64]], axis=1).astype(b16)
    shard[:, 640:768] = turned[:, 64:192].astype(b16)
    rows[...] = jnp.zeros_like(rows)
    count = kernel.shape[2]
    rows[0:4, 0 : small.shape[1]] = small[...].astype(f32)
    for part in range(3):
        rows[4 + part * heads : 4 + part * heads + heads, 0:count] = kernel[part].astype(f32)
    shard[:, 768:896] = rows[...].T[: shard.shape[0]].astype(b16)


def small_rows(scal, stacks, heads, norms, taps, columns, features):
    count = features.shape[0] // (2 * stacks[0].shape[0])
    for rel_seq, stack in enumerate(stacks):
        for rel in range(stack.shape[0]):
            block = stack[rel, :, 768:896].astype(f32)
            columns[group_rows(stack, rel, rel_seq, scal), :] = block
            group = (scal[1] ^ rel) * 2 + (scal[2] ^ rel_seq)
            features[pl.ds(pl.multiple_of(group * count, 8), count), :] = block[0:count]
    norms[...] = columns[...].T[0:8]
    taps[...] = jnp.zeros_like(taps)
    low = lanes_like((1, 128)) < 64
    for tap in range(KERNEL):
        turned = features[pl.ds(tap, HEAD_DIM, stride=KERNEL), :].T
        turned = jnp.concatenate([turned, jnp.zeros_like(turned)], axis=1)
        for part in range(3):
            one, two, three = (turned[4 + part * heads + i : 5 + part * heads + i] for i in range(3))
            taps[4 + tap : 5 + tap, part * PADW : part * PADW + 128] = jnp.where(low, one, half_roll(two))
            taps[4 + tap : 5 + tap, part * PADW + 128 : part * PADW + 256] = jnp.where(low, three, 0.0)


def norm_body(half, quarter, scal, *refs):
    pieces, hats, form = refs[:4], refs[4], refs[5]
    head = scal[0]
    for side in range(2):
        for rel in range(4):
            base = (head ^ rel) * quarter
            piece = pieces[2 * side + rel % 2]
            hat, _ = norm_rows(piece[rel // 2 * quarter : rel // 2 * quarter + quarter, :].astype(f32))
            if side == 0:
                hats[ds(half + base, quarter), :] = hat
                form[ds(base, quarter), :] = hat.astype(b16)
            else:
                hats[ds(base, quarter), :] = hat


def front_body(half, quarter, heads, paired, scal, *refs):
    hats, w_own, w_other, cot = refs[:4]
    refs = refs[1:]
    refs = refs[3:]
    if not paired:
        norms_in, taps_in, refs = refs[0], refs[1], refs[2:]
    normed, projected, wpad, query, key, value, extra, norms, taps = refs[:9]
    proj, columns, features, wo = refs[9:]
    if paired:
        small_rows(scal, (w_own, w_other), heads, norms, taps, columns, features)
    else:
        norms[...] = norms_in[...]
        taps[...] = taps_in[...]
    gain, bias = norms[0:1, :], norms[1:2, :]
    low = lanes_like((w_own.shape[1], 128)) < 64
    for rel_seq, stack in enumerate((w_own, w_other)):
        for rel in range(stack.shape[0]):
            rows = group_rows(stack, rel, rel_seq, scal)
            for part in range(3):
                wpad[rows, part * 256 : part * 256 + 128] = stack[rel, :, part * 128 : part * 128 + 128]
            shared = stack[rel, :, 384:512].astype(f32)
            wpad[rows, 128:256] = jnp.where(low, shared, 0.0).astype(b16)
            wpad[rows, 384:512] = jnp.where(low, half_roll(shared), 0.0).astype(b16)
            mid = stack[rel, :, 512:640].astype(f32)
            last = half_roll(stack[rel, :, 640:768].astype(f32))
            wpad[rows, 640:768] = jnp.where(low, mid, 0.0).astype(b16)
            wo[rows, 0:128] = jnp.where(low, half_roll(mid), last)
            wo[rows, 128:256] = last
    extra[0:quarter, :] = cot[...]
    width = heads * HEAD_DIM
    extra[quarter : quarter + width, :] = wo[...].T[0:width].astype(b16)
    proj[0:16, :] = jnp.zeros((16, proj.shape[1]), b16)

    def project(block, own):
        base = block * quarter
        rounded = (hats[ds(base, quarter), :] * gain + bias).astype(b16)
        proj[pl.ds(pl.multiple_of(base + 16, 16), quarter), :] = dot(rounded, wpad[...]).astype(b16)
        if own:
            rows = ds(base - half, quarter)
            normed[rows, :] = rounded

    @pl.loop(0, 4)
    def _(block):
        project(block, False)

    @pl.loop(4, 8)
    def _(block):
        project(block, True)

    projected[...] = proj[half : 2 * half + 16, :]
    bounds = edges(scal)

    def convolve(block, own):
        base = block * quarter
        pos = base + lax.broadcasted_iota(jnp.int32, (quarter, 1), 0)
        start = doc_start(pos, bounds)
        for part, out in enumerate((query, key, value)):
            if part == 0 and not own:
                continue
            cols = slice(part * PADW, part * PADW + PADW)
            rows = proj[pl.ds(pl.multiple_of(base, 16), quarter + 16), cols].astype(f32)
            mixed = taps[4:5, cols] * rows[16:]
            for back in range(1, KERNEL):
                earlier = pltpu.roll(rows, back, 0)[16:]
                mixed = mixed + jnp.where(pos - back >= start, taps[4 + back : 5 + back, cols] * earlier, 0.0)
            mixed = mixed.astype(b16)
            if part == 0:
                out[ds(base - half, quarter), :] = mixed * jnp.asarray(HEAD_DIM**-0.5, b16)
            else:
                out[ds(base, quarter), :] = mixed

    @pl.loop(0, 4)
    def _(block):
        convolve(block, False)

    @pl.loop(4, 8)
    def _(block):
        convolve(block, True)


def masked_queries(query, slots, heads):
    lane = lanes_like(query.shape) // HEAD_DIM
    for head in range(heads):
        slots[head] = jnp.where(lane == head, query[...], jnp.zeros((), b16))


def attention_body(half, heads, scal, query, key, value, packed, out_t, lse, vt, qm, peak, total):
    bounds = edges(scal)
    masked_queries(query, qm, heads)

    @pl.loop(0, 2 * half // 256)
    def _(block):
        turned = value[ds(block * 256, 256), :].astype(f32).T
        vt[:, ds(block * 256, 256)] = turned[: heads * HEAD_DIM].astype(b16)

    out_t[...] = jnp.zeros_like(out_t)
    peak[...] = jnp.full_like(peak, masked_score)
    total[...] = jnp.zeros_like(total)
    for block in range(half // QF):
        first = half + block * QF
        cols = slice(block * QF, block * QF + QF)
        pos = first + lanes_like((1, QF))
        start = doc_start(pos, bounds)
        low = doc_start(jnp.int32(first), bounds) // KB

        @pl.loop(low, (first + QF) // KB)
        def _(kb):
            keys = key[ds(kb * KB, KB), :]
            key_pos = kb * KB + lax.broadcasted_iota(jnp.int32, (KB, 1), 0)
            allowed = (key_pos >= start) & (key_pos <= pos)
            for head in range(heads):
                rows = slice(head * HEAD_DIM, head * HEAD_DIM + HEAD_DIM)
                one = slice(head, head + 1)
                scores = dot(keys, qm[head, cols, :], 1, 1)
                scores = jnp.where(allowed, scores, masked_score)
                old = peak[one, cols]
                new = jnp.maximum(old, jnp.max(scores, axis=0, keepdims=True))
                weights = jnp.exp(scores - new)
                shrink = jnp.exp(old - new)
                peak[one, cols] = new
                total[one, cols] = shrink * total[one, cols] + jnp.sum(weights, axis=0, keepdims=True)
                out_t[rows, cols] = shrink * out_t[rows, cols] + dot(
                    vt[rows, ds(kb * KB, KB)], weights.astype(b16)
                )

    for head in range(heads):
        rows = slice(head * HEAD_DIM, head * HEAD_DIM + HEAD_DIM)
        out_t[rows, :] = out_t[rows, :] / total[head : head + 1, :]
    lse[...] = peak[...] + jnp.log(jnp.maximum(total[...], 1e-30))
    for block in range(half // 256):
        cols = slice(block * 256, block * 256 + 256)
        packed[cols, :] = out_t[0:128, cols].T.astype(b16)
    for block in range(half // 512):
        cols = slice(block * 256, block * 256 + 256)
        later = slice(half // 2 + block * 256, half // 2 + block * 256 + 256)
        both = jnp.concatenate([out_t[128:192, cols], out_t[128:192, later]], axis=0)
        packed[half + block * 256 : half + block * 256 + 256, :] = both.T.astype(b16)


def back_blocks(half, heads, scal, first_kb, last_kb, refs, finish):
    key, value, qm, dom, lse, row_dot, kt, query_t, key_sum, value_sum = refs
    bounds = edges(scal)

    @pl.loop(first_kb, last_kb)
    def _(kb):
        key_sum[...] = jnp.zeros_like(key_sum)
        value_sum[...] = jnp.zeros_like(value_sum)
        for block in range(half // QB):
            first = half + block * QB
            cols = slice(block * QB, block * QB + QB)
            low = doc_start(jnp.int32(first), bounds)

            @pl.when((kb * KB + KB > low) & (kb * KB < first + QB))
            def _():
                pos = first + lanes_like((1, QB))
                start = doc_start(pos, bounds)
                keys = key[ds(kb * KB, KB), :]
                values = value[ds(kb * KB, KB), :]
                key_pos = kb * KB + lax.broadcasted_iota(jnp.int32, (KB, 1), 0)
                allowed = (key_pos >= start) & (key_pos <= pos)
                for head in range(heads):
                    rows = slice(head * HEAD_DIM, head * HEAD_DIM + HEAD_DIM)
                    one = slice(head, head + 1)
                    own_q = qm[head, cols, :]
                    own_g = dom[head, cols, :]
                    scores = jnp.where(allowed, dot(keys, own_q, 1, 1) - lse[one, cols], masked_score)
                    weights = jnp.exp(scores)
                    grads = weights * (dot(values, own_g, 1, 1) - row_dot[one, cols])
                    grads = grads.astype(b16)
                    value_sum[...] += dot(weights.astype(b16), own_g)
                    key_sum[...] += dot(grads, own_q)
                    query_t[rows, cols] += dot(kt[rows, ds(kb * KB, KB)], grads)

        finish(kb, key_sum[...], value_sum[...])


def spread_groups(source, scal, keep, sent, cols=slice(None)):
    for rel_seq, out in enumerate((keep, sent)):
        for rel in range(out.shape[0]):
            out[rel, :, cols] = source[group_rows(out, rel, rel_seq, scal), :].astype(out.dtype)


def branch_body(quarter, heads, scal, *refs):
    branches = refs[:4]
    extra, out_t, dout, row_dot, keep, sent, proj_grad, turned = refs[4:]
    head = scal[0]
    width = heads * HEAD_DIM
    weights = jnp.concatenate([extra[quarter:, :], jnp.zeros((PADW - width, extra.shape[1]), b16)], axis=0)
    proj_grad[...] = jnp.zeros_like(proj_grad)
    row_dot[...] = jnp.zeros_like(row_dot)
    for rel, branch in enumerate(branches):
        base = (head ^ rel) * quarter
        grad = dot(branch[...], weights, 1, 1).astype(b16)
        dout[ds(base, quarter), :] = grad
        attended = out_t[:, ds(base, quarter)]
        product = grad.astype(f32).T[:width] * attended
        for one in range(heads):
            row_dot[one : one + 1, ds(base, quarter)] = jnp.sum(
                product[one * HEAD_DIM : one * HEAD_DIM + HEAD_DIM], axis=0, keepdims=True
            )
        proj_grad[...] += dot(attended.astype(b16), branch[...])
    turned[...] = proj_grad[...].T
    spread_groups(turned, scal, keep, sent)


def remote_back_body(half, heads, scal, *refs):
    query, key, value, dout, lse, row_dot = refs[:6]
    remote, query_t, kt = refs[6:9]
    qm, dom, key_sum, value_sum = refs[9:]
    width = heads * HEAD_DIM
    masked_queries(query, qm, heads)
    masked_queries(dout, dom, heads)

    @pl.loop(0, 2 * half // 256)
    def _(block):
        kt[:, ds(block * 256, 256)] = key[ds(block * 256, 256), :].astype(f32).T[:width].astype(b16)

    query_t[...] = jnp.zeros_like(query_t)

    def finish(kb, dk, dv):
        rows = ds(kb * KB, KB)
        remote[rows, 0:128] = dk[:, 0:128].astype(b16)
        remote[rows, 128:256] = dv[:, 0:128].astype(b16)
        remote[rows, 256:384] = (dk[:, 128:256] + half_roll(dv[:, 128:256])).astype(b16)

    back_blocks(
        half, heads, scal, 0, half // KB,
        (key, value, qm, dom, lse, row_dot, kt, query_t, key_sum, value_sum), finish,
    )


def local_back_body(half, heads, scal, *refs):
    query, key, value, dout, lse, row_dot, kt, query_in, taps = refs[:9]
    dq, dk_out, dv_out, front = refs[9:13]
    qm, dom, key_sum, value_sum, query_t = refs[13:]
    masked_queries(query, qm, heads)
    masked_queries(dout, dom, heads)
    query_t[...] = query_in[...]

    def finish(kb, dk, dv):
        rows = ds(kb * KB - half, KB)
        dk_out[rows, :] = dk.astype(b16)
        dv_out[rows, :] = dv.astype(b16)

    back_blocks(
        half, heads, scal, half // KB, 2 * half // KB,
        (key, value, qm, dom, lse, row_dot, kt, query_t, key_sum, value_sum), finish,
    )
    width = heads * HEAD_DIM
    scale = HEAD_DIM**-0.5
    for block in range(half // 256):
        cols = slice(block * 256, block * 256 + 256)
        turned = (query_t[:, cols] * scale).T
        dq[cols, 0:128] = turned[:, 0:128].astype(b16)
        dq[cols, 128:256] = jnp.concatenate(
            [turned[:, 128:width], jnp.zeros((256, PADW - width), f32)], axis=1
        ).astype(b16)
    bounds = edges(scal)
    pos = half + lax.broadcasted_iota(jnp.int32, (8, 1), 0)
    start = doc_start(pos, bounds)
    for part, grads in enumerate((dq, dk_out, dv_out)):
        cols = slice(part * PADW, part * PADW + PADW)
        rounded = grads[0:16, :].astype(b16).astype(f32)[0:8]
        result = jnp.zeros((8, PADW), f32)
        for back in range(1, KERNEL):
            moved = pltpu.roll(jnp.where(pos - back >= start, taps[4 + back : 5 + back, cols] * rounded, 0.0), 8 - back, 0)
            place = lax.broadcasted_iota(jnp.int32, (8, 1), 0)
            result = result + jnp.where(place >= 8 - back, moved, 0.0)
        front[:, cols] = result


def weights_body(scal, *refs):
    own, other, inner, outer = refs
    width = inner.shape[1]
    for rel_seq, stack in enumerate((own, other)):
        for rel in range(stack.shape[0]):
            rows = group_rows(stack, rel, rel_seq, scal)
            inner[rows, :] = stack[rel, :, :width]
            outer[rows, :] = stack[rel, :, width:]


def feed_body(half, quarter, scal, *refs):
    attended, extras, inputs = refs[0:4], refs[4:8], refs[8:10]
    inner, outer, norms = refs[10:13]
    normed, squared, inner_grad, keep, sent, middle_own = refs[13:]
    head = scal[0]
    for rel in range(4):
        base = (head ^ rel) * quarter
        late = base >= half // 2
        middle = inputs[rel % 2][rel // 2 * quarter : rel // 2 * quarter + quarter, :].astype(f32)
        for part in range(4):
            left = attended[part][ds(base, quarter), :]
            right = attended[part][ds(half + lax.rem(base, half // 2), quarter), :].astype(f32)
            right = jnp.where(late, half_roll(right), right).astype(b16)
            both = jnp.concatenate([left, right], axis=1)
            weights = extras[part][quarter:, :]
            middle = middle + dot(both[:, : weights.shape[0]], weights)
        if rel == 0:
            middle_own[...] = middle
        hat, _ = norm_rows(middle)
        rounded = (hat * norms[2:3, :] + norms[3:4, :]).astype(b16)
        rows = slice(rel * quarter, rel * quarter + quarter)
        normed[rows, :] = rounded
        positive = jnp.maximum(dot(rounded, inner[...]), 0.0)
        squared[rows, :] = (positive * positive).astype(b16)
        grads = (dot(extras[rel][0:quarter, :], outer[...]) * 2.0 * positive).astype(b16)
        inner_grad[rows, :] = grads
        part = dot(grads, inner[...], 1, 1)
        place = slice((rel // 2) * quarter, (rel // 2) * quarter + quarter)
        if rel % 2 == 0:
            keep[place, :] = part
        else:
            sent[place, :] = part.astype(b16)


def outer_grads_body(quarter, scal, *refs):
    extras, squared, total, cot = refs[0:4], refs[4], refs[5], refs[6]
    for rel in range(4):
        cot[rel * quarter : rel * quarter + quarter, :] = extras[rel][0:quarter, :]
    for tile in range(total.shape[0] // 256):
        cols = slice(tile * 256, tile * 256 + 256)
        total[cols, :] = dot(cot[:, cols], squared[...], 0, 0)


def feed_grads_body(quarter, scal, *refs):
    normed, squared, inner_grad, outer, outer_total = refs[:5]
    keep, sent, kept, away, total = refs[5:]
    width = total.shape[1]
    for rel in range(4):
        rows = slice(rel * quarter, rel * quarter + quarter)
        part = dot(squared[rows, :], outer[...], 1, 1)
        place = slice((rel // 2) * quarter, (rel // 2) * quarter + quarter)
        if rel % 2 == 0:
            keep[place, :] = part
        else:
            sent[place, :] = part.astype(b16)
    for tile in range(total.shape[0] // 256):
        cols = slice(tile * 256, tile * 256 + 256)
        total[cols, :] = dot(normed[:, cols], inner_grad[...], 0, 0)
    spread_groups(total, scal, kept, away, slice(0, width))
    spread_groups(outer_total, scal, kept, away, slice(width, 2 * width))


def norm_back_body(row, scal, part, got, values, skip, norms, grad_in, rounded, sums):
    del scal
    grad = part[...] + got[0 : part.shape[0], :].astype(f32)
    hat, inverse = norm_rows(values[...].astype(f32))
    scaled = grad * norms[row : row + 1, :]
    back = inverse * (
        scaled
        - jnp.mean(scaled, axis=-1, keepdims=True)
        - hat * jnp.mean(scaled * hat, axis=-1, keepdims=True)
    )
    result = skip[...].astype(f32) + back
    grad_in[...] = result
    rounded[...] = result.astype(b16)
    sums[...] = jnp.zeros_like(sums)
    sums[0:1, :] = jnp.sum(grad * hat, axis=0, keepdims=True)
    sums[1:2, :] = jnp.sum(grad, axis=0, keepdims=True)


def tail_body(half, quarter, scal, *refs):
    dq, dk, dv, remote, front, projected, normed, taps = refs[:8]
    proj_grad, w_keep, w_send, sums = refs[8:12]
    mixed, total, dense = refs[12:]
    bounds = edges(scal)
    low = lanes_like((quarter, 128)) < 64
    sums[...] = jnp.zeros_like(sums)
    for block in range(half // quarter):
        rows = slice(block * quarter, block * quarter + quarter)
        shared = remote[rows, 256:384].astype(f32)
        mixed[rows, 0:256] = dq[rows, :]
        mixed[rows, 256:384] = (dk[rows, 0:128].astype(f32) + remote[rows, 0:128].astype(f32)).astype(b16)
        mixed[rows, 384:512] = (dk[rows, 128:256].astype(f32) + jnp.where(low, shared, 0.0)).astype(b16)
        mixed[rows, 512:640] = (dv[rows, 0:128].astype(f32) + remote[rows, 128:256].astype(f32)).astype(b16)
        mixed[rows, 640:768] = (dv[rows, 128:256].astype(f32) + jnp.where(low, half_roll(shared), 0.0)).astype(b16)
    mixed[half : half + 16, :] = jnp.zeros((16, mixed.shape[1]), b16)

    @pl.loop(0, half // quarter)
    def _(block):
        base = block * quarter
        pos = half + base + lax.broadcasted_iota(jnp.int32, (quarter + 16, 1), 0)
        start = doc_start(pos, bounds)
        for part in range(3):
            cols = slice(part * PADW, part * PADW + PADW)
            grads = mixed[pl.ds(pl.multiple_of(base, 16), quarter + 16), cols].astype(f32)
            values = projected[pl.ds(pl.multiple_of(base, 16), quarter + 16), cols].astype(f32)
            here = grads[:quarter]
            result = taps[4:5, cols] * here
            sums[4:5, cols] += jnp.sum(here * values[16:], axis=0, keepdims=True)
            for back in range(1, KERNEL):
                same = pos - back >= start
                held = jnp.where(same, grads, 0.0)
                ahead = pltpu.roll(held, quarter + 16 - back, 0)[:quarter]
                result = result + taps[4 + back : 5 + back, cols] * ahead
                earlier = pltpu.roll(values, back, 0)[16:]
                sums[4 + back : 5 + back, cols] += jnp.sum(held[:quarter] * earlier, axis=0, keepdims=True)
            proj_grad[ds(base, quarter), cols] = result.astype(b16)

        @pl.when(block == half // quarter - 1)
        def _():
            added = jnp.concatenate([jnp.zeros((8, front.shape[1]), f32), front[...]], axis=0)
            tail_pos = 2 * half - 16 + lax.broadcasted_iota(jnp.int32, (32, 1), 0)
            tail_start = doc_start(tail_pos, bounds)
            grads = mixed[half - 16 : half + 16, :].astype(f32)
            result = taps[4:5, :] * grads[:16]
            for back in range(1, KERNEL):
                held = jnp.where(tail_pos - back >= tail_start, grads, 0.0)
                result = result + taps[4 + back : 5 + back, :] * pltpu.roll(held, 32 - back, 0)[:16]
            proj_grad[half - 16 : half, :] = (result + added).astype(b16)

    for tile in range(total.shape[0] // 256):
        rows = slice(tile * 256, tile * 256 + 256)
        total[rows, :] = dot(normed[:, rows], proj_grad[...], 0, 0)
        for part in range(3):
            dense[rows, part * 128 : part * 128 + 128] = total[rows, part * 256 : part * 256 + 128]
        dense[rows, 384:512] = total[rows, 128:256] + half_roll(total[rows, 384:512])
        dense[rows, 512:640] = total[rows, 640:768]
    spread_groups(dense, scal, w_keep, w_send)


def tail_norm_body(quarter, scal, proj_grad, wpad, form, second, keep, sent, sums):
    head = scal[0]
    sums[...] = jnp.zeros_like(sums)
    sums[2:4, :] = second[0:2, :]
    for rel in (1, 3, 0, 2):
        base = (head ^ rel) * quarter
        part = dot(proj_grad[ds(base, quarter), :], wpad[...], 1, 1)
        sums[0:1, :] += jnp.sum(part * form[ds(base, quarter), :].astype(f32), axis=0, keepdims=True)
        sums[1:2, :] += jnp.sum(part, axis=0, keepdims=True)
        place = slice((rel // 2) * quarter, (rel // 2) * quarter + quarter)
        if rel % 2 == 0:
            keep[place, :] = part
        else:
            sent[place, :] = part.astype(b16)
    keep[2 * quarter :, :] = sums[...]
    sent[2 * quarter :, :] = sums[...].astype(b16)


def pad_heads(values, width):
    shaped = values.reshape(values.shape[:-1] + (3, width))
    padded = jnp.pad(shaped, [(0, 0)] * (shaped.ndim - 1) + [(0, PADW - width)])
    return padded.reshape(values.shape[:-1] + (3 * PADW,))


def gather_small(norms, conv_kernel, model, width):
    norms = lax.all_gather(norms, ("batch", "seq"), axis=0, tiled=True).astype(f32).T
    taps = lax.all_gather(conv_kernel, ("batch", "seq"), axis=2, tiled=True).astype(f32)
    taps = taps.reshape(3, width, KERNEL).transpose(2, 0, 1).reshape(KERNEL, 3 * width)
    return jnp.pad(norms, ((0, 4), (0, 0))), jnp.pad(pad_heads(taps, width), ((4, 1), (0, 0)))


def on_device(
    block_input, segment_ids, norm1_gain, norm1_bias, qkv_weight, conv_kernel, out_weight,
    norm2_gain, norm2_bias, inner_weight, outer_weight, cotangent,
):
    quarter = block_input.shape[2]
    half = quarter * lax.axis_size("heads")
    width = qkv_weight.shape[2]
    heads = width // HEAD_DIM
    group = qkv_weight.shape[0]
    groups = lax.axis_size("batch") * lax.axis_size("seq")
    model = group * groups
    hidden = inner_weight.shape[1]
    head, batch, seq = lax.axis_index("heads"), lax.axis_index("batch"), lax.axis_index("seq")
    own = batch * 2 + seq
    stacks = (groups // 2, group) if pairwise(group) else (1, model // 2)

    ids = segment_ids.reshape(-1)
    docs = jnp.arange(DOCS, dtype=jnp.int32)
    firsts = jnp.sum((ids[None, :] < docs[:, None]).astype(jnp.int32), axis=1) - (seq - 1) * half
    scal = jnp.concatenate([jnp.stack([head, batch, seq]), firsts, jnp.zeros((1,), jnp.int32)]).astype(jnp.int32)

    x_own = block_input.reshape(quarter, model)
    cot_own = cotangent.reshape(quarter, model)

    share = conv_kernel.shape[2]

    paired = pairwise(group)
    qkv = qkv_weight
    small = [norm1_gain, norm1_bias, norm2_gain, norm2_bias]
    small_args = []
    if paired:
        (shard,) = call(
            functools.partial(shard_body, heads), [((group, 896), b16)],
            qkv.transpose(1, 0, 2), out_weight, jnp.stack(small), conv_kernel,
            scratch=[
                pltpu.VMEM((3, group, width), b16), pltpu.VMEM(out_weight.shape, b16), pltpu.VMEM((4, group), b16),
                pltpu.VMEM(conv_kernel.shape, b16), pltpu.VMEM((128, 128), f32), pltpu.SemaphoreType.DMA((4,)),
            ],
            limit=4, plain=True,
        )
    else:
        small_args = gather_small(jnp.stack(small, axis=1), conv_kernel, model, width)
        shard = jnp.concatenate(
            [qkv[:, 0, :128], qkv[:, 1, :128], qkv[:, 2, :128], qkv[:, 0, 128:], qkv[:, 1, 128:], qkv[:, 2, 128:],
             out_weight.T, jnp.zeros((group, 128), b16)], axis=1,
        )
    shards, first_shard = gather_batch_steps(shard)
    far_seq = [(2 * h + t, 2 * (h ^ 2) + (t ^ 1)) for h in range(lax.axis_size("heads")) for t in range(2)]
    x_other, x_far, x_far_other = after(
        (swap(x_own, "seq", 1), swap(x_own, "heads", 2), lax.ppermute(x_own, ("heads", "seq"), far_seq)), first_shard
    )
    x_pieces = gather_cores(x_own, x_far)
    y_pieces = gather_cores(x_other, x_far_other)
    hats, form_one = call(
        functools.partial(norm_body, half, quarter),
        [((2 * half, model), f32), ((half, model), b16)],
        scal, *x_pieces, *y_pieces, flops=2 * half * model, limit=6,
    )
    w_own, w_other = gather_seq(shards)
    w_other = after(w_other, hats)

    feed_shards = gather_batch(after(jnp.concatenate([inner_weight, outer_weight.T], axis=1), shards))

    normed_one, projected, wpad, query, key, value, extra, norms, taps = call(
        functools.partial(front_body, half, quarter, heads, paired),
        [
            ((half, model), b16), ((half + 16, 3 * PADW), b16), ((model, 3 * PADW), b16),
            ((half, PADW), b16), ((2 * half, PADW), b16), ((2 * half, PADW), b16), ((quarter + width, model), b16),
            ((8, model), f32), ((8, 3 * PADW), f32),
        ],
        scal, hats, w_own, w_other, cot_own, *small_args,
        scratch=[
            pltpu.VMEM((2 * half + 16, 3 * PADW), b16),
            pltpu.VMEM((model, 128), f32), pltpu.VMEM((KERNEL * HEAD_DIM, 128), f32), pltpu.VMEM((model, PADW), f32),
        ],
        flops=4 * half * model * 3 * width, limit=12,
    )

    feed_own, feed_other = gather_seq(after(feed_shards, query))
    extra_pieces = gather_heads(extra)

    packed, out_t, lse = call(
        functools.partial(attention_body, half, heads),
        [((half + half // 2, 128), b16), ((width, half), f32), ((8, half), f32)],
        scal, query, key, value,
        scratch=[
            pltpu.VMEM((width, 2 * half), b16), pltpu.VMEM((heads, half, PADW), b16),
            pltpu.VMEM((8, half), f32), pltpu.VMEM((8, half), f32),
        ],
        flops=4 * half * half * width, limit=7,
    )
    packed_pieces = gather_heads(packed)
    feed_own, feed_other, _ = lax.optimization_barrier((feed_own, feed_other, packed))
    inner_full, outer_full = call(
        weights_body, [((model, hidden), b16), ((model, hidden), b16)], scal, feed_own, feed_other, limit=4,
    )

    normed_two, squared, inner_grad, keep, sent, middle_own = call(
        functools.partial(feed_body, half, quarter),
        [((half, model), b16), ((half, hidden), b16), ((half, hidden), b16),
         ((2 * quarter, model), f32), ((2 * quarter, model), b16), ((quarter, model), f32)],
        scal, *packed_pieces, *extra_pieces, *x_pieces, inner_full, outer_full, norms,
        flops=2 * half * model * (model + 3 * hidden), limit=12,
    )
    got = swap(sent, "heads", 1)
    (outer_total,) = call(
        functools.partial(outer_grads_body, quarter), [((model, hidden), f32)],
        scal, *extra_pieces, squared,
        scratch=[pltpu.VMEM((half, model), b16)], flops=2 * half * model * hidden, limit=8,
    )
    got = after(got, outer_total)
    dn_here, dn_far = scatter_far(keep, got, quarter)
    out_keep, out_sent, ff_keep, ff_send = call(
        functools.partial(feed_grads_body, quarter),
        [((2 * quarter, model), f32), ((2 * quarter, model), b16),
         (stacks + (2 * hidden,), b16), (stacks + (2 * hidden,), b16)],
        scal, after(normed_two, got), squared, inner_grad, outer_full, outer_total,
        scratch=[pltpu.VMEM((model, hidden), f32)],
        flops=4 * half * model * hidden, limit=8,
    )
    dn_far = after(dn_far, out_sent)
    ff_got = scatter_seq(ff_send)
    middle_grad, branch, sums_two = call(
        functools.partial(norm_back_body, 2),
        [((quarter, model), f32), ((quarter, model), b16), ((8, model), f32)],
        scal, dn_here, dn_far, middle_own, cot_own, norms, limit=6,
    )
    branch_pieces = gather_heads(branch)
    out_got = swap(after(out_sent, branch), "heads", 1)

    dout, row_dot, pj_keep, pj_send = call(
        functools.partial(branch_body, quarter, heads),
        [((half, PADW), b16), ((8, half), f32), (stacks + (width,), f32), (stacks + (width,), b16)],
        scal, *branch_pieces, extra, out_t,
        scratch=[pltpu.VMEM((width, model), f32), pltpu.VMEM((model, width), f32)],
        flops=4 * half * model * width, limit=6,
    )
    pj_got = scatter_seq(pj_send)
    out_here, out_far = scatter_far(out_keep, after(out_got, dout), quarter)
    remote, query_t, kt = call(
        functools.partial(remote_back_body, half, heads),
        [((half, 384), b16), ((width, half), f32), ((width, 2 * half), b16)],
        scal, query, key, value, dout, lse, row_dot,
        scratch=[
            pltpu.VMEM((heads, half, PADW), b16), pltpu.VMEM((heads, half, PADW), b16),
            pltpu.VMEM((KB, PADW), f32), pltpu.VMEM((KB, PADW), f32),
        ],
        flops=10 * half * half * width, limit=8,
    )
    remote_in = lax.ppermute(remote, "seq", [(1, 0)])
    ff_got, pj_got = after((ff_got, pj_got), remote)
    ff_own, ff_rest = join_seq((ff_keep, ff_got))

    dq, dk, dv, front = call(
        functools.partial(local_back_body, half, heads),
        [((half, PADW), b16), ((half, PADW), b16), ((half, PADW), b16), ((8, 3 * PADW), f32)],
        scal, query, key, value, dout, lse, row_dot, kt, after(query_t, ff_rest, pj_got), taps,
        scratch=[
            pltpu.VMEM((heads, half, PADW), b16), pltpu.VMEM((heads, half, PADW), b16),
            pltpu.VMEM((KB, PADW), f32), pltpu.VMEM((KB, PADW), f32), pltpu.VMEM((width, half), f32),
        ],
        flops=10 * half * half * width, limit=8,
    )
    front_in = lax.ppermute(front, "seq", [(1, 0)])
    remote_in = after(remote_in, dq)
    block_output = (middle_own + out_here + after(out_far, dq).astype(f32)).astype(b16)

    proj_grad, w_keep, w_send, sums_taps = call(
        functools.partial(tail_body, half, quarter),
        [((half, 3 * PADW), b16), (stacks + (640,), f32), (stacks + (640,), b16), ((8, 3 * PADW), f32)],
        scal, dq, dk, dv, remote_in, front_in, projected, normed_one, taps,
        scratch=[
            pltpu.VMEM((half + 16, 3 * PADW), b16), pltpu.VMEM((model, 3 * PADW), f32), pltpu.VMEM((model, 640), f32),
        ],
        flops=2 * half * model * 3 * width, limit=12,
    )
    w_got = scatter_seq(w_send)
    keep, sent, sums = call(
        functools.partial(tail_norm_body, quarter),
        [((2 * quarter + 8, model), f32), ((2 * quarter + 8, model), b16), ((8, model), f32)],
        scal, proj_grad, wpad, form_one, sums_two,
        flops=2 * half * model * 3 * width, limit=8,
    )
    got = swap(sent, "heads", 1)
    dn_here, dn_far = scatter_far(keep, got, quarter)
    small = sums + got[2 * quarter :].astype(f32)
    small = jnp.concatenate([small[0:4], sums_taps[4:8]])
    small = small + swap(small, "seq", 1)
    ff_out, _ = scatter_batch(ff_own, ff_rest, None, small)
    small = jnp.concatenate([small[0:4] + swap(small[0:4], "heads", 2), small[4:8]])
    qkv_own, qkv_rest = join_seq((w_keep[..., : 3 * width], after(w_got, small)[..., : 3 * width]), (pj_keep, pj_got))
    cut = small.shape[1] // 2
    small = jnp.concatenate([small[:, :cut], small[:, cut:]])
    input_grad, _, _ = call(
        functools.partial(norm_back_body, 0),
        [((quarter, model), f32), ((quarter, model), b16), ((8, model), f32)],
        scal, dn_here, dn_far, x_own, middle_grad, norms, limit=6,
    )
    qkv_out, small = scatter_batch(qkv_own, qkv_rest, small, input_grad)
    pj_out = qkv_out[:, 3 * width :]
    small = jnp.concatenate([small[:8], small[8:]], axis=1)

    qkv_out = jnp.stack(
        [
            jnp.concatenate([qkv_out[:, 0:128], qkv_out[:, 384:448]], axis=1),
            jnp.concatenate([qkv_out[:, 128:256], qkv_out[:, 448:512]], axis=1),
            jnp.concatenate([qkv_out[:, 256:384], qkv_out[:, 512:576]], axis=1),
        ],
        axis=1,
    )
    gains = lax.dynamic_slice_in_dim(small[0:4], own * group, group, 1)
    kernel_out = small[4 : 4 + KERNEL].reshape(KERNEL, 3, PADW)[:, :, :width].reshape(KERNEL, 3, heads, HEAD_DIM)
    kernel_out = kernel_out.transpose(1, 2, 3, 0).reshape(3, heads, HEAD_DIM * KERNEL)
    kernel_out = lax.dynamic_slice_in_dim(kernel_out, own * share, share, 2)
    return (
        block_output.reshape(block_input.shape),
        input_grad.reshape(block_input.shape),
        gains[0],
        gains[1],
        qkv_out,
        kernel_out,
        pj_out.T,
        gains[2],
        gains[3],
        ff_out[:, :hidden],
        ff_out[:, hidden : 2 * hidden].T,
    )


def solution(mesh):
    return jax.shard_map(
        on_device,
        mesh=mesh,
        in_specs=(
            P("batch", "seq", "heads", None),
            P("batch", None),
            P(("batch", "seq")),
            P(("batch", "seq")),
            P(("batch", "seq"), None, "heads"),
            P(None, "heads", ("batch", "seq")),
            P("heads", ("batch", "seq")),
            P(("batch", "seq")),
            P(("batch", "seq")),
            P(("batch", "seq"), "heads"),
            P("heads", ("batch", "seq")),
            P("batch", "seq", "heads", None),
        ),
        out_specs=(
            P("batch", "seq", "heads", None),
            P("batch", "seq", "heads", None),
            P(("batch", "seq")),
            P(("batch", "seq")),
            P(("batch", "seq"), None, "heads"),
            P(None, "heads", ("batch", "seq")),
            P("heads", ("batch", "seq")),
            P(("batch", "seq")),
            P(("batch", "seq")),
            P(("batch", "seq"), "heads"),
            P("heads", ("batch", "seq")),
        ),
        check_vma=False,
    )
```
